32 devices in a mesh: ea: 4 (over y, x), ha: 8 (over z, core).
Axes of the slice: x: 2, y: 2, z: 4, core: 2. Of those that a mesh axis runs over, the one named last changes fastest.
Arguments:
- tokens: bfloat16 [768, 13312], P('ea', 'ha'), may hold values from -6 to 6
- image_counts: int32 [128], P('ha'), may hold values from 40 to 98, as said below
- kept_patches: int32 [128, 98], P('ha'), may hold values from 0 to 195, as said below
- norm1_gain: bfloat16 [768], P('ea'), may hold values from 0.25 to 1.75
- norm1_bias: bfloat16 [768], P('ea'), may hold values from -3 to 3
- qkv_weight: bfloat16 [768, 2304], P('ea', 'ha'), may hold values from -0.21875 to 0.21875
- query_bias: bfloat16 [768], P('ea'), may hold values from -3 to 3
- value_bias: bfloat16 [768], P('ea'), may hold values from -3 to 3
- out_weight: bfloat16 [768, 768], P('ea', 'ha'), may hold values from -0.625 to 0.625
- out_bias: bfloat16 [768], P('ea'), may hold values from -1.75 to 1.75
- norm2_gain: bfloat16 [768], P('ea'), may hold values from 0.25 to 1.75
- norm2_bias: bfloat16 [768], P('ea'), may hold values from -3 to 3
- in_weight: bfloat16 [768, 3072], P('ea', 'ha'), may hold values from -0.21875 to 0.21875
- in_bias: bfloat16 [3072], P('ha'), may hold values from -3 to 3
- back_weight: bfloat16 [3072, 768], P('ha', 'ea'), may hold values from -0.109375 to 0.109375
- back_bias: bfloat16 [768], P('ea'), may hold values from -1.75 to 1.75
- cotangent: bfloat16 [768, 13312], P('ea', 'ha'), may hold values from -6 to 6
Outputs:
- output: bfloat16 [768, 13312], P('ea', 'ha')
- grad_tokens: float32 [768, 13312], P('ea', 'ha')
- grad_norm1_gain: float32 [768], P('ea')
- grad_norm1_bias: float32 [768], P('ea')
- grad_qkv_weight: float32 [768, 2304], P('ea', 'ha')
- grad_query_bias: float32 [768], P('ea')
- grad_value_bias: float32 [768], P('ea')
- grad_out_weight: float32 [768, 768], P('ea', 'ha')
- grad_out_bias: float32 [768], P('ea')
- grad_norm2_gain: float32 [768], P('ea')
- grad_norm2_bias: float32 [768], P('ea')
- grad_in_weight: float32 [768, 3072], P('ea', 'ha')
- grad_in_bias: float32 [3072], P('ha')
- grad_back_weight: float32 [3072, 768], P('ha', 'ea')
- grad_back_bias: float32 [768], P('ea')
The draws below stay inside these ranges and needn't reach their ends.
Inputs may be any that keep to these rules, and one draw needn't show every extreme that they name: `image_counts`: each image has between 40 and 98 visible patches; some image has exactly 98 and some exactly 40. `kept_patches`: each row lists distinct patch numbers of its image; only its first image_counts entries are used, in packing order.
All inputs are finite; a program needn't handle non-finite values.
Results may differ from the reference program's by a relative error of at most 0.017.
Values may be sent and summed in bfloat16 or wider, within the bound.
No kernel may reach another device: no remote copies, remote signals or barrier semaphores. Data moves between devices by JAX's collectives and lax.ppermute only.
A program may use at most 192 MiB of HBM per device.

```python
import jax
import jax.numpy as jnp
from jax import lax

HEADS = 12
HEAD_DIM = 64
FF = 3072
D = 768
PATCHES = 196
GRID = 14
MOST = 98
LEAST = 40
IMG_DEV = 16
IMAGES = 128
ROWS_DEV = 1664
TOKENS = 13312
N_HA = 8


def draw_image_counts(key, part):
    drawn = jax.random.randint(key, (IMAGES,), LEAST, MOST + 1, dtype=jnp.int32)
    return drawn.at[0].set(MOST).at[1].set(LEAST)


def draw_kept_patches(key, part):
    several = jax.random.split(key, IMAGES)
    return jax.vmap(lambda single: jax.random.permutation(single, PATCHES)[:MOST])(several).astype(jnp.int32)


def steps_of(own_key, extent, cuts, smallest, largest):
    loudness, own = 1.0, jax.random.fold_in(own_key, 6)
    for dim, parts in cuts:
        heights = jnp.exp(jax.random.uniform(jax.random.fold_in(own, dim), (parts,), jnp.float32, smallest / len(cuts), largest / len(cuts)))
        loudness = loudness * jnp.repeat(heights, extent[dim] // parts).reshape([-1 if axis == dim else 1 for axis in range(len(extent))])
    return loudness


def noise(own_key, shape, scale, bound, cuts=(), kind=jnp.bfloat16):
    array = jax.random.normal(own_key, shape, jnp.float32) * scale
    if len(cuts) > 0:
        array = steps_of(own_key, shape, cuts, -0.22, 0.18) * array
    return jnp.clip(array, min=-bound, max=bound).astype(kind)


def setup_inputs(seed: int = 0) -> dict:
    keys = jax.random.split(jax.random.key(seed), 18)
    tokens = noise(keys[0], (D, TOKENS), 1.0, 6.0, ((0, 4), (1, 8)))
    image_counts = draw_image_counts(jax.random.fold_in(keys[17], 71), 0)
    kept_patches = draw_kept_patches(jax.random.fold_in(keys[17], 71), 0)
    norm1_gain = jnp.clip(1.0 + 0.15 * jax.random.normal(keys[3], (D,), jnp.float32), 0.25, 1.75).astype(jnp.bfloat16)
    norm1_bias = noise(keys[4], (D,), 0.5, 3.0, ((0, 4),))
    qkv_weight = noise(keys[5], (D, 3 * D), D ** -0.5, 0.21875, ((0, 4), (1, 8)))
    query_bias = noise(keys[6], (D,), 0.5, 3.0, ((0, 4),))
    value_bias = noise(keys[7], (D,), 0.5, 3.0, ((0, 4),))
    out_weight = noise(keys[8], (D, D), (D // 8) ** -0.5, 0.625, ((0, 4), (1, 8)))
    out_bias = noise(keys[9], (D,), 0.3, 1.75, ((0, 4),))
    norm2_gain = jnp.clip(1.0 + 0.15 * jax.random.normal(keys[10], (D,), jnp.float32), 0.25, 1.75).astype(jnp.bfloat16)
    norm2_bias = noise(keys[11], (D,), 0.5, 3.0, ((0, 4),))
    in_weight = noise(keys[12], (D, FF), D ** -0.5, 0.21875, ((0, 4), (1, 8)))
    in_bias = noise(keys[13], (FF,), 0.5, 3.0, ((0, 8),))
    back_weight = noise(keys[14], (FF, D), FF ** -0.5, 0.109375, ((0, 8), (1, 4)))
    back_bias = noise(keys[15], (D,), 0.3, 1.75, ((0, 4),))
    cotangent = noise(keys[16], (D, TOKENS), 1.0, 6.0, ((0, 4), (1, 8)))
    return dict(tokens=tokens, image_counts=image_counts, kept_patches=kept_patches, norm1_gain=norm1_gain, norm1_bias=norm1_bias, qkv_weight=qkv_weight, query_bias=query_bias, value_bias=value_bias, out_weight=out_weight, out_bias=out_bias, norm2_gain=norm2_gain, norm2_bias=norm2_bias, in_weight=in_weight, in_bias=in_bias, back_weight=back_weight, back_bias=back_bias, cotangent=cotangent)


@jax.custom_vjp
def low(v):
    return lax.optimization_barrier(v.astype(jnp.bfloat16)).astype(jnp.float32)

@jax.custom_vjp
def low_back(v):
    return v

def low_keep(v):
    return (low(v), None)

def low_pass(kept, grad):
    return (grad,)

def back_keep(v):
    return (v, None)

def back_low(kept, grad):
    return (low(grad),)
low.defvjp(low_keep, low_pass)
low_back.defvjp(back_keep, back_low)
EPSILON = 1e-06
NEGATIVE = -1e+30
HIGHEST = lax.Precision.HIGHEST

def positions(patch_index, full_width):
    quarter = full_width // 4
    omega = 1.0 / 10000.0 ** (jnp.arange(quarter, dtype=jnp.float32) / quarter)
    row_part = (patch_index // GRID).astype(jnp.float32)[:, None] * omega[None, :]
    col_part = (patch_index % GRID).astype(jnp.float32)[:, None] * omega[None, :]
    return jnp.concatenate([jnp.sin(row_part), jnp.cos(row_part), jnp.sin(col_part), jnp.cos(col_part)], 1)

def layout(image_counts, kept_patches, row_count, full_width):
    image_total, slot_count = kept_patches.shape
    image_ends = jnp.cumsum(image_counts).astype(jnp.int32)
    image_starts = (image_ends - image_counts).astype(jnp.int32)
    row_ids = jnp.arange(row_count, dtype=jnp.int32)
    segment = lax.optimization_barrier(jnp.sum((row_ids[:, None] >= image_ends[None, :]).astype(jnp.int32), 1)).astype(jnp.int32)
    live_rows = (row_ids < image_ends[image_total - 1]).astype(jnp.float32)
    clipped = jnp.minimum(segment, image_total - 1)
    onehot = (clipped[:, None] == jnp.arange(image_total, dtype=jnp.int32)[None, :]).astype(jnp.int32)
    first_row = lax.optimization_barrier(jnp.sum(onehot * image_starts[None, :], 1)).astype(jnp.int32)
    within = jnp.clip(row_ids - first_row, 0, slot_count - 1)
    patch_index = jnp.take(kept_patches.reshape(-1), (clipped * slot_count + within).astype(jnp.int32))
    return (segment, live_rows, positions(patch_index, full_width))

def normalize(values, gain, shift):
    center = lax.optimization_barrier(jnp.mean(values, -1, keepdims=True))
    centred = values - center
    spread = lax.optimization_barrier(jnp.mean(centred * centred, -1, keepdims=True))
    return centred * lax.rsqrt(spread + EPSILON) * gain + shift

def group_forward(params, block_start, segment):
    norm1_gain, norm1_bias, qkv_weight, query_bias, value_bias, out_weight, out_bias, norm2_gain, norm2_bias, in_weight, in_bias, back_weight, back_bias = params
    row_count = block_start.shape[0]
    first_normed = low(normalize(block_start, norm1_gain, norm1_bias))
    joined = jnp.dot(first_normed, qkv_weight, precision=HIGHEST).reshape(row_count, HEADS, 3, HEAD_DIM)
    qkv_shift = jnp.stack([query_bias.reshape(HEADS, HEAD_DIM), jnp.zeros((HEADS, HEAD_DIM), jnp.float32), value_bias.reshape(HEADS, HEAD_DIM)], 1)
    joined = low_back(low(joined + qkv_shift))
    same_image = segment[:, None] == segment[None, :]

    def attend(query, key_rows, value_rows):
        scores = low_back(jnp.dot(query, key_rows.T, precision=HIGHEST) * HEAD_DIM ** (-0.5))
        scores = jnp.where(same_image, scores, NEGATIVE)
        probabilities = low(jax.nn.softmax(scores, -1))
        return jnp.dot(probabilities, value_rows, precision=HIGHEST)
    mixed_rows = jax.vmap(attend, in_axes=1, out_axes=1)(joined[:, :, 0], joined[:, :, 1], joined[:, :, 2])
    mixed_rows = low_back(low(mixed_rows.reshape(row_count, HEADS * HEAD_DIM)))
    middle = block_start + low_back(jnp.dot(mixed_rows, out_weight, precision=HIGHEST) + out_bias)
    second_normed = low(normalize(middle, norm2_gain, norm2_bias))
    hidden = low_back(jnp.dot(second_normed, in_weight, precision=HIGHEST) + in_bias)
    activated = low(jax.nn.gelu(hidden, approximate=False))
    return middle + jnp.dot(activated, back_weight, precision=HIGHEST) + back_bias

def reference(tokens, image_counts, kept_patches, norm1_gain, norm1_bias, qkv_weight, query_bias, value_bias, out_weight, out_bias, norm2_gain, norm2_bias, in_weight, in_bias, back_weight, back_bias, cotangent):
    counts_grouped = image_counts.reshape(N_HA, IMG_DEV)
    patches_grouped = kept_patches.reshape(N_HA, IMG_DEV, MOST)
    segments, live_all, placed = jax.vmap(lambda counts_one, patches_one: layout(counts_one, patches_one, ROWS_DEV, D))(counts_grouped, patches_grouped)
    starts_all = tokens.astype(jnp.float32).T.reshape(N_HA, ROWS_DEV, D) + placed
    params = tuple((member.astype(jnp.float32) for member in (norm1_gain, norm1_bias, qkv_weight, query_bias, value_bias, out_weight, out_bias, norm2_gain, norm2_bias, in_weight, in_bias, back_weight, back_bias)))

    def forward(weights, inputs):

        def advance(carried, pieces):
            block_start, segment, live_mask = pieces
            result = jax.checkpoint(group_forward)(weights, block_start, segment) * live_mask[:, None]
            return (carried, result)
        _, outputs = lax.scan(advance, jnp.zeros((), jnp.float32), (inputs, segments, live_all))
        return outputs
    outputs, pullback = jax.vjp(forward, params, starts_all)
    gradients, grad_starts = pullback(cotangent.astype(jnp.float32).T.reshape(N_HA, ROWS_DEV, D))
    return (outputs.reshape(TOKENS, D).T.astype(jnp.bfloat16), grad_starts.reshape(TOKENS, D).T, gradients[0], gradients[1], gradients[2], gradients[3], gradients[4], gradients[5], gradients[6], gradients[7], gradients[8], gradients[9], gradients[10], gradients[11], gradients[12])
```

```python
from functools import partial

import jax
import jax.numpy as jnp
from jax import lax
from jax.experimental import pallas as pl
from jax.experimental.pallas import tpu as pltpu
from jax.sharding import PartitionSpec as P

HEAD_DIM = 64
GRID = 14
EPSILON = 1e-06
NEGATIVE = -1e30
BLOCKS = 8
VEC_ROWS = 16
NN = (((1,), (0,)), ((), ()))
NT = (((1,), (1,)), ((), ()))
TN = (((0,), (0,)), ((), ()))
F32 = jnp.float32
BF16 = jnp.bfloat16
SMEM = pl.BlockSpec(memory_space=pltpu.SMEM)
VMEM = pl.BlockSpec(memory_space=pltpu.VMEM)
PARAMS = pltpu.CompilerParams(vmem_limit_bytes=56 * 1024 * 1024)


def dot(a, b, dims):
    return lax.dot_general(a, b, dims, preferred_element_type=F32)


def iota(shape, axis):
    return lax.broadcasted_iota(jnp.int32, shape, axis)


def prefix(counts, starts):
    total = jnp.int32(0)
    for i in range(counts.shape[0]):
        starts[i] = total
        total = total + counts[i]


def select_rows(sel, counts, starts, part, images, rows, window, slots):
    first = starts[part * images]
    base = jnp.minimum(first // 128, (slots - window) // 128) * 128
    base = pl.multiple_of(base, 128)
    row = iota((rows, window), 0)
    gap = iota((rows, window), 1) - row
    for i in range(images):
        image = part * images + i
        hit = (gap == starts[image] - base) & (row < counts[image])
        sel[i * rows : (i + 1) * rows, :] = jnp.where(hit, 1.0, 0.0).astype(BF16)
    return base


def pack_kernel(images, rows, window, meta, counts, tokens, cotangent, x_out, y_out, starts, sel):
    prefix(counts, starts)
    for d in range(x_out.shape[0]):
        base = select_rows(
            sel, counts, starts, meta[0] ^ d, images, rows, window, tokens.shape[1]
        )
        chosen = sel[...]
        x_out[d] = dot(chosen, tokens[:, pl.ds(base, window)], NT).astype(BF16)
        y_out[d] = dot(chosen, cotangent[:, pl.ds(base, window)], NT).astype(BF16)


def unpack_kernel(images, rows, window, meta, counts, *refs):
    parts, (out, starts, sel, total) = refs[:-4], refs[-4:]
    prefix(counts, starts)
    total[...] = jnp.zeros_like(total)
    for d, part in enumerate(parts):
        base = select_rows(sel, counts, starts, meta[0] ^ d, images, rows, window, out.shape[1])
        total[:, pl.ds(base, window)] += dot(part[...], sel[...], TN)
    out[...] = total[...].astype(out.dtype)


def norm_parts(values):
    center = jnp.mean(values, 1, keepdims=True)
    centred = values - center
    factor = lax.rsqrt(jnp.mean(centred * centred, 1, keepdims=True) + EPSILON)
    return centred * factor, factor


def norm_back(grad, xhat, factor, gain):
    scaled = grad * gain
    mean = jnp.mean(scaled, 1, keepdims=True)
    across = jnp.mean(scaled * xhat, 1, keepdims=True)
    return factor * (scaled - mean - xhat * across)


def colsum(values):
    return jnp.sum(values, 0, keepdims=True)


def attend_kernel(images, rows, meta, counts, *refs):
    x_refs, (patches, sines, cosines, g1) = refs[:4], refs[4:8]
    x1_out, x0, h1_out, qkv_out, p_out, o_out, vecs, inb, wq, wo = refs[8:]
    me = meta[0]
    parts = len(x_refs)
    narrow = x_refs[0].shape[1]
    wide = 3 * narrow
    half = wide // 2
    outer = narrow // 2
    heads = narrow // HEAD_DIM
    for d in range(parts):
        low, high = d * narrow, (d + 1) * narrow
        vecs[:, low:high] = g1[(me ^ d) * BLOCKS, narrow:, :narrow].astype(F32)
        for z in range(parts):
            for k in range(2):
                block = g1[(me ^ d) * BLOCKS + 2 * z + k, :narrow, :half]
                wq[z, low:high, k * half : (k + 1) * half] = block
                block = g1[z * BLOCKS + 2 * (me ^ d) + k, :narrow, half:]
                wo[z, :, low + k * outer : low + (k + 1) * outer] = block
    for h in range(BLOCKS):
        inb[h] = g1[h, narrow:, :].astype(F32)[8:9]
    pieces = []
    for d in range(parts):
        e = me ^ d
        table = jnp.where(e % 2 == 0, sines[...], cosines[...])
        high = table.astype(BF16)
        rest = table - high.astype(F32)
        middle = rest.astype(BF16)
        low = (rest - middle.astype(F32)).astype(BF16)
        stacked = jnp.concatenate([high, middle, low], 0)
        depth = table.shape[0]
        for i in range(images):
            patch = patches[pl.ds(me * images + i, 1), :rows]
            row = (patch * 4682) >> 16
            place = jnp.where(e < 2, row, patch - row * GRID)
            hot = jnp.where(iota((depth, rows), 0) == place, 1.0, 0.0).astype(BF16)
            placed = dot(jnp.concatenate([hot, hot, hot], 0), stacked, TN)
            x0[i * rows : (i + 1) * rows, d * narrow : (d + 1) * narrow] = (
                x_refs[d][i * rows : (i + 1) * rows, :].astype(F32) + placed
            )
    xhat, _ = norm_parts(x0[...])
    h1 = (xhat * vecs[0:1] + vecs[1:2]).astype(BF16)
    h1_out[...] = h1
    for z in range(parts):
        shift = g1[z * BLOCKS, narrow:, :].astype(F32)
        shift = jnp.concatenate([shift[6:7], shift[7:8, : wide - shift.shape[1]]], 1)
        qkv_out[z] = (dot(h1, wq[z], NN) + shift).astype(BF16)
    factor = HEAD_DIM ** (-0.5)
    for b in range(images):
        seen = iota((rows, rows), 1) < counts[me * images + b]
        span = slice(b * rows, (b + 1) * rows)
        for z in range(parts):
            mixed = []
            for i in range(heads):
                at = 3 * HEAD_DIM * i
                query = qkv_out[z, span, at : at + HEAD_DIM]
                key = qkv_out[z, span, at + HEAD_DIM : at + 2 * HEAD_DIM]
                value = qkv_out[z, span, at + 2 * HEAD_DIM : at + 3 * HEAD_DIM]
                scores = jnp.where(seen, dot(query, key, NT) * factor, NEGATIVE)
                weights = jnp.exp(scores - jnp.max(scores, 1, keepdims=True))
                chance = (weights / jnp.sum(weights, 1, keepdims=True)).astype(BF16)
                p_out[z * heads + i, b] = chance
                mixed.append(dot(chance, value, NN).astype(BF16))
            o_out[span, z * narrow : (z + 1) * narrow] = jnp.concatenate(mixed, 1)
    attn = dot(o_out[...], jnp.concatenate([wo[z] for z in range(parts)], 0), NN)
    x1_out[...] = x0[...] + attn + vecs[4:5]


def hidden_kernel(meta, *refs):
    x1, y_refs, (vecs, inb, g2, g3) = refs[0], refs[1:5], refs[5:9]
    d2, d3, dinb, out, dx1, da, vec_grads = refs[9:16]
    h2s, dys, y_total, dh_total = refs[16:]
    me = meta[0]
    parts, narrow = len(y_refs), y_refs[0].shape[1]
    step = pl.program_id(0)

    @pl.when(step == 0)
    def _():
        for d in range(parts):
            dys[:, d * narrow : (d + 1) * narrow] = y_refs[d][...]
        xhat, _ = norm_parts(x1[...])
        h2s[...] = (xhat * vecs[2:3] + vecs[3:4]).astype(BF16)
        y_total[...] = jnp.zeros_like(y_total)
        dh_total[...] = jnp.zeros_like(dh_total)

    w_in = jnp.concatenate([g2[me ^ d, 0] for d in range(parts)], 0)
    w_back = jnp.concatenate([g3[me ^ d, 0] for d in range(parts)], 0)
    h2 = h2s[...]
    dy = dys[...]
    hidden = dot(h2, w_in, NN) + inb[0]
    gate = 0.5 + 0.5 * lax.erf(hidden * (0.5**0.5))
    active = (hidden * gate).astype(BF16)
    slope = gate + hidden * jnp.exp(-0.5 * hidden * hidden) * 0.3989422804014327
    y_total[...] += dot(active, w_back, NT)
    grad_hidden = dot(dy, w_back, NN) * slope
    low = grad_hidden.astype(BF16)
    dinb[0] = colsum(low.astype(F32))
    dh_total[...] += dot(low, w_in, NT)
    d_back = dot(dy, active, TN)
    d_in = dot(h2, low, TN)
    for d in range(parts):
        d2[me ^ d, 0] = d_in[d * narrow : (d + 1) * narrow].astype(d2.dtype)
        d3[me ^ d, 0] = d_back[d * narrow : (d + 1) * narrow].astype(d3.dtype)

    @pl.when(step == pl.num_programs(0) - 1)
    def _():
        values = x1[...]
        result = (values + y_total[...] + vecs[5:6]).astype(BF16)
        for d in range(parts):
            out[d] = result[:, d * narrow : (d + 1) * narrow]
        xhat, factor = norm_parts(values)
        grad = dh_total[...]
        dy_wide = dys[...].astype(F32)
        total = dy_wide + norm_back(grad, xhat, factor, vecs[2:3])
        dx1[...] = total
        narrowed = total.astype(BF16)
        da[...] = narrowed
        vec_grads[0:1] = colsum(grad * xhat)
        vec_grads[1:2] = colsum(grad)
        vec_grads[2:3] = colsum(narrowed.astype(F32))
        vec_grads[3:4] = colsum(dy_wide)
        vec_grads[4:8] = jnp.zeros_like(vec_grads[4:8])


def attend_back_kernel(images, rows, da, o_ref, qkv, p_ref, wo, dqkv, dwo, dshift, do_ref):
    parts, narrow = wo.shape[0], wo.shape[1]
    heads = narrow // HEAD_DIM
    factor = HEAD_DIM ** (-0.5)
    grad = da[...]
    for z in range(parts):
        do_ref[z] = dot(grad, wo[z], NT).astype(BF16)
        dwo[z] = dot(o_ref[:, z * narrow : (z + 1) * narrow], grad, TN).astype(dwo.dtype)
    for b in range(images):
        span = slice(b * rows, (b + 1) * rows)
        for z in range(parts):
            grads = []
            for i in range(heads):
                at = 3 * HEAD_DIM * i
                query = qkv[z, span, at : at + HEAD_DIM]
                key = qkv[z, span, at + HEAD_DIM : at + 2 * HEAD_DIM]
                value = qkv[z, span, at + 2 * HEAD_DIM : at + 3 * HEAD_DIM]
                grad_head = do_ref[z, span, i * HEAD_DIM : (i + 1) * HEAD_DIM]
                low = p_ref[z * heads + i, b]
                chance = low.astype(F32)
                grad_chance = dot(grad_head, value, NT)
                inner = jnp.sum(chance * grad_chance, 1, keepdims=True)
                grad_score = (chance * (grad_chance - inner)).astype(BF16)
                grads.append((dot(grad_score, key, NN) * factor).astype(BF16))
                grads.append((dot(grad_score, query, TN) * factor).astype(BF16))
                grads.append(dot(low, grad_head, TN).astype(BF16))
            dqkv[z, span, :] = jnp.concatenate(grads, 1)
    for z in range(parts):
        dshift[z] = colsum(dqkv[z].astype(F32))


def last_kernel(meta, x0, h1, dqkv, wq, dx1, vecs, dwo, dshift, dinb, vec_grads, d1, gx, rows_ref):
    me = meta[0]
    parts, narrow = gx.shape[0], gx.shape[2]
    half = wq.shape[2] // 2
    outer = narrow // 2
    width = d1.shape[3]
    grad = dot(dqkv[0], wq[0], NT)
    for z in range(1, parts):
        grad += dot(dqkv[z], wq[z], NT)
    xhat, factor = norm_parts(x0[...])
    result = (dx1[...] + norm_back(grad, xhat, factor, vecs[0:1])).astype(BF16)
    rows_ref[0:1] = colsum(grad * xhat)
    rows_ref[1:2] = colsum(grad)
    rows_ref[2:6] = vec_grads[0:4]
    for d in range(parts):
        gx[d] = result[:, d * narrow : (d + 1) * narrow]
    feature = h1[...]
    for z in range(parts):
        dw = dot(feature, dqkv[z], TN).astype(d1.dtype)
        for d in range(parts):
            for k in range(2):
                d1[me ^ d, 2 * z + k, :narrow, :half] = dw[
                    d * narrow : (d + 1) * narrow, k * half : (k + 1) * half
                ]
                at = d * narrow + k * outer
                d1[z, 2 * (me ^ d) + k, :narrow, half:] = dwo[z, :, at : at + outer]
    gap = jnp.zeros((6, width - narrow), F32)
    for d in range(parts):
        shift = dshift[me ^ d]
        six = jnp.concatenate([rows_ref[0:6, d * narrow : (d + 1) * narrow], gap], 1)
        second = jnp.concatenate([shift[:, width:], gap[0:1, : 2 * width - 2 * half]], 1)
        for h in range(BLOCKS):
            tail = [six, shift[:, :width], second, dinb[h], jnp.zeros((7, width), F32)]
            d1[me ^ d, h, narrow:, :] = jnp.concatenate(tail, 0).astype(d1.dtype)


def call(kernel, outs, operands, scratch=(), name=None):
    specs = []
    values = []
    for value in operands:
        specs.append(SMEM if value.dtype == jnp.int32 and value.ndim == 1 else VMEM)
        values.append(value)
    return pl.pallas_call(
        kernel,
        out_shape=outs,
        in_specs=specs,
        out_specs=jax.tree.map(lambda _: VMEM, outs),
        scratch_shapes=scratch,
        compiler_params=PARAMS,
        name=name,
    )(*values)


def shaped(dtype, *shape):
    return jax.ShapeDtypeStruct(shape, dtype)


def exchange(block, d):
    size = lax.axis_size("ea")
    return block if d == 0 else lax.ppermute(block, "ea", [(e, e ^ d) for e in range(size)])


def vector_rows(vectors, shift, bias):
    width = bias.shape[-1]
    rows = [jnp.pad(v, (0, width - v.shape[0])) for v in vectors]
    rows += [shift[:width], jnp.pad(shift[width:], (0, 2 * width - shift.shape[0])), bias]
    return jnp.stack(rows + [jnp.zeros_like(bias)] * (VEC_ROWS - len(rows)))


def shards(
    tokens,
    image_counts,
    kept_patches,
    norm1_gain,
    norm1_bias,
    qkv_weight,
    query_bias,
    value_bias,
    out_weight,
    out_bias,
    norm2_gain,
    norm2_bias,
    in_weight,
    in_bias,
    back_weight,
    back_bias,
    cotangent,
):
    parts = lax.axis_size("ea")
    columns = lax.axis_size("ha")
    me = lax.axis_index("ea")
    mine = lax.axis_index("ha")
    meta = jnp.stack([me, mine]).astype(jnp.int32)
    narrow, slots = tokens.shape
    full = narrow * parts
    images = image_counts.shape[0] // parts
    most = kept_patches.shape[1]
    rows = -(-most // 16) * 16
    count = images * rows
    window = min(slots, (images * most + 127 + 127) // 128 * 128)
    heads = full // HEAD_DIM
    group_heads = narrow // HEAD_DIM
    hidden_block = in_weight.shape[1] * columns // BLOCKS
    half = 3 * narrow // 2

    pairs = jnp.zeros((group_heads, HEAD_DIM), BF16)
    shift = jnp.stack(
        [query_bias.reshape(group_heads, HEAD_DIM), pairs, value_bias.reshape(group_heads, HEAD_DIM)],
        1,
    ).reshape(-1)
    vectors = (norm1_gain, norm1_bias, norm2_gain, norm2_bias, out_bias, back_bias)
    back_turned = back_weight.T
    if columns == BLOCKS:
        below = vector_rows(vectors, shift, in_bias)
        first = jnp.concatenate([jnp.concatenate([qkv_weight, out_weight], 1), below], 0)
        g1 = lax.all_gather(first, ("ea", "ha"))
        g2 = lax.all_gather(in_weight, ("ea", "ha"))
        g3 = lax.all_gather(back_turned, ("ea", "ha"))
    else:

        def whole(weight):
            wide = lax.all_gather(weight, "ha", axis=1, tiled=True)
            blocks = wide.reshape(narrow, BLOCKS, -1).transpose(1, 0, 2)
            return lax.all_gather(blocks, "ea")

        biases = lax.all_gather(in_bias, "ha", tiled=True).reshape(BLOCKS, -1)
        below = jax.vmap(lambda bias: vector_rows(vectors, shift, bias))(biases)
        g1 = jnp.concatenate([whole(qkv_weight), whole(out_weight)], 3)
        g1 = jnp.concatenate([g1, lax.all_gather(below, "ea")], 2)
        g2 = whole(in_weight)
        g3 = whole(back_turned)
        g1 = g1.reshape(parts * BLOCKS, narrow + VEC_ROWS, hidden_block)
    g2 = g2.reshape(parts, BLOCKS, narrow, hidden_block)
    g3 = g3.reshape(parts, BLOCKS, narrow, hidden_block)

    x_packed, y_packed = call(
        partial(pack_kernel, images, rows, window),
        (shaped(BF16, parts, count, narrow),) * 2,
        (meta, image_counts, tokens, cotangent),
        (pltpu.SMEM((image_counts.shape[0],), jnp.int32), pltpu.VMEM((count, window), BF16)),
        "pack",
    )
    xs = [exchange(x_packed[d], d) for d in range(parts)]
    ys = [exchange(y_packed[d], d) for d in range(parts)]

    omega = 1.0 / 10000.0 ** (jnp.arange(narrow, dtype=F32) / narrow)
    angles = jnp.arange(16, dtype=F32)[:, None] * omega[None, :]
    patches = jnp.pad(kept_patches, ((0, 0), (0, 128 - most)))

    x1, x0, h1, qkv, chances, mixed, vecs, inb, wq, wo = call(
        partial(attend_kernel, images, rows),
        (
            shaped(F32, count, full),
            shaped(F32, count, full),
            shaped(BF16, count, full),
            shaped(BF16, parts, count, 3 * narrow),
            shaped(BF16, heads, images, rows, rows),
            shaped(BF16, count, full),
            shaped(F32, VEC_ROWS, full),
            shaped(F32, BLOCKS, 1, hidden_block),
            shaped(BF16, parts, full, 3 * narrow),
            shaped(BF16, parts, narrow, full),
        ),
        (meta, image_counts, *xs, patches, jnp.sin(angles), jnp.cos(angles), g1),
        name="attend",
    )

    whole_spec = lambda *shape: pl.BlockSpec(shape, lambda h: (0,) * len(shape))
    block_spec = pl.BlockSpec((parts, 1, narrow, hidden_block), lambda h: (0, h, 0, 0))
    bias_spec = pl.BlockSpec((1, 1, hidden_block), lambda h: (h, 0, 0))
    d2, d3, dinb, outs, dx1, da, vec_grads = pl.pallas_call(
        hidden_kernel,
        grid=(BLOCKS,),
        out_shape=(
            shaped(BF16, parts, BLOCKS, narrow, hidden_block),
            shaped(BF16, parts, BLOCKS, narrow, hidden_block),
            shaped(F32, BLOCKS, 1, hidden_block),
            shaped(BF16, parts, count, narrow),
            shaped(F32, count, full),
            shaped(BF16, count, full),
            shaped(F32, 8, full),
        ),
        in_specs=[SMEM, whole_spec(count, full)]
        + [whole_spec(count, narrow)] * parts
        + [whole_spec(VEC_ROWS, full), bias_spec, block_spec, block_spec],
        out_specs=(
            block_spec,
            block_spec,
            bias_spec,
            whole_spec(parts, count, narrow),
            whole_spec(count, full),
            whole_spec(count, full),
            whole_spec(8, full),
        ),
        scratch_shapes=(
            pltpu.VMEM((count, full), BF16),
            pltpu.VMEM((count, full), BF16),
            pltpu.VMEM((count, full), F32),
            pltpu.VMEM((count, full), F32),
        ),
        compiler_params=PARAMS,
        name="hidden",
    )(meta, x1, *ys, vecs, inb, g2, g3)

    dqkv, dwo, dshift = call(
        partial(attend_back_kernel, images, rows),
        (
            shaped(BF16, parts, count, 3 * narrow),
            shaped(BF16, parts, narrow, full),
            shaped(F32, parts, 1, 3 * narrow),
        ),
        (da, mixed, qkv, chances, wo),
        (pltpu.VMEM((parts, count, narrow), BF16),),
        "attend_back",
    )
    d1, gx = call(
        last_kernel,
        (
            shaped(BF16, parts, BLOCKS, narrow + VEC_ROWS, hidden_block),
            shaped(BF16, parts, count, narrow),
        ),
        (meta, x0, h1, dqkv, wq, dx1, vecs, dwo, dshift, dinb, vec_grads),
        (pltpu.VMEM((8, full), F32),),
        "last",
    )

    def unpack(blocks, dtype):
        return call(
            partial(unpack_kernel, images, rows, window),
            shaped(dtype, narrow, slots),
            (meta, image_counts, *[exchange(blocks[d], d) for d in range(parts)]),
            (
                pltpu.SMEM((image_counts.shape[0],), jnp.int32),
                pltpu.VMEM((count, window), BF16),
                pltpu.VMEM((narrow, slots), F32),
            ),
            "unpack",
        )

    output = unpack(outs, BF16)
    grad_tokens = unpack(gx, F32)

    if columns == BLOCKS:

        def scatter(blocks):
            flat = blocks.reshape(parts * BLOCKS, *blocks.shape[2:])
            return lax.psum_scatter(flat, ("ea", "ha")).astype(F32)

        s1, grad_in, grad_back = scatter(d1), scatter(d2), scatter(d3)
        grad_qkv, grad_out, small = s1[:narrow, :half], s1[:narrow, half:], s1[narrow:]
        grad_in_bias = small[8]
    else:

        def scatter(blocks):
            mixed_blocks = lax.psum_scatter(blocks.astype(F32), "ea")
            flat = mixed_blocks.transpose(1, 0, 2).reshape(narrow, -1)
            return lax.psum_scatter(flat, "ha", scatter_dimension=1, tiled=True)

        grad_in, grad_back = scatter(d2), scatter(d3)
        grad_qkv, grad_out = scatter(d1[:, :, :narrow, :half]), scatter(d1[:, :, :narrow, half:])
        small = lax.psum(d1[:, :, narrow:].astype(F32), ("ea", "ha"))
        size = in_bias.shape[0]
        grad_in_bias = lax.dynamic_slice_in_dim(small[0, :, 8].reshape(-1), mine * size, size, 0)
        small = lax.dynamic_index_in_dim(small[:, 0], me, 0, False)
    small_shift = jnp.concatenate([small[6], small[7]])[: 3 * narrow]
    small_shift = small_shift.reshape(group_heads, 3, HEAD_DIM)
    return (
        output,
        grad_tokens,
        small[0, :narrow],
        small[1, :narrow],
        grad_qkv,
        small_shift[:, 0].reshape(-1),
        small_shift[:, 2].reshape(-1),
        grad_out,
        small[4, :narrow],
        small[2, :narrow],
        small[3, :narrow],
        grad_in,
        grad_in_bias,
        grad_back.T,
        small[5, :narrow],
    )


def solution(mesh):
    return jax.shard_map(
        shards,
        mesh=mesh,
        in_specs=(
            P("ea", "ha"),
            P("ha"),
            P("ha", None),
            P("ea"),
            P("ea"),
            P("ea", "ha"),
            P("ea"),
            P("ea"),
            P("ea", "ha"),
            P("ea"),
            P("ea"),
            P("ea"),
            P("ea", "ha"),
            P("ha"),
            P("ha", "ea"),
            P("ea"),
            P("ea", "ha"),
        ),
        out_specs=(
            P("ea", "ha"),
            P("ea", "ha"),
            P("ea"),
            P("ea"),
            P("ea", "ha"),
            P("ea"),
            P("ea"),
            P("ea", "ha"),
            P("ea"),
            P("ea"),
            P("ea"),
            P("ea", "ha"),
            P("ha"),
            P("ha", "ea"),
            P("ea"),
        ),
        check_vma=False,
    )
```

```python
from functools import partial

import jax
import jax.numpy as jnp
from jax import lax
from jax.experimental import pallas as pl
from jax.experimental.pallas import tpu as pltpu
from jax.sharding import PartitionSpec as P

HEAD_DIM = 64
GRID = 14
EPSILON = 1e-06
NEGATIVE = -1e30
BLOCKS = 8
VEC_ROWS = 16
NN = (((1,), (0,)), ((), ()))
NT = (((1,), (1,)), ((), ()))
TN = (((0,), (0,)), ((), ()))
F32 = jnp.float32
BF16 = jnp.bfloat16
SMEM = pl.BlockSpec(memory_space=pltpu.SMEM)
VMEM = pl.BlockSpec(memory_space=pltpu.VMEM)
PARAMS = pltpu.CompilerParams(vmem_limit_bytes=56 * 1024 * 1024)


def dot(a, b, dims):
    return lax.dot_general(a, b, dims, preferred_element_type=F32)


def iota(shape, axis):
    return lax.broadcasted_iota(jnp.int32, shape, axis)


def prefix(counts, starts):
    total = jnp.int32(0)
    for i in range(counts.shape[0]):
        starts[i] = total
        total = total + counts[i]


def select_rows(sel, counts, starts, part, images, rows, window, slots):
    first = starts[part * images]
    base = jnp.minimum(first // 128, (slots - window) // 128) * 128
    base = pl.multiple_of(base, 128)
    row = iota((rows, window), 0)
    gap = iota((rows, window), 1) - row
    for i in range(images):
        image = part * images + i
        hit = (gap == starts[image] - base) & (row < counts[image])
        sel[i * rows : (i + 1) * rows, :] = jnp.where(hit, 1.0, 0.0).astype(BF16)
    return base


def pack_kernel(images, rows, window, meta, counts, tokens, cotangent, packed, starts, sel):
    prefix(counts, starts)
    for d in range(packed.shape[0]):
        base = select_rows(
            sel, counts, starts, meta[0] ^ d, images, rows, window, tokens.shape[1]
        )
        span = pl.ds(base, window)
        both = jnp.concatenate([tokens[:, span], cotangent[:, span]], 0)
        packed[d] = dot(sel[...], both, NT).astype(BF16)


def shard_kernel(qkv, out, into, back, hidden_bias, query, value, *refs):
    vectors, (first, second) = refs[:-2], refs[-2:]
    narrow, half = qkv.shape
    width = first.shape[1]
    first[:narrow, :half] = qkv[...]
    first[:narrow, half:] = out[...]
    empty = jnp.zeros((1, width), F32)
    wide = lambda ref: ref[...].astype(F32).reshape(1, -1)
    rows = [jnp.concatenate([wide(ref), empty[:, narrow:]], 1) for ref in vectors]
    query, value = wide(query), wide(value)
    shift = []
    for i in range(narrow // HEAD_DIM):
        at = slice(i * HEAD_DIM, (i + 1) * HEAD_DIM)
        shift += [query[:, at], empty[:, :HEAD_DIM], value[:, at]]
    shift = jnp.concatenate(shift + [empty[:, : 2 * width - 2 * half]], 1)
    rows += [shift[:, :width], shift[:, width:], wide(hidden_bias)]
    rows.append(jnp.zeros((VEC_ROWS - len(rows), width), F32))
    first[narrow:, :] = jnp.concatenate(rows, 0).astype(BF16)
    second[:narrow, :] = into[...]
    second[narrow:, :] = back[...]


def unpack_kernel(images, rows, window, meta, counts, *refs):
    outs, grads, (output, grad, starts, sel, total, grad_total) = refs[:4], refs[4:8], refs[8:]
    narrow, slots = output.shape
    prefix(counts, starts)
    total[...] = jnp.zeros_like(total)
    grad_total[...] = jnp.zeros_like(grad_total)
    for d in range(len(outs)):
        base = select_rows(sel, counts, starts, meta[0] ^ d, images, rows, window, slots)
        span = pl.ds(base, window)
        for pair, into in ((outs[d], total), (grads[d], grad_total)):
            tall = jnp.concatenate([pair[:, :narrow], pair[:, narrow:]], 0)
            into[:, span] += dot(tall, sel[...], TN)
    output[...] = total[...].astype(output.dtype)
    grad[...] = grad_total[...]


def store_halves(out, values):
    low, narrow = out.shape[1], out.shape[2] // 2
    for d in range(out.shape[0]):
        span = slice(d * narrow, (d + 1) * narrow)
        out[d] = jnp.concatenate([values[:low, span], values[low:, span]], 1).astype(out.dtype)


def norm_parts(values):
    center = jnp.mean(values, 1, keepdims=True)
    centred = values - center
    factor = lax.rsqrt(jnp.mean(centred * centred, 1, keepdims=True) + EPSILON)
    return centred * factor, factor


def norm_back(grad, xhat, factor, gain):
    scaled = grad * gain
    mean = jnp.mean(scaled, 1, keepdims=True)
    across = jnp.mean(scaled * xhat, 1, keepdims=True)
    return factor * (scaled - mean - xhat * across)


def colsum(values):
    return jnp.sum(values, 0, keepdims=True)


def place(d, core):
    return d if d in (0, 3) else jnp.where(core == 0, d, 3 - d)


def column_of(meta, p, s):
    core = meta[2] ^ p
    z = (meta[1] + core + 2 * (s // 2)) % 4
    return z, core ^ (s % 2)


def whole_block(refs, s, rows, swap):
    one, two = refs[1][s, rows], refs[2][s, rows]
    return jnp.concatenate(
        [refs[0][s, rows], jnp.where(swap, two, one), jnp.where(swap, one, two), refs[3][s, rows]], 0
    )


def attend_kernel(images, rows, meta, counts, *refs):
    x_refs, (patches, sines, cosines), arrays = refs[:4], refs[4:7], (refs[7:11], refs[11:15])
    x1_out, x0, h1_out, qkv_out, p_out, o_out, vecs, inb, wq, wo = refs[15:25]
    shifts, wo_parts = refs[25:]
    me = meta[0]
    parts = len(x_refs)
    narrow = x_refs[0].shape[1] // 2
    wide = 3 * narrow
    half = wide // 2
    outer = narrow // 2
    heads = narrow // HEAD_DIM

    def unfold(core):
        for p in range(2):
            for a in range(parts):
                d = a if a in (0, 3) or (core ^ p) == 0 else 3 - a
                low, high = d * narrow, (d + 1) * narrow
                for s in range(4):
                    z = (meta[1] + (core ^ p) + 2 * (s // 2)) % 4
                    k = core ^ p ^ (s % 2)
                    ref = arrays[p][a]
                    wq[z, low:high, k * half : (k + 1) * half] = ref[s, :narrow, :half]
                    wo_parts[me ^ d, z, :, k * outer : (k + 1) * outer] = ref[s, :narrow, half:]
                    if a == 0:
                        inb[2 * z + k] = ref[s, narrow:, :].astype(F32)[8:9]
                if p == 0:
                    small = arrays[p][a][0, narrow:, :].astype(F32)
                    vecs[:, low:high] = small[:, :narrow]
                    rest = small[7:8, : wide - small.shape[1]]
                    shifts[me ^ d] = jnp.concatenate([small[6:7], rest], 1)

    pl.when(meta[2] == 0)(partial(unfold, 0))
    pl.when(meta[2] == 1)(partial(unfold, 1))
    for t in range(parts):
        for d in range(parts):
            wo[t, :, d * narrow : (d + 1) * narrow] = wo_parts[t, me ^ d]
    for d in range(parts):
        e = me ^ d
        table = jnp.where(e % 2 == 0, sines[...], cosines[...])
        high = table.astype(BF16)
        rest = table - high.astype(F32)
        middle = rest.astype(BF16)
        low = (rest - middle.astype(F32)).astype(BF16)
        stacked = jnp.concatenate([high, middle, low], 0)
        depth = table.shape[0]
        for i in range(images):
            patch = patches[pl.ds(me * images + i, 1), :rows]
            row = (patch * 4682) >> 16
            spot = jnp.where(e < 2, row, patch - row * GRID)
            hot = jnp.where(iota((depth, rows), 0) == spot, 1.0, 0.0).astype(BF16)
            placed = dot(jnp.concatenate([hot, hot, hot], 0), stacked, TN)
            x0[i * rows : (i + 1) * rows, d * narrow : (d + 1) * narrow] = (
                x_refs[d][i * rows : (i + 1) * rows, :narrow].astype(F32) + placed
            )
    xhat, _ = norm_parts(x0[...])
    h1 = (xhat * vecs[0:1] + vecs[1:2]).astype(BF16)
    h1_out[...] = h1
    for z in range(parts):
        qkv_out[z] = (dot(h1, wq[z], NN) + shifts[z]).astype(BF16)
    factor = HEAD_DIM ** (-0.5)
    for b in range(images):
        seen = iota((rows, rows), 1) < counts[me * images + b]
        span = slice(b * rows, (b + 1) * rows)
        for z in range(parts):
            mixed = []
            for i in range(heads):
                at = 3 * HEAD_DIM * i
                query = qkv_out[z, span, at : at + HEAD_DIM]
                key = qkv_out[z, span, at + HEAD_DIM : at + 2 * HEAD_DIM]
                value = qkv_out[z, span, at + 2 * HEAD_DIM : at + 3 * HEAD_DIM]
                scores = jnp.where(seen, dot(query, key, NT) * factor, NEGATIVE)
                weights = jnp.exp(scores - jnp.max(scores, 1, keepdims=True))
                chance = (weights / jnp.sum(weights, 1, keepdims=True)).astype(BF16)
                p_out[z * heads + i, b] = chance
                mixed.append(dot(chance, value, NN).astype(BF16))
            o_out[span, z * narrow : (z + 1) * narrow] = jnp.concatenate(mixed, 1)
    attn = dot(o_out[...], jnp.concatenate([wo[z] for z in range(parts)], 0), NN)
    x1_out[...] = x0[...] + attn + vecs[4:5]


def hidden_step(p, meta, h2, dy, inb, refs):
    narrow = refs[0].shape[1] // 2
    step = pl.program_id(0)
    swap = (meta[2] ^ p) == 1
    z, k = column_of(meta, p, step)
    w_in = whole_block(refs, 0, slice(0, narrow), swap)
    w_back = whole_block(refs, 0, slice(narrow, 2 * narrow), swap)
    hidden = dot(h2, w_in, NN) + inb[2 * z + k]
    gate = 0.5 + 0.5 * lax.erf(hidden * (0.5**0.5))
    active = (hidden * gate).astype(BF16)
    slope = gate + hidden * jnp.exp(-0.5 * hidden * hidden) * 0.3989422804014327
    low = (dot(dy, w_back, NN) * slope).astype(BF16)
    return active, low, dot(active, w_back, NT), dot(low, w_in, NT)


def hidden_a_kernel(meta, *refs):
    x1, y_refs, (vecs, inb), arrays = refs[0], refs[1:5], refs[5:7], refs[7:11]
    sent, dinb, h2s, dys, y_total, dh_total = refs[11:]
    parts, narrow = len(y_refs), y_refs[0].shape[1] // 2

    @pl.when(pl.program_id(0) == 0)
    def _():
        for d in range(parts):
            dys[:, d * narrow : (d + 1) * narrow] = y_refs[d][:, narrow:]
        xhat, _ = norm_parts(x1[...])
        h2s[...] = (xhat * vecs[2:3] + vecs[3:4]).astype(BF16)
        y_total[...] = jnp.zeros_like(y_total)
        dh_total[...] = jnp.zeros_like(dh_total)

    h2, dy = h2s[...], dys[...]
    active, low, y_part, dh_part = hidden_step(0, meta, h2, dy, inb, arrays)
    y_total[...] += y_part
    dh_total[...] += dh_part
    dinb[0] = colsum(low.astype(F32))
    d_in = dot(h2, low, TN).astype(BF16)
    d_back = dot(dy, active, TN).astype(BF16)
    for d in range(parts):
        q = place(d, 1 - meta[2])
        sent[q, 0, :narrow] = d_in[d * narrow : (d + 1) * narrow]
        sent[q, 0, narrow:] = d_back[d * narrow : (d + 1) * narrow]


def hidden_b_kernel(meta, x1, h2s, dys, y_first, dh_first, vecs, inb, *refs):
    arrays = refs[:4]
    act, dus, dinb, out, dx1, da, vec_grads, y_total, dh_total = refs[4:]
    step = pl.program_id(0)

    @pl.when(step == 0)
    def _():
        y_total[...] = y_first[...]
        dh_total[...] = dh_first[...]

    active, low, y_part, dh_part = hidden_step(1, meta, h2s[...], dys[...], inb, arrays)
    act[...] = active
    dus[...] = low
    y_total[...] += y_part
    dh_total[...] += dh_part
    dinb[0] = colsum(low.astype(F32))

    @pl.when(step == pl.num_programs(0) - 1)
    def _():
        values = x1[...]
        store_halves(out, values + y_total[...] + vecs[5:6])
        xhat, factor = norm_parts(values)
        grad = dh_total[...]
        dy_wide = dys[...].astype(F32)
        total = dy_wide + norm_back(grad, xhat, factor, vecs[2:3])
        dx1[...] = total
        narrowed = total.astype(BF16)
        da[...] = narrowed
        vec_grads[0:1] = colsum(grad * xhat)
        vec_grads[1:2] = colsum(grad)
        vec_grads[2:3] = colsum(narrowed.astype(F32))
        vec_grads[3:4] = colsum(dy_wide)
        vec_grads[4:8] = jnp.zeros_like(vec_grads[4:8])


def hidden_grad_kernel(meta, h2s, dys, act, dus, arrived, kept, sent, d_in, d_back):
    narrow = kept.shape[2] // 2
    d_in[...] = dot(h2s[...], dus[...], TN)
    d_back[...] = dot(dys[...], act[...], TN)
    for q in range(4):
        start = place(q, meta[2]) * narrow
        span = pl.ds(pl.multiple_of(start, narrow) if q in (1, 2) else start, narrow)
        into = kept if q < 2 else sent
        top = d_in[span, :] + arrived[q, 0, :narrow].astype(F32)
        low = d_back[span, :] + arrived[q, 0, narrow:].astype(F32)
        into[q % 2, 0, :narrow] = top.astype(BF16)
        into[q % 2, 0, narrow:] = low.astype(BF16)


def attend_back_kernel(images, rows, da, o_ref, qkv, p_ref, wo, dqkv, dwo, dshift, do_ref):
    parts, narrow = wo.shape[0], wo.shape[1]
    heads = narrow // HEAD_DIM
    factor = HEAD_DIM ** (-0.5)
    grad = da[...]
    for z in range(parts):
        do_ref[z] = dot(grad, wo[z], NT).astype(BF16)
        dw = dot(o_ref[:, z * narrow : (z + 1) * narrow], grad, TN)
        for d in range(parts):
            dwo[z, d] = dw[:, d * narrow : (d + 1) * narrow]
    for b in range(images):
        span = slice(b * rows, (b + 1) * rows)
        for z in range(parts):
            grads = []
            for i in range(heads):
                at = 3 * HEAD_DIM * i
                query = qkv[z, span, at : at + HEAD_DIM]
                key = qkv[z, span, at + HEAD_DIM : at + 2 * HEAD_DIM]
                value = qkv[z, span, at + 2 * HEAD_DIM : at + 3 * HEAD_DIM]
                grad_head = do_ref[z, span, i * HEAD_DIM : (i + 1) * HEAD_DIM]
                low = p_ref[z * heads + i, b]
                chance = low.astype(F32)
                grad_chance = dot(grad_head, value, NT)
                inner = jnp.sum(chance * grad_chance, 1, keepdims=True)
                grad_score = (chance * (grad_chance - inner)).astype(BF16)
                grads.append((dot(grad_score, key, NN) * factor).astype(BF16))
                grads.append((dot(grad_score, query, TN) * factor).astype(BF16))
                grads.append(dot(low, grad_head, TN).astype(BF16))
            dqkv[z, span, :] = jnp.concatenate(grads, 1)
    for z in range(parts):
        dshift[z] = colsum(dqkv[z].astype(F32))


def first_back_kernel(x0, dqkv, wq, dx1, vecs, vec_grads, gx, vec_rows, rows_out):
    parts, narrow = gx.shape[0], gx.shape[2] // 2
    grad = dot(dqkv[0], wq[0], NT)
    for z in range(1, parts):
        grad += dot(dqkv[z], wq[z], NT)
    xhat, factor = norm_parts(x0[...])
    store_halves(gx, dx1[...] + norm_back(grad, xhat, factor, vecs[0:1]))
    rows_out[0:1] = colsum(grad * xhat)
    rows_out[1:2] = colsum(grad)
    rows_out[2:6] = vec_grads[0:4]
    rows_out[6:8] = jnp.zeros_like(rows_out[6:8])
    for d in range(parts):
        vec_rows[d] = rows_out[:, d * narrow : (d + 1) * narrow]


def first_grad(p, meta, h1, dqkv, dwo, dshift, dinb, vec_rows, dw, store):
    me = meta[0]
    width = dinb.shape[2]
    narrow = dwo.shape[2]
    half, outer = 3 * narrow // 2, narrow // 2
    gap = jnp.zeros((6, width - narrow), F32)
    feature = h1[...]
    for jj in range(2):
        z, _ = column_of(meta, p, 2 * jj)
        dw[...] = dot(feature, dqkv[z], TN)
        for q in range(4):
            d = place(q, meta[2] ^ 1 ^ p)
            start = d * narrow
            span = pl.ds(pl.multiple_of(start, narrow) if q in (1, 2) else start, narrow)
            both, out_both = dw[span, :], dwo[me ^ d, z ^ me]
            shift = dshift[me ^ d]
            second = jnp.concatenate([shift[:, width:], gap[0:1, : 2 * width - 2 * half]], 1)
            six = vec_rows[d, 0:6, :]
            six = jnp.concatenate([six, gap], 1)
            for m in range(2):
                s = 2 * jj + m
                _, k = column_of(meta, p, s)
                left = jnp.where(k == 0, both[:, :half], both[:, half:])
                right = jnp.where(k == 0, out_both[:, :outer], out_both[:, outer:])
                tail = [six, shift[:, :width], second, dinb[s], jnp.zeros((7, width), F32)]
                store(q, s, jnp.concatenate([left, right], 1), jnp.concatenate(tail, 0))


def first_sent_kernel(meta, h1, dqkv, dwo, dshift, dinb, vec_rows, sent, dw):
    narrow = dwo.shape[2]

    def store(q, s, top, low):
        sent[q, s, :narrow] = top.astype(BF16)
        sent[q, s, narrow:] = low.astype(BF16)

    first_grad(0, meta, h1, dqkv, dwo, dshift, dinb, vec_rows, dw, store)


def first_kept_kernel(meta, h1, dqkv, dwo, dshift, dinb, vec_rows, arrived, kept, sent, dw):
    narrow = dwo.shape[2]

    def store(q, s, top, low):
        into = kept if q < 2 else sent
        into[q % 2, s, :narrow] = (top + arrived[q, s, :narrow].astype(F32)).astype(BF16)
        into[q % 2, s, narrow:] = (low + arrived[q, s, narrow:].astype(F32)).astype(BF16)

    first_grad(1, meta, h1, dqkv, dwo, dshift, dinb, vec_rows, dw, store)


def call(kernel, outs, operands, scratch=(), name=None):
    specs = []
    for value in operands:
        specs.append(SMEM if value.dtype == jnp.int32 and value.ndim == 1 else VMEM)
    return pl.pallas_call(
        kernel,
        out_shape=outs,
        in_specs=specs,
        out_specs=jax.tree.map(lambda _: VMEM, outs),
        scratch_shapes=scratch,
        compiler_params=PARAMS,
        name=name,
    )(*operands)


def shaped(dtype, *shape):
    return jax.ShapeDtypeStruct(shape, dtype)


def exchange(block, d):
    size = lax.axis_size("ea")
    return block if d == 0 else lax.ppermute(block, "ea", [(e, e ^ d) for e in range(size)])


class Wires:
    def __init__(self, parts, columns):
        self.parts, self.chips = parts, columns // 2

    def over_z(self, blocks, back=False):
        pulled = []
        for s in range(4):
            pairs = []
            for z in range(self.chips):
                for c in range(2):
                    core = 1 - c if back else c
                    far = (z + core + 2 * (s // 2)) % self.chips
                    there, here = 2 * far + (core ^ (s % 2)), 2 * z + c
                    pairs.append((here, there) if back else (there, here))
            pulled.append(lax.ppermute(blocks[s], "ha", pairs))
        return pulled

    def swap(self, block):
        return lax.ppermute(block, "ha", [(h, h ^ 1) for h in range(2 * self.chips)])

    def stage(self, block, second):
        pairs = []
        columns = 2 * self.chips
        for e in range(self.parts):
            for h in range(columns):
                d = 1 + ((h % 2) ^ second)
                pairs.append((e * columns + h, (e ^ d) * columns + h))
        return lax.ppermute(block, ("ea", "ha"), pairs)

    def spread(self, mine):
        one = self.stage(mine, 0)
        two = self.stage(mine, 1)
        three = self.stage(one, 1)
        own = (mine, one, two, three)
        return own, tuple(self.swap(block) for block in own)

    def finish(self, once, arrived):
        total = add(once, arrived)
        return self.over_z([total[s] for s in range(4)], back=True)


def after(value, *others):
    return lax.optimization_barrier((value, others))[0]


def add(a, b):
    return (a.astype(F32) + b.astype(F32)).astype(BF16)


def vector_rows(vectors, shift, bias):
    width = bias.shape[-1]
    rows = [jnp.pad(v, (0, width - v.shape[0])) for v in vectors]
    rows += [shift[:width], jnp.pad(shift[width:], (0, 2 * width - shift.shape[0])), bias]
    return jnp.stack(rows + [jnp.zeros_like(bias)] * (VEC_ROWS - len(rows)))


def grid_call(kernel, outs, out_specs, operands, in_specs, scratch, name):
    return pl.pallas_call(
        kernel,
        grid=(4,),
        out_shape=outs,
        in_specs=in_specs,
        out_specs=out_specs,
        scratch_shapes=scratch,
        compiler_params=PARAMS,
        name=name,
    )(*operands)


def whole_spec(*shape):
    return pl.BlockSpec(shape, lambda s: (0,) * len(shape))


def shards(
    tokens,
    image_counts,
    kept_patches,
    norm1_gain,
    norm1_bias,
    qkv_weight,
    query_bias,
    value_bias,
    out_weight,
    out_bias,
    norm2_gain,
    norm2_bias,
    in_weight,
    in_bias,
    back_weight,
    back_bias,
    cotangent,
):
    parts = lax.axis_size("ea")
    columns = lax.axis_size("ha")
    me = lax.axis_index("ea")
    mine = lax.axis_index("ha")
    direct = columns == BLOCKS
    wires = Wires(parts, columns)
    if direct:
        meta = jnp.stack([me, mine // 2, mine % 2]).astype(jnp.int32)
    else:
        meta = jnp.stack([me, 0 * mine, 0 * mine]).astype(jnp.int32)
    narrow, slots = tokens.shape
    full = narrow * parts
    images = image_counts.shape[0] // parts
    most = kept_patches.shape[1]
    rows = -(-most // 16) * 16
    count = images * rows
    window = min(slots, (images * most + 127 + 127) // 128 * 128)
    heads = full // HEAD_DIM
    group_heads = narrow // HEAD_DIM
    width = in_weight.shape[1] * columns // BLOCKS
    half = 3 * narrow // 2

    vectors = (norm1_gain, norm1_bias, norm2_gain, norm2_bias, out_bias, back_bias)
    if direct:
        first, second = call(
            shard_kernel,
            (shaped(BF16, narrow + VEC_ROWS, width), shaped(BF16, 2 * narrow, width)),
            (qkv_weight, out_weight, in_weight, back_weight.T, in_bias, query_bias, value_bias)
            + vectors,
            name="shard",
        )
        z_first = wires.over_z([first] * 4)
        tokens = after(tokens, first)

    packed = call(
        partial(pack_kernel, images, rows, window),
        shaped(BF16, parts, count, 2 * narrow),
        (meta, image_counts, tokens, cotangent),
        (pltpu.SMEM((image_counts.shape[0],), jnp.int32), pltpu.VMEM((count, window), BF16)),
        "pack",
    )
    xs = [exchange(packed[d], d) for d in range(parts)]

    if direct:
        z_first = jnp.stack(after(z_first, *xs))
        z_second = wires.over_z([after(second, z_first)] * 4)
        g1 = wires.spread(z_first)
        z_second = jnp.stack(after(z_second, g1[0][3]))
        g2 = wires.spread(z_second)
        xs = after(xs, z_second)
    else:
        pairs = jnp.zeros((group_heads, HEAD_DIM), BF16)
        by_head = lambda bias: bias.reshape(group_heads, HEAD_DIM)
        shift = jnp.stack([by_head(query_bias), pairs, by_head(value_bias)], 1).reshape(-1)

        def whole(weight):
            wide = lax.all_gather(weight, "ha", axis=1, tiled=True)
            blocks = wide.reshape(narrow, BLOCKS, -1).transpose(1, 0, 2)
            return lax.all_gather(blocks, "ea")

        def arrange(blocks):
            sides = []
            for p in range(2):
                side = []
                for a in range(parts):
                    d = a if p == 0 or a in (0, 3) else 3 - a
                    row = lax.dynamic_index_in_dim(blocks, me ^ d, 0, False)
                    side.append(jnp.stack([row[2 * (p + 2 * (s // 2)) + (p ^ (s % 2))] for s in range(4)]))
                sides.append(tuple(side))
            return sides

        biases = lax.all_gather(in_bias, "ha", tiled=True).reshape(BLOCKS, -1)
        below = jax.vmap(lambda bias: vector_rows(vectors, shift, bias))(biases)
        g1 = jnp.concatenate([whole(qkv_weight), whole(out_weight)], 3)
        g1 = arrange(jnp.concatenate([g1, lax.all_gather(below, "ea")], 2))
        g2 = arrange(jnp.concatenate([whole(in_weight), whole(back_weight.T)], 2))

    omega = 1.0 / 10000.0 ** (jnp.arange(narrow, dtype=F32) / narrow)
    angles = jnp.arange(16, dtype=F32)[:, None] * omega[None, :]
    patches = jnp.pad(kept_patches, ((0, 0), (0, 128 - most)))

    x1, x0, h1, qkv, chances, mixed, vecs, inb, wq, wo = call(
        partial(attend_kernel, images, rows),
        (
            shaped(F32, count, full),
            shaped(F32, count, full),
            shaped(BF16, count, full),
            shaped(BF16, parts, count, 3 * narrow),
            shaped(BF16, heads, images, rows, rows),
            shaped(BF16, count, full),
            shaped(F32, VEC_ROWS, full),
            shaped(F32, BLOCKS, 1, width),
            shaped(BF16, parts, full, 3 * narrow),
            shaped(BF16, parts, narrow, full),
        ),
        (meta, image_counts, *xs, patches, jnp.sin(angles), jnp.cos(angles), *g1[0], *g1[1]),
        (
            pltpu.VMEM((parts, 1, 3 * narrow), F32),
            pltpu.VMEM((parts, parts, narrow, narrow), BF16),
        ),
        "attend",
    )

    block_spec = pl.BlockSpec((1, 2 * narrow, width), lambda s: (s, 0, 0))
    slot_spec = pl.BlockSpec((4, 1, 2 * narrow, width), lambda s: (0, s, 0, 0))
    pair_spec = pl.BlockSpec((2, 1, 2 * narrow, width), lambda s: (0, s, 0, 0))
    bias_spec = pl.BlockSpec((1, 1, width), lambda s: (s, 0, 0))
    column_spec = pl.BlockSpec((count, width), lambda s: (0, s))
    inb_spec = whole_spec(BLOCKS, 1, width)
    wide_spec = whole_spec(count, full)
    sent2, dinb_a, h2, dy, y_first, dh_first = grid_call(
        hidden_a_kernel,
        (
            shaped(BF16, 4, 4, 2 * narrow, width),
            shaped(F32, 4, 1, width),
            shaped(BF16, count, full),
            shaped(BF16, count, full),
            shaped(F32, count, full),
            shaped(F32, count, full),
        ),
        (slot_spec, bias_spec, wide_spec, wide_spec, wide_spec, wide_spec),
        (meta, x1, *xs, vecs, inb, *g2[0]),
        [SMEM, wide_spec]
        + [whole_spec(count, 2 * narrow)] * parts
        + [whole_spec(VEC_ROWS, full), inb_spec]
        + [block_spec] * 4,
        (),
        "hidden_a",
    )
    act, dus, dinb_b, outs, dx1, da, vec_grads = grid_call(
        hidden_b_kernel,
        (
            shaped(BF16, count, 4 * width),
            shaped(BF16, count, 4 * width),
            shaped(F32, 4, 1, width),
            shaped(BF16, parts, count // 2, 2 * narrow),
            shaped(F32, count, full),
            shaped(BF16, count, full),
            shaped(F32, 8, full),
        ),
        (
            column_spec,
            column_spec,
            bias_spec,
            whole_spec(parts, count // 2, 2 * narrow),
            wide_spec,
            wide_spec,
            whole_spec(8, full),
        ),
        (meta, x1, h2, dy, y_first, dh_first, vecs, inb, *g2[1]),
        [SMEM] + [wide_spec] * 5 + [whole_spec(VEC_ROWS, full), inb_spec] + [block_spec] * 4,
        (pltpu.VMEM((count, full), F32), pltpu.VMEM((count, full), F32)),
        "hidden_b",
    )
    arrived2 = wires.swap(sent2) if direct else jnp.zeros_like(sent2)
    kept2, passed2 = grid_call(
        hidden_grad_kernel,
        (shaped(BF16, 2, 4, 2 * narrow, width),) * 2,
        (pair_spec, pair_spec),
        (meta, h2, dy, act, dus, arrived2),
        [SMEM, wide_spec, wide_spec, column_spec, column_spec, slot_spec],
        (pltpu.VMEM((full, width), F32), pltpu.VMEM((full, width), F32)),
        "hidden_grad",
    )
    outs = [exchange(outs[d], d) for d in range(parts)]

    dqkv, dwo, dshift = call(
        partial(attend_back_kernel, images, rows),
        (
            shaped(BF16, parts, count, 3 * narrow),
            shaped(F32, parts, parts, narrow, narrow),
            shaped(F32, parts, 1, 3 * narrow),
        ),
        (after(da, kept2), mixed, qkv, chances, wo),
        (pltpu.VMEM((parts, count, narrow), BF16),),
        "attend_back",
    )
    gx, vec_rows = call(
        first_back_kernel,
        (shaped(BF16, parts, count // 2, 2 * narrow), shaped(F32, parts, 8, narrow)),
        (x0, dqkv, wq, dx1, vecs, vec_grads),
        (pltpu.VMEM((8, full), F32),),
        name="first_back",
    )
    if direct:
        arrived = wires.stage(passed2, 1)
        once2, next2 = add(kept2[0], arrived[0]), add(kept2[1], arrived[1])
        h1 = after(h1, next2, gx)
        next2 = wires.stage(next2, 0)
    dw_scratch = (pltpu.VMEM((full, 3 * narrow), F32),)
    block1 = narrow + VEC_ROWS
    sent1 = call(
        first_sent_kernel,
        shaped(BF16, 4, 4, block1, width),
        (meta, h1, dqkv, dwo, dshift, dinb_a, vec_rows),
        dw_scratch,
        "first_sent",
    )
    arrived1 = wires.swap(sent1) if direct else jnp.zeros_like(sent1)
    kept1, passed1 = call(
        first_kept_kernel,
        (shaped(BF16, 2, 4, block1, width),) * 2,
        (meta, h1, dqkv, dwo, dshift, dinb_b, vec_rows, arrived1),
        dw_scratch,
        "first_kept",
    )
    if direct:
        arrived = wires.stage(passed1, 1)
        z_second = wires.finish(once2, after(next2, kept1))
        once1, next1 = add(kept1[0], arrived[0]), add(kept1[1], arrived[1])
        gx = after(gx, next1)
        z_first = wires.finish(once1, wires.stage(next1, 0))

    output, grad_tokens = call(
        partial(unpack_kernel, images, rows, window),
        (shaped(BF16, narrow, slots), shaped(F32, narrow, slots)),
        (meta, image_counts, *outs, *[exchange(gx[d], d) for d in range(parts)]),
        (
            pltpu.SMEM((image_counts.shape[0],), jnp.int32),
            pltpu.VMEM((count, window), BF16),
            pltpu.VMEM((narrow, slots), F32),
            pltpu.VMEM((narrow, slots), F32),
        ),
        "unpack",
    )

    if direct:
        s2 = sum(piece.astype(F32) for piece in z_second)
        s1 = sum(piece.astype(F32) for piece in z_first)
        grad_in, grad_back = s2[:narrow], s2[narrow:]
        grad_qkv, grad_out, small = s1[:narrow, :half], s1[:narrow, half:], s1[narrow:]
        grad_in_bias = small[8]
    else:

        def spread(sent, kept, passed):
            later = jnp.concatenate([kept, passed], 0)
            tall = []
            for e in range(parts):
                d = me ^ e
                row = [None] * BLOCKS
                for p, side in ((0, sent), (1, later)):
                    q = jnp.where((d == 0) | (d == 3) | (p == 1), d, 3 - d)
                    four = lax.dynamic_index_in_dim(side, q, 0, False)
                    for s in range(4):
                        row[2 * (p + 2 * (s // 2)) + (p ^ (s % 2))] = four[s]
                tall.append(jnp.stack(row))
            return jnp.stack(tall).astype(F32)

        def scatter(blocks):
            flat = lax.psum_scatter(blocks, "ea").transpose(1, 0, 2).reshape(narrow, -1)
            return lax.psum_scatter(flat, "ha", scatter_dimension=1, tiled=True)

        d2, d1 = spread(sent2, kept2, passed2), spread(sent1, kept1, passed1)
        grad_in, grad_back = scatter(d2[:, :, :narrow]), scatter(d2[:, :, narrow:])
        grad_qkv, grad_out = scatter(d1[:, :, :narrow, :half]), scatter(d1[:, :, :narrow, half:])
        small = lax.psum(d1[:, :, narrow:], ("ea", "ha"))
        size = in_bias.shape[0]
        grad_in_bias = lax.dynamic_slice_in_dim(small[0, :, 8].reshape(-1), mine * size, size, 0)
        small = lax.dynamic_index_in_dim(small[:, 0], me, 0, False)
    small_shift = jnp.concatenate([small[6], small[7]])[: 3 * narrow]
    small_shift = small_shift.reshape(group_heads, 3, HEAD_DIM)
    return (
        output,
        grad_tokens,
        small[0, :narrow],
        small[1, :narrow],
        grad_qkv,
        small_shift[:, 0].reshape(-1),
        small_shift[:, 2].reshape(-1),
        grad_out,
        small[4, :narrow],
        small[2, :narrow],
        small[3, :narrow],
        grad_in,
        grad_in_bias,
        grad_back.T,
        small[5, :narrow],
    )


def solution(mesh):
    return jax.shard_map(
        shards,
        mesh=mesh,
        in_specs=(
            P("ea", "ha"),
            P("ha"),
            P("ha", None),
            P("ea"),
            P("ea"),
            P("ea", "ha"),
            P("ea"),
            P("ea"),
            P("ea", "ha"),
            P("ea"),
            P("ea"),
            P("ea"),
            P("ea", "ha"),
            P("ha"),
            P("ha", "ea"),
            P("ea"),
            P("ea", "ha"),
        ),
        out_specs=(
            P("ea", "ha"),
            P("ea", "ha"),
            P("ea"),
            P("ea"),
            P("ea", "ha"),
            P("ea"),
            P("ea"),
            P("ea", "ha"),
            P("ea"),
            P("ea"),
            P("ea"),
            P("ea", "ha"),
            P("ha"),
            P("ha", "ea"),
            P("ea"),
        ),
        check_vma=False,
    )
```

```python
from functools import partial

import jax
import jax.numpy as jnp
from jax import lax
from jax.experimental import pallas as pl
from jax.experimental.pallas import tpu as pltpu
from jax.sharding import PartitionSpec as P

HEAD_DIM = 64
GRID = 14
EPSILON = 1e-06
NEGATIVE = -1e30
BLOCKS = 8
VEC_ROWS = 16
NN = (((1,), (0,)), ((), ()))
NT = (((1,), (1,)), ((), ()))
TN = (((0,), (0,)), ((), ()))
F32 = jnp.float32
BF16 = jnp.bfloat16
SMEM = pl.BlockSpec(memory_space=pltpu.SMEM)
VMEM = pl.BlockSpec(memory_space=pltpu.VMEM)
PARAMS = pltpu.CompilerParams(vmem_limit_bytes=56 * 1024 * 1024)


def dot(a, b, dims):
    return lax.dot_general(a, b, dims, preferred_element_type=F32)


def iota(shape, axis):
    return lax.broadcasted_iota(jnp.int32, shape, axis)


def prefix(counts, starts):
    total = jnp.int32(0)
    for i in range(counts.shape[0]):
        starts[i] = total
        total = total + counts[i]


def select_rows(sel, counts, starts, part, images, rows, window, slots):
    first = starts[part * images]
    base = jnp.minimum(first // 128, (slots - window) // 128) * 128
    base = pl.multiple_of(base, 128)
    row = iota((rows, window), 0)
    gap = iota((rows, window), 1) - row
    for i in range(images):
        image = part * images + i
        hit = (gap == starts[image] - base) & (row < counts[image])
        sel[i * rows : (i + 1) * rows, :] = jnp.where(hit, 1.0, 0.0).astype(BF16)
    return base


def pack_kernel(images, rows, window, meta, counts, tokens, cotangent, *refs):
    (mine, pair, single), (starts, sel) = refs[:3], refs[3:]
    prefix(counts, starts)
    for a in range(4):
        part = meta[0] ^ place(a, meta[2])
        base = select_rows(sel, counts, starts, part, images, rows, window, tokens.shape[1])
        span = pl.ds(base, window)
        both = jnp.concatenate([tokens[:, span], cotangent[:, span]], 0)
        block = dot(sel[...], both, NT).astype(BF16)
        if a in (0, 2):
            (single if a else mine)[...] = block
        else:
            pair[a // 2] = block


def shard_kernel(qkv, out, into, back, hidden_bias, query, value, *refs):
    vectors, (first, second) = refs[:-2], refs[-2:]
    narrow, half = qkv.shape
    width = first.shape[1]
    first[:narrow, :half] = qkv[...]
    first[:narrow, half:] = out[...]
    empty = jnp.zeros((1, width), F32)
    wide = lambda ref: ref[...].astype(F32).reshape(1, -1)
    rows = [jnp.concatenate([wide(ref), empty[:, narrow:]], 1) for ref in vectors]
    query, value = wide(query), wide(value)
    shift = []
    for i in range(narrow // HEAD_DIM):
        at = slice(i * HEAD_DIM, (i + 1) * HEAD_DIM)
        shift += [query[:, at], empty[:, :HEAD_DIM], value[:, at]]
    shift = jnp.concatenate(shift + [empty[:, : 2 * width - 2 * half]], 1)
    rows += [shift[:, :width], shift[:, width:], wide(hidden_bias)]
    rows.append(jnp.zeros((VEC_ROWS - len(rows), width), F32))
    first[narrow:, :] = jnp.concatenate(rows, 0).astype(BF16)
    second[:narrow, :] = into[...]
    second[narrow:, :] = back[...]


def unpack_kernel(images, rows, window, meta, counts, *refs):
    outs, grads, second = refs[:2], refs[2:4], refs[4]
    output, grad, starts, sel, total, grad_total = refs[5:]
    narrow, slots = output.shape
    prefix(counts, starts)
    total[...] = jnp.zeros_like(total)
    grad_total[...] = jnp.zeros_like(grad_total)
    for a in range(4):
        part = meta[0] ^ place(a, meta[2])
        base = select_rows(sel, counts, starts, part, images, rows, window, slots)
        span = pl.ds(base, window)
        for i, (refs, into) in enumerate(((outs, total), (grads, grad_total))):
            pair = refs[0][...] if a == 0 else refs[1][0] if a == 1 else second[2 * i + a - 2]
            tall = jnp.concatenate([pair[:, :narrow], pair[:, narrow:]], 0)
            into[:, span] += dot(tall, sel[...], TN)
    output[...] = total[...].astype(output.dtype)
    grad[...] = grad_total[...]


def store_halves(core, mine, pair, single, values):
    low, narrow = mine.shape[0], mine.shape[1] // 2
    parts = []
    for d in range(4):
        span = slice(d * narrow, (d + 1) * narrow)
        both = [values[:low, span], values[low:, span]]
        parts.append(jnp.concatenate(both, 1).astype(mine.dtype))
    mine[...] = parts[0]
    pair[0] = jnp.where(core == 0, parts[1], parts[2])
    single[...] = jnp.where(core == 0, parts[2], parts[1])
    pair[1] = parts[3]


def turned(core, mine, first, second):
    one, two = first[0], second[0]
    swap = core == 1
    return [mine[...], jnp.where(swap, two, one), jnp.where(swap, one, two), second[1]]


def norm_parts(values):
    center = jnp.mean(values, 1, keepdims=True)
    centred = values - center
    factor = lax.rsqrt(jnp.mean(centred * centred, 1, keepdims=True) + EPSILON)
    return centred * factor, factor


def norm_back(grad, xhat, factor, gain):
    scaled = grad * gain
    mean = jnp.mean(scaled, 1, keepdims=True)
    across = jnp.mean(scaled * xhat, 1, keepdims=True)
    return factor * (scaled - mean - xhat * across)


def colsum(values):
    return jnp.sum(values, 0, keepdims=True)


def place(d, core):
    return d if d in (0, 3) else jnp.where(core == 0, d, 3 - d)


def column_of(meta, p, s):
    return (meta[1] + s) % 4, meta[2] ^ p


def whole_block(refs, rows, swap):
    columns = []
    for s in range(2):
        one, two = refs[1][s, rows], refs[2][s, rows]
        one, two = jnp.where(swap, two, one), jnp.where(swap, one, two)
        columns.append(jnp.concatenate([refs[0][s, rows], one, two, refs[3][s, rows]], 0))
    return jnp.concatenate(columns, 1)


def head_part(qkv, z, span, head, part):
    at = (3 * head + part) * HEAD_DIM
    return qkv[z, span, at : at + HEAD_DIM]


def attend_kernel(images, rows, meta, counts, *refs):
    x_refs, (patches, sines, cosines), arrays = refs[:3], refs[3:6], (refs[6:10], refs[10:14])
    x1_out, x0, h1_out, qkv_out, p_out, o_out, vecs, inb, wq, wo = refs[14:24]
    shifts, wo_parts = refs[24:]
    me = meta[0]
    parts, narrow = wo.shape[0], wo.shape[1]
    wide = 3 * narrow
    half = wide // 2
    outer = narrow // 2
    heads = narrow // HEAD_DIM

    def unfold(core):
        for p in range(2):
            for a in range(parts):
                d = a if a in (0, 3) or (core ^ p) == 0 else 3 - a
                low, high = d * narrow, (d + 1) * narrow
                for s in range(4):
                    z = (meta[1] + s) % 4
                    k = core ^ p
                    ref = arrays[p][a]
                    wq[z, low:high, k * half : (k + 1) * half] = ref[s, :narrow, :half]
                    wo_parts[me ^ d, z, :, k * outer : (k + 1) * outer] = ref[s, :narrow, half:]
                    if a == 0:
                        inb[2 * z + k] = ref[s, narrow:, :].astype(F32)[8:9]
                if p == 0:
                    small = arrays[p][a][0, narrow:, :].astype(F32)
                    vecs[:, low:high] = small[:, :narrow]
                    rest = small[7:8, : wide - small.shape[1]]
                    shifts[me ^ d] = jnp.concatenate([small[6:7], rest], 1)

    pl.when(meta[2] == 0)(partial(unfold, 0))
    pl.when(meta[2] == 1)(partial(unfold, 1))
    for t in range(parts):
        for d in range(parts):
            wo[t, :, d * narrow : (d + 1) * narrow] = wo_parts[t, me ^ d]
    tokens = turned(meta[2], *x_refs)
    for d in range(parts):
        e = me ^ d
        table = jnp.where(e % 2 == 0, sines[...], cosines[...])
        high = table.astype(BF16)
        rest = table - high.astype(F32)
        middle = rest.astype(BF16)
        low = (rest - middle.astype(F32)).astype(BF16)
        stacked = jnp.concatenate([high, middle, low], 0)
        depth = table.shape[0]
        for i in range(images):
            patch = patches[pl.ds(me * images + i, 1), :rows]
            row = (patch * 4682) >> 16
            spot = jnp.where(e < 2, row, patch - row * GRID)
            hot = jnp.where(iota((depth, rows), 0) == spot, 1.0, 0.0).astype(BF16)
            placed = dot(jnp.concatenate([hot, hot, hot], 0), stacked, TN)
            x0[i * rows : (i + 1) * rows, d * narrow : (d + 1) * narrow] = (
                tokens[d][i * rows : (i + 1) * rows, :narrow].astype(F32) + placed
            )
    xhat, _ = norm_parts(x0[...])
    h1 = (xhat * vecs[0:1] + vecs[1:2]).astype(BF16)
    h1_out[...] = h1
    for z in range(parts):
        qkv_out[z] = (dot(h1, wq[z], NN) + shifts[z]).astype(BF16)
    factor = HEAD_DIM ** (-0.5)
    each = [(z, i) for z in range(parts) for i in range(heads)]
    for b in range(images):
        seen = iota((rows, rows), 0) < counts[me * images + b]
        span = slice(b * rows, (b + 1) * rows)
        scores, mixed = [], []
        for z, i in each:
            query, key = (head_part(qkv_out, z, span, i, part) for part in (0, 1))
            scores.append(jnp.where(seen, dot(key, query, NT) * factor, NEGATIVE))
        for n, score in enumerate(scores):
            weights = jnp.exp(score - jnp.max(score, 0, keepdims=True))
            scale = 1.0 / jnp.sum(weights, 0, keepdims=True)
            p_out[n, b] = (weights * scale).astype(BF16)
        for n, (z, i) in enumerate(each):
            value = head_part(qkv_out, z, span, i, 2)
            mixed.append(dot(p_out[n, b], value, TN).astype(BF16))
        for z in range(parts):
            together = jnp.concatenate(mixed[z * heads : (z + 1) * heads], 1)
            o_out[span, z * narrow : (z + 1) * narrow] = together
    attn = dot(o_out[...], jnp.concatenate([wo[z] for z in range(parts)], 0), NN)
    x1_out[...] = x0[...] + attn + vecs[4:5]


def hidden_step(p, meta, h2, dy, inb, refs):
    narrow = refs[0].shape[1] // 2
    step = pl.program_id(0)
    swap = (meta[2] ^ p) == 1
    w_in = whole_block(refs, slice(0, narrow), swap)
    w_back = whole_block(refs, slice(narrow, 2 * narrow), swap)
    biases = []
    for s in range(2):
        z, k = column_of(meta, p, 2 * step + s)
        biases.append(inb[2 * z + k])
    hidden = dot(h2, w_in, NN) + jnp.concatenate(biases, 1)
    gate = 0.5 + 0.5 * lax.erf(hidden * (0.5**0.5))
    active = (hidden * gate).astype(BF16)
    slope = gate + hidden * jnp.exp(-0.5 * hidden * hidden) * 0.3989422804014327
    low = (dot(dy, w_back, NN) * slope).astype(BF16)
    return active, low, dot(active, w_back, NT), dot(low, w_in, NT)


def store_bias(dinb, low):
    total = colsum(low.astype(F32))
    width = dinb.shape[2]
    for s in range(2):
        dinb[s] = total[:, s * width : (s + 1) * width]


def hidden_a_kernel(meta, *refs):
    x1, y_refs, (vecs, inb), arrays = refs[0], refs[1:4], refs[4:6], refs[6:10]
    sent, dinb, h2s, dys, y_total, dh_total = refs[10:]
    parts, narrow = 4, y_refs[0].shape[1] // 2

    @pl.when(pl.program_id(0) == 0)
    def _():
        for d, part in enumerate(turned(meta[2], *y_refs)):
            dys[:, d * narrow : (d + 1) * narrow] = part[:, narrow:]
        xhat, _ = norm_parts(x1[...])
        h2s[...] = (xhat * vecs[2:3] + vecs[3:4]).astype(BF16)
        y_total[...] = jnp.zeros_like(y_total)
        dh_total[...] = jnp.zeros_like(dh_total)

    h2, dy = h2s[...], dys[...]
    active, low, y_part, dh_part = hidden_step(1, meta, h2, dy, inb, arrays)
    y_total[...] += y_part
    dh_total[...] += dh_part
    store_bias(dinb, low)
    d_in = dot(h2, low, TN).astype(BF16)
    d_back = dot(dy, active, TN).astype(BF16)
    for d in range(parts):
        q = place(d, 1 - meta[2])
        width = sent.shape[3]
        for s in range(2):
            part = (slice(d * narrow, (d + 1) * narrow), slice(s * width, (s + 1) * width))
            sent[q, s, :narrow] = d_in[part]
            sent[q, s, narrow:] = d_back[part]


def hidden_b_kernel(meta, x1, h2s, dys, y_first, dh_first, vecs, inb, *refs):
    arrays = refs[:4]
    (act, dus, dinb), turn, (dx1, da, vec_grads, y_total, dh_total) = refs[4:7], refs[7:10], refs[10:]
    step = pl.program_id(0)

    @pl.when(step == 0)
    def _():
        y_total[...] = y_first[...]
        dh_total[...] = dh_first[...]

    active, low, y_part, dh_part = hidden_step(0, meta, h2s[...], dys[...], inb, arrays)
    act[...] = active
    dus[...] = low
    y_total[...] += y_part
    dh_total[...] += dh_part
    store_bias(dinb, low)

    @pl.when(step == pl.num_programs(0) - 1)
    def _():
        values = x1[...]
        store_halves(meta[2], *turn, values + y_total[...] + vecs[5:6])
        xhat, factor = norm_parts(values)
        grad = dh_total[...]
        dy_wide = dys[...].astype(F32)
        total = dy_wide + norm_back(grad, xhat, factor, vecs[2:3])
        dx1[...] = total
        narrowed = total.astype(BF16)
        da[...] = narrowed
        vec_grads[0:1] = colsum(grad * xhat)
        vec_grads[1:2] = colsum(grad)
        vec_grads[2:3] = colsum(narrowed.astype(F32))
        vec_grads[3:4] = colsum(dy_wide)
        vec_grads[4:8] = jnp.zeros_like(vec_grads[4:8])


def hidden_grad_kernel(meta, h2s, dys, act, dus, arrived, kept, sent, d_in, d_back):
    narrow, width = kept.shape[2] // 2, kept.shape[3]
    d_in[...] = dot(h2s[...], dus[...], TN)
    d_back[...] = dot(dys[...], act[...], TN)
    for q in range(4):
        start = place(q, meta[2]) * narrow
        span = pl.ds(pl.multiple_of(start, narrow) if q in (1, 2) else start, narrow)
        into = kept if q < 2 else sent
        for s in range(2):
            columns = slice(s * width, (s + 1) * width)
            top = d_in[span, columns] + arrived[q, s, :narrow].astype(F32)
            low = d_back[span, columns] + arrived[q, s, narrow:].astype(F32)
            into[q % 2, s, :narrow] = top.astype(BF16)
            into[q % 2, s, narrow:] = low.astype(BF16)


def attend_back_kernel(images, rows, meta, da, o_ref, qkv, p_ref, wo, h1, *refs):
    dqkv, halves, dwo, dshift, sent, do_ref, dw_ref = refs
    parts, narrow = wo.shape[0], wo.shape[1]
    heads = narrow // HEAD_DIM
    factor = HEAD_DIM ** (-0.5)
    grad = da[...]
    outer = narrow // 2
    for z in range(parts):
        do_ref[z] = dot(grad, wo[z], NT).astype(BF16)
    each = [(z, i) for z in range(parts) for i in range(heads)]
    for b in range(images):
        span = slice(b * rows, (b + 1) * rows)
        grad_heads, grad_scores, grads = [], [], []
        for z, i in each:
            grad_head = do_ref[z, span, i * HEAD_DIM : (i + 1) * HEAD_DIM]
            grad_heads.append(grad_head)
            grad_scores.append(dot(head_part(qkv, z, span, i, 2), grad_head, NT))
        for n in range(len(each)):
            chance = p_ref[n, b].astype(F32)
            inner = jnp.sum(chance * grad_scores[n], 0, keepdims=True)
            grad_scores[n] = (chance * (grad_scores[n] - inner)).astype(BF16)
        for n, (z, i) in enumerate(each):
            query, key = (head_part(qkv, z, span, i, part) for part in (0, 1))
            grads.append((dot(grad_scores[n], key, TN) * factor).astype(BF16))
            grads.append((dot(grad_scores[n], query, NN) * factor).astype(BF16))
            grads.append(dot(p_ref[n, b], grad_heads[n], NN).astype(BF16))
        for z in range(parts):
            together = grads[3 * z * heads : 3 * (z + 1) * heads]
            dqkv[z, span, :] = jnp.concatenate(together, 1)
    half = dqkv.shape[2] // 2
    for z in range(parts):
        dshift[z] = colsum(dqkv[z].astype(F32))
        for k in range(2):
            halves[z, k] = dqkv[z, :, k * half : (k + 1) * half]
        dw = dot(o_ref[:, z * narrow : (z + 1) * narrow], grad, TN)
        for d in range(parts):
            for k in range(2):
                at = d * narrow + k * outer
                dwo[z, d, k] = dw[:, at : at + outer]

    def store(q, s, block):
        sent[q, s] = block.astype(BF16)

    first_grad(1, meta, h1, halves, dwo, dw_ref, store)


def first_back_kernel(
    meta, x0, dqkv, wq, dx1, vecs, vec_grads, dshift, dinb_a, dinb_b, *refs
):
    turn, (sent, kept, rows_out) = refs[:3], refs[3:]
    me = meta[0]
    parts, narrow = dqkv.shape[0], dqkv.shape[2] // 3
    width = dinb_a.shape[2]
    grad = dot(dqkv[0], wq[0], NT)
    for z in range(1, parts):
        grad += dot(dqkv[z], wq[z], NT)
    xhat, factor = norm_parts(x0[...])
    store_halves(meta[2], *turn, dx1[...] + norm_back(grad, xhat, factor, vecs[0:1]))
    rows_out[0:1] = colsum(grad * xhat)
    rows_out[1:2] = colsum(grad)
    rows_out[2:6] = vec_grads[0:4]
    gap = jnp.zeros((6, width - narrow), F32)
    tail = jnp.zeros((VEC_ROWS - 9, width), F32)
    for d in range(parts):
        six = jnp.concatenate([rows_out[0:6, d * narrow : (d + 1) * narrow], gap], 1)
        shift = dshift[me ^ d]
        second = jnp.concatenate([shift[:, width:], gap[0:1, : 2 * width - shift.shape[1]]], 1)
        for s in range(4):
            for p, dinb, out in ((1, dinb_a, sent), (0, dinb_b, kept)):
                lines = [six, shift[:, :width], second, dinb[s], tail]
                out[place(d, meta[2] ^ p), s] = jnp.concatenate(lines, 0).astype(BF16)


def first_grad(p, meta, h1, halves, dwo, dw, store):
    me = meta[0]
    narrow = dwo.shape[3]
    feature = h1[...]
    for s in range(4):
        z, k = column_of(meta, p, s)
        dw[...] = dot(feature, halves[z, k], TN)
        for q in range(4):
            d = place(q, meta[2] ^ p)
            start = d * narrow
            span = pl.ds(pl.multiple_of(start, narrow) if q in (1, 2) else start, narrow)
            store(q, s, jnp.concatenate([dw[span, :], dwo[me ^ d, z ^ me, k]], 1))


def first_kept_kernel(meta, h1, halves, dwo, below, arrived, arrived_below, kept, sent, dw):
    narrow = dwo.shape[3]

    def store(q, s, block):
        into = kept if q < 2 else sent
        into[q % 2, s, :narrow] = (block + arrived[q, s].astype(F32)).astype(BF16)
        into[q % 2, s, narrow:] = add(below[q, s], arrived_below[q, s])

    first_grad(0, meta, h1, halves, dwo, dw, store)


def finish_kernel(*refs):
    pieces, (qkv, out, hidden_bias, query, value), vectors = refs[:4], refs[4:9], refs[9:]
    narrow, half = qkv.shape
    total = pieces[0][...].astype(F32)
    for piece in pieces[1:]:
        total += piece[...].astype(F32)
    qkv[...] = total[:narrow, :half]
    out[...] = total[:narrow, half:]
    for i, ref in enumerate(vectors):
        ref[...] = total[narrow + i : narrow + i + 1, :narrow].reshape(ref.shape)
    shift = jnp.concatenate([total[narrow + 6 : narrow + 7], total[narrow + 7 : narrow + 8]], 1)
    heads = range(narrow // HEAD_DIM)
    for ref, part in ((query, 0), (value, 2)):
        pieces = [shift[:, (3 * i + part) * HEAD_DIM :][:, :HEAD_DIM] for i in heads]
        ref[...] = jnp.concatenate(pieces, 1).reshape(ref.shape)
    hidden_bias[...] = total[narrow + 8 : narrow + 9].reshape(hidden_bias.shape)


def call(kernel, outs, operands, scratch=(), name=None):
    specs = []
    for value in operands:
        specs.append(SMEM if value.dtype == jnp.int32 and value.ndim == 1 else VMEM)
    return pl.pallas_call(
        kernel,
        out_shape=outs,
        in_specs=specs,
        out_specs=jax.tree.map(lambda _: VMEM, outs),
        scratch_shapes=scratch,
        compiler_params=PARAMS,
        name=name,
    )(*operands)


def shaped(dtype, *shape):
    return jax.ShapeDtypeStruct(shape, dtype)


def exchange(block, d):
    size = lax.axis_size("ea")
    return block if d == 0 else lax.ppermute(block, "ea", [(e, e ^ d) for e in range(size)])


class Wires:
    def __init__(self, parts, columns):
        self.parts, self.chips = parts, columns // 2

    def over_z(self, blocks, back=False):
        pulled = [blocks[0]]
        for s in range(1, 4):
            pairs = []
            for h in range(2 * self.chips):
                far = (h + 2 * s) % (2 * self.chips)
                pairs.append((h, far) if back else (far, h))
            pulled.append(lax.ppermute(blocks[s], "ha", pairs))
        return pulled

    def turn(self, pair):
        if 2 * self.chips == BLOCKS:
            return self.stage(pair, 0)
        one = exchange(pair[0], 1)
        return jnp.stack([one, exchange(pair[1], 1)])

    def turn_again(self, *pairs):
        both = jnp.stack([block for single, first in pairs for block in (single, first[1])])
        return self.stage(both, 1) if 2 * self.chips == BLOCKS else exchange(both, 2)

    def swap(self, block):
        return lax.ppermute(block, "ha", [(h, h ^ 1) for h in range(2 * self.chips)])

    def stage(self, block, second):
        pairs = []
        columns = 2 * self.chips
        for e in range(self.parts):
            for h in range(columns):
                d = 1 + ((h % 2) ^ second)
                pairs.append((e * columns + h, (e ^ d) * columns + h))
        return lax.ppermute(block, ("ea", "ha"), pairs)

    def spread(self, mine, behind=(), swap_behind=()):
        one = self.stage(mine, 0)
        two = self.stage(mine, 1)
        mine, one, two = after((mine, one, two), *behind)
        three = self.stage(one, 1)
        mine, one, two = after((mine, one, two), *swap_behind)
        own = (mine, one, two, three)
        return own, tuple(self.swap(block) for block in own)

    def finish(self, once, arrived):
        total = add(once, arrived)
        return self.over_z([total[s] for s in range(4)], back=True)


def after(value, *others):
    return lax.optimization_barrier((value, others))[0]


def add(a, b):
    return (a.astype(F32) + b.astype(F32)).astype(BF16)


def vector_rows(vectors, shift, bias):
    width = bias.shape[-1]
    rows = [jnp.pad(v, (0, width - v.shape[0])) for v in vectors]
    rows += [shift[:width], jnp.pad(shift[width:], (0, 2 * width - shift.shape[0])), bias]
    return jnp.stack(rows + [jnp.zeros_like(bias)] * (VEC_ROWS - len(rows)))


def grid_call(kernel, outs, out_specs, operands, in_specs, scratch, name):
    return pl.pallas_call(
        kernel,
        out_shape=outs,
        grid_spec=pltpu.PrefetchScalarGridSpec(
            num_scalar_prefetch=1,
            grid=(2,),
            in_specs=in_specs,
            out_specs=out_specs,
            scratch_shapes=scratch,
        ),
        compiler_params=PARAMS,
        name=name,
    )(*operands)


def whole_spec(*shape):
    return pl.BlockSpec(shape, lambda s, meta: (0,) * len(shape))


def shards(
    tokens,
    image_counts,
    kept_patches,
    norm1_gain,
    norm1_bias,
    qkv_weight,
    query_bias,
    value_bias,
    out_weight,
    out_bias,
    norm2_gain,
    norm2_bias,
    in_weight,
    in_bias,
    back_weight,
    back_bias,
    cotangent,
):
    parts = lax.axis_size("ea")
    columns = lax.axis_size("ha")
    me = lax.axis_index("ea")
    mine = lax.axis_index("ha")
    direct = columns == BLOCKS
    wires = Wires(parts, columns)
    if direct:
        meta = jnp.stack([me, mine // 2, mine % 2]).astype(jnp.int32)
    else:
        meta = jnp.stack([me, 0 * mine, 0 * mine]).astype(jnp.int32)
    narrow, slots = tokens.shape
    full = narrow * parts
    images = image_counts.shape[0] // parts
    most = kept_patches.shape[1]
    rows = -(-most // 16) * 16
    count = images * rows
    window = min(slots, (images * most + 127 + 127) // 128 * 128)
    heads = full // HEAD_DIM
    group_heads = narrow // HEAD_DIM
    width = in_weight.shape[1] * columns // BLOCKS
    half = 3 * narrow // 2

    vectors = (norm1_gain, norm1_bias, norm2_gain, norm2_bias, out_bias, back_bias)
    if direct:
        first, second = call(
            shard_kernel,
            (shaped(BF16, narrow + VEC_ROWS, width), shaped(BF16, 2 * narrow, width)),
            (qkv_weight, out_weight, in_weight, back_weight.T, in_bias, query_bias, value_bias)
            + vectors,
            name="shard",
        )

    turn_shapes = lambda r, c: (shaped(BF16, r, c), shaped(BF16, 2, r, c), shaped(BF16, r, c))
    packed = call(
        partial(pack_kernel, images, rows, window),
        turn_shapes(count, 2 * narrow),
        (meta, image_counts, tokens, cotangent),
        (pltpu.SMEM((image_counts.shape[0],), jnp.int32), pltpu.VMEM((count, window), BF16)),
        "pack",
    )

    if direct:
        turned_once = wires.turn(packed[1])
        z_first = wires.over_z([first] * 4)
        turned_once = after(turned_once, *z_first[1:])
        xs = (packed[0], turned_once, wires.turn_again((packed[2], turned_once)))
        z_second = wires.over_z([after(second, *z_first)] * 4)
        g1 = wires.spread(jnp.stack(z_first), (), (*z_second, xs[2]))
        z_second = jnp.stack(after(z_second, g1[0][1]))
        xs = after(xs, z_second)
    else:
        turned_once = wires.turn(packed[1])
        xs = (packed[0], turned_once, wires.turn_again((packed[2], turned_once)))
        pairs = jnp.zeros((group_heads, HEAD_DIM), BF16)
        by_head = lambda bias: bias.reshape(group_heads, HEAD_DIM)
        shift = jnp.stack([by_head(query_bias), pairs, by_head(value_bias)], 1).reshape(-1)

        def whole(weight):
            wide = lax.all_gather(weight, "ha", axis=1, tiled=True)
            blocks = wide.reshape(narrow, BLOCKS, -1).transpose(1, 0, 2)
            return lax.all_gather(blocks, "ea")

        def arrange(blocks):
            sides = []
            for p in range(2):
                side = []
                for a in range(parts):
                    d = a if p == 0 or a in (0, 3) else 3 - a
                    row = lax.dynamic_index_in_dim(blocks, me ^ d, 0, False)
                    side.append(jnp.stack([row[2 * s + p] for s in range(4)]))
                sides.append(tuple(side))
            return sides

        biases = lax.all_gather(in_bias, "ha", tiled=True).reshape(BLOCKS, -1)
        below = jax.vmap(lambda bias: vector_rows(vectors, shift, bias))(biases)
        g1 = jnp.concatenate([whole(qkv_weight), whole(out_weight)], 3)
        g1 = jnp.concatenate([g1, lax.all_gather(below, "ea")], 2)
        g1 = arrange(g1)
        g2 = arrange(jnp.concatenate([whole(in_weight), whole(back_weight.T)], 2))

    omega = 1.0 / 10000.0 ** (jnp.arange(narrow, dtype=F32) / narrow)
    angles = jnp.arange(16, dtype=F32)[:, None] * omega[None, :]
    patches = jnp.pad(kept_patches, ((0, 0), (0, 128 - most)))

    x1, x0, h1, qkv, chances, mixed, vecs, inb, wq, wo = call(
        partial(attend_kernel, images, rows),
        (
            shaped(F32, count, full),
            shaped(F32, count, full),
            shaped(BF16, count, full),
            shaped(BF16, parts, count, 3 * narrow),
            shaped(BF16, heads, images, rows, rows),
            shaped(BF16, count, full),
            shaped(F32, VEC_ROWS, full),
            shaped(F32, BLOCKS, 1, width),
            shaped(BF16, parts, full, 3 * narrow),
            shaped(BF16, parts, narrow, full),
        ),
        (meta, image_counts, *xs, patches, jnp.sin(angles), jnp.cos(angles), *g1[0], *g1[1]),
        (
            pltpu.VMEM((parts, 1, 3 * narrow), F32),
            pltpu.VMEM((parts, parts, narrow, narrow), BF16),
        ),
        "attend",
    )

    if direct:
        g2 = wires.spread(z_second, (x1,))
    block_spec = pl.BlockSpec((2, 2 * narrow, width), lambda s, meta: (s, 0, 0))
    slot_spec = pl.BlockSpec((4, 2, 2 * narrow, width), lambda s, meta: (0, s, 0, 0))
    pair_spec = pl.BlockSpec((2, 2, 2 * narrow, width), lambda s, meta: (0, s, 0, 0))
    bias_spec = pl.BlockSpec((2, 1, width), lambda s, meta: (s, 0, 0))
    column_spec = pl.BlockSpec((count, 2 * width), lambda s, meta: (0, s))
    inb_spec = whole_spec(BLOCKS, 1, width)
    wide_spec = whole_spec(count, full)
    sent2, dinb_a, h2, dy, y_first, dh_first = grid_call(
        hidden_a_kernel,
        (
            shaped(BF16, 4, 4, 2 * narrow, width),
            shaped(F32, 4, 1, width),
            shaped(BF16, count, full),
            shaped(BF16, count, full),
            shaped(F32, count, full),
            shaped(F32, count, full),
        ),
        (slot_spec, bias_spec, wide_spec, wide_spec, wide_spec, wide_spec),
        (meta, x1, *xs, vecs, inb, *g2[1]),
        [wide_spec]
        + [whole_spec(count, 2 * narrow)]
        + [whole_spec(2, count, 2 * narrow)] * 2
        + [whole_spec(VEC_ROWS, full), inb_spec]
        + [block_spec] * 4,
        (),
        "hidden_a",
    )
    act, dus, dinb_b, *outs, dx1, da, vec_grads = grid_call(
        hidden_b_kernel,
        (
            shaped(BF16, count, 4 * width),
            shaped(BF16, count, 4 * width),
            shaped(F32, 4, 1, width),
            *turn_shapes(count // 2, 2 * narrow),
            shaped(F32, count, full),
            shaped(BF16, count, full),
            shaped(F32, 8, full),
        ),
        (
            column_spec,
            column_spec,
            bias_spec,
            whole_spec(count // 2, 2 * narrow),
            whole_spec(2, count // 2, 2 * narrow),
            whole_spec(count // 2, 2 * narrow),
            wide_spec,
            wide_spec,
            whole_spec(8, full),
        ),
        (meta, x1, h2, dy, y_first, dh_first, vecs, inb, *g2[0]),
        [wide_spec] * 5 + [whole_spec(VEC_ROWS, full), inb_spec] + [block_spec] * 4,
        (pltpu.VMEM((count, full), F32), pltpu.VMEM((count, full), F32)),
        "hidden_b",
    )
    outs[1] = wires.turn(outs[1])
    arrived2 = wires.swap(sent2) if direct else jnp.zeros_like(sent2)
    kept2, passed2 = grid_call(
        hidden_grad_kernel,
        (shaped(BF16, 2, 4, 2 * narrow, width),) * 2,
        (pair_spec, pair_spec),
        (meta, h2, dy, act, dus, arrived2),
        [wide_spec, wide_spec, column_spec, column_spec, slot_spec],
        (pltpu.VMEM((full, 2 * width), F32), pltpu.VMEM((full, 2 * width), F32)),
        "hidden_grad",
    )

    passed2 = after(passed2, outs[1])
    dqkv, halves, dwo, dshift, sent1 = call(
        partial(attend_back_kernel, images, rows),
        (
            shaped(BF16, parts, count, 3 * narrow),
            shaped(BF16, parts, 2, count, half),
            shaped(F32, parts, parts, 2, narrow, narrow // 2),
            shaped(F32, parts, 1, 3 * narrow),
            shaped(BF16, 4, 4, narrow, width),
        ),
        (meta, after(da, kept2), mixed, qkv, chances, wo, h1),
        (pltpu.VMEM((parts, count, narrow), BF16), pltpu.VMEM((full, half), F32)),
        "attend_back",
    )
    *gx, sent_below, kept_below = call(
        first_back_kernel,
        turn_shapes(count // 2, 2 * narrow)
        + (shaped(BF16, 4, 4, VEC_ROWS, width),) * 2,
        (meta, x0, dqkv, wq, dx1, vecs, vec_grads, dshift, dinb_a, dinb_b),
        (pltpu.VMEM((8, full), F32),),
        name="first_back",
    )
    if direct:
        arrived1 = wires.swap(sent1)
        arrived_below = wires.swap(sent_below)
        arrived = after(wires.stage(passed2, 1), gx[0])
        once2, next2 = add(kept2[0], arrived[0]), add(kept2[1], arrived[1])
        h1 = after(h1, next2)
        next2 = wires.stage(next2, 0)
    else:
        arrived1, arrived_below = jnp.zeros_like(sent1), jnp.zeros_like(sent_below)
    kept1, passed1 = call(
        first_kept_kernel,
        (shaped(BF16, 2, 4, narrow + VEC_ROWS, width),) * 2,
        (meta, h1, halves, dwo, kept_below, arrived1, arrived_below),
        (pltpu.VMEM((full, half), F32),),
        "first_kept",
    )
    gx[1] = wires.turn(after(gx[1], kept1))
    if direct:
        arrived = wires.stage(passed1, 1)
        z_second = wires.finish(once2, after(next2, kept1))
        arrived = after(arrived, z_second[1])
        once1, next1 = add(kept1[0], arrived[0]), add(kept1[1], arrived[1])
        z_first = wires.finish(once1, wires.stage(next1, 0))
        gx[1] = after(gx[1], *z_second)
    second = wires.turn_again((outs[2], outs[1]), (gx[2], gx[1]))

    output, grad_tokens = call(
        partial(unpack_kernel, images, rows, window),
        (shaped(BF16, narrow, slots), shaped(F32, narrow, slots)),
        (meta, image_counts, *outs[:2], *gx[:2], second),
        (
            pltpu.SMEM((image_counts.shape[0],), jnp.int32),
            pltpu.VMEM((count, window), BF16),
            pltpu.VMEM((narrow, slots), F32),
            pltpu.VMEM((narrow, slots), F32),
        ),
        "unpack",
    )

    if direct:
        s2 = sum(piece.astype(F32) for piece in z_second)
        grad_in, grad_back = s2[:narrow], s2[narrow:]
        line = shaped(F32, narrow)
        grad_qkv, grad_out, grad_in_bias, grad_query, grad_value, *small = call(
            finish_kernel,
            (shaped(F32, narrow, half), shaped(F32, narrow, narrow // 2), shaped(F32, width))
            + (line,) * 8,
            z_first,
            name="finish",
        )
    else:

        def spread(sent, kept, passed):
            later = jnp.concatenate([kept, passed], 0)
            tall = []
            for e in range(parts):
                d = me ^ e
                row = [None] * BLOCKS
                for p, side in ((1, sent), (0, later)):
                    q = jnp.where((d == 0) | (d == 3) | (p == 0), d, 3 - d)
                    four = lax.dynamic_index_in_dim(side, q, 0, False)
                    for s in range(4):
                        row[2 * s + p] = four[s]
                tall.append(jnp.stack(row))
            return jnp.stack(tall).astype(F32)

        def scatter(blocks):
            flat = lax.psum_scatter(blocks, "ea").transpose(1, 0, 2).reshape(narrow, -1)
            return lax.psum_scatter(flat, "ha", scatter_dimension=1, tiled=True)

        sent1 = jnp.concatenate([sent1, sent_below], 2)
        d2, d1 = spread(sent2, kept2, passed2), spread(sent1, kept1, passed1)
        grad_in, grad_back = scatter(d2[:, :, :narrow]), scatter(d2[:, :, narrow:])
        grad_qkv, grad_out = scatter(d1[:, :, :narrow, :half]), scatter(d1[:, :, :narrow, half:])
        small = lax.psum(d1[:, :, narrow:], ("ea", "ha"))
        size = in_bias.shape[0]
        grad_in_bias = lax.dynamic_slice_in_dim(small[0, :, 8].reshape(-1), mine * size, size, 0)
        small = lax.dynamic_index_in_dim(small[:, 0], me, 0, False)
        shift = jnp.concatenate([small[6], small[7]])[: 3 * narrow]
        shift = shift.reshape(group_heads, 3, HEAD_DIM)
        grad_query, grad_value = shift[:, 0].reshape(-1), shift[:, 2].reshape(-1)
        small = small[:, :narrow]
    return (
        output,
        grad_tokens,
        small[0],
        small[1],
        grad_qkv,
        grad_query,
        grad_value,
        grad_out,
        small[4],
        small[2],
        small[3],
        grad_in,
        grad_in_bias,
        grad_back.T,
        small[5],
    )


def solution(mesh):
    return jax.shard_map(
        shards,
        mesh=mesh,
        in_specs=(
            P("ea", "ha"),
            P("ha"),
            P("ha", None),
            P("ea"),
            P("ea"),
            P("ea", "ha"),
            P("ea"),
            P("ea"),
            P("ea", "ha"),
            P("ea"),
            P("ea"),
            P("ea"),
            P("ea", "ha"),
            P("ha"),
            P("ha", "ea"),
            P("ea"),
            P("ea", "ha"),
        ),
        out_specs=(
            P("ea", "ha"),
            P("ea", "ha"),
            P("ea"),
            P("ea"),
            P("ea", "ha"),
            P("ea"),
            P("ea"),
            P("ea", "ha"),
            P("ea"),
            P("ea"),
            P("ea"),
            P("ea", "ha"),
            P("ha"),
            P("ha", "ea"),
            P("ea"),
        ),
        check_vma=False,
    )
```

```python
from functools import partial

import jax
import jax.numpy as jnp
from jax import lax
from jax.experimental import pallas as pl
from jax.experimental.pallas import tpu as pltpu
from jax.sharding import PartitionSpec as P

HEAD_DIM = 64
GRID = 14
EPSILON = 1e-06
NEGATIVE = -1e30
BLOCKS = 8
VEC_ROWS = 16
NN = (((1,), (0,)), ((), ()))
NT = (((1,), (1,)), ((), ()))
TN = (((0,), (0,)), ((), ()))
F32 = jnp.float32
BF16 = jnp.bfloat16
SMEM = pl.BlockSpec(memory_space=pltpu.SMEM)
VMEM = pl.BlockSpec(memory_space=pltpu.VMEM)
PARAMS = pltpu.CompilerParams(vmem_limit_bytes=56 * 1024 * 1024)


def dot(a, b, dims):
    return lax.dot_general(a, b, dims, preferred_element_type=F32)


def iota(shape, axis):
    return lax.broadcasted_iota(jnp.int32, shape, axis)


def prefix(counts, starts):
    total = jnp.int32(0)
    for i in range(counts.shape[0]):
        starts[i] = total
        total = total + counts[i]


def select_rows(sel, counts, starts, part, images, rows, window, slots):
    first = starts[part * images]
    base = jnp.minimum(first // 128, (slots - window) // 128) * 128
    base = pl.multiple_of(base, 128)
    row = iota((rows, window), 0)
    gap = iota((rows, window), 1) - row
    for i in range(images):
        image = part * images + i
        hit = (gap == starts[image] - base) & (row < counts[image])
        sel[i * rows : (i + 1) * rows, :] = jnp.where(hit, 1.0, 0.0).astype(BF16)
    return base


def pack_kernel(images, rows, window, meta, counts, tokens, cotangent, *refs):
    (mine, pair, single), (starts, sel) = refs[:3], refs[3:]
    prefix(counts, starts)
    for a in range(4):
        part = meta[0] ^ place(a, meta[2])
        base = select_rows(sel, counts, starts, part, images, rows, window, tokens.shape[1])
        span = pl.ds(base, window)
        both = jnp.concatenate([tokens[:, span], cotangent[:, span]], 0)
        block = dot(sel[...], both, NT).astype(BF16)
        if a in (0, 2):
            (single if a else mine)[...] = block
        else:
            pair[a // 2] = block


def shard_kernel(qkv, out, into, back, hidden_bias, query, value, *refs):
    vectors, (first, second) = refs[:-2], refs[-2:]
    narrow, half = qkv.shape
    width = first.shape[1]
    first[:narrow, :half] = qkv[...]
    first[:narrow, half:] = out[...]
    empty = jnp.zeros((1, width), F32)
    wide = lambda ref: ref[...].astype(F32).reshape(1, -1)
    rows = [jnp.concatenate([wide(ref), empty[:, narrow:]], 1) for ref in vectors]
    query, value = wide(query), wide(value)
    shift = []
    for i in range(narrow // HEAD_DIM):
        at = slice(i * HEAD_DIM, (i + 1) * HEAD_DIM)
        shift += [query[:, at], empty[:, :HEAD_DIM], value[:, at]]
    shift = jnp.concatenate(shift + [empty[:, : 2 * width - 2 * half]], 1)
    rows += [shift[:, :width], shift[:, width:], wide(hidden_bias)]
    rows.append(jnp.zeros((VEC_ROWS - len(rows), width), F32))
    first[narrow:, :] = jnp.concatenate(rows, 0).astype(BF16)
    second[:narrow, :] = into[...]
    second[narrow:, :] = back[...]


def unpack_kernel(images, rows, window, meta, counts, *refs):
    outs, grads, second = refs[:2], refs[2:4], refs[4]
    output, grad, starts, sel, total, grad_total = refs[5:]
    narrow, slots = output.shape
    prefix(counts, starts)
    total[...] = jnp.zeros_like(total)
    grad_total[...] = jnp.zeros_like(grad_total)
    for a in range(4):
        part = meta[0] ^ place(a, meta[2])
        base = select_rows(sel, counts, starts, part, images, rows, window, slots)
        span = pl.ds(base, window)
        for i, (refs, into) in enumerate(((outs, total), (grads, grad_total))):
            pair = refs[0][...] if a == 0 else refs[1][0] if a == 1 else second[2 * i + a - 2]
            tall = jnp.concatenate([pair[:, :narrow], pair[:, narrow:]], 0)
            into[:, span] += dot(tall, sel[...], TN)
    output[...] = total[...].astype(output.dtype)
    grad[...] = grad_total[...]


def store_halves(core, mine, pair, single, values):
    low, narrow = mine.shape[0], mine.shape[1] // 2
    parts = []
    for d in range(4):
        span = slice(d * narrow, (d + 1) * narrow)
        both = [values[:low, span], values[low:, span]]
        parts.append(jnp.concatenate(both, 1).astype(mine.dtype))
    mine[...] = parts[0]
    pair[0] = jnp.where(core == 0, parts[1], parts[2])
    single[...] = jnp.where(core == 0, parts[2], parts[1])
    pair[1] = parts[3]


def turned(core, mine, first, second):
    one, two = first[0], second[0]
    swap = core == 1
    return [mine[...], jnp.where(swap, two, one), jnp.where(swap, one, two), second[1]]


def norm_parts(values):
    center = jnp.mean(values, 1, keepdims=True)
    centred = values - center
    factor = lax.rsqrt(jnp.mean(centred * centred, 1, keepdims=True) + EPSILON)
    return centred * factor, factor


def norm_back(grad, xhat, factor, gain):
    scaled = grad * gain
    mean = jnp.mean(scaled, 1, keepdims=True)
    across = jnp.mean(scaled * xhat, 1, keepdims=True)
    return factor * (scaled - mean - xhat * across)


def colsum(values):
    return jnp.sum(values, 0, keepdims=True)


def place(d, core):
    return d if d in (0, 3) else jnp.where(core == 0, d, 3 - d)


def column_of(meta, p, s):
    return (meta[1] + s) % 4, meta[2] ^ p


def whole_block(refs, rows, swap):
    columns = []
    for s in range(refs[0].shape[0]):
        one, two = refs[1][s, rows], refs[2][s, rows]
        one, two = jnp.where(swap, two, one), jnp.where(swap, one, two)
        columns.append(jnp.concatenate([refs[0][s, rows], one, two, refs[3][s, rows]], 0))
    return jnp.concatenate(columns, 1)


def head_part(qkv, z, span, head, part):
    at = (3 * head + part) * HEAD_DIM
    return qkv[z, span, at : at + HEAD_DIM]


def attend_kernel(images, rows, meta, counts, *refs):
    x_refs, (patches, sines, cosines), arrays = refs[:3], refs[3:6], (refs[6:10], refs[10:14])
    x1_out, x0, h1_out, qkv_out, p_out, o_out, vecs, inb, wq, wo = refs[14:24]
    shifts, wo_parts = refs[24:]
    me = meta[0]
    parts, narrow = wo.shape[0], wo.shape[1]
    wide = 3 * narrow
    half = wide // 2
    outer = narrow // 2
    heads = narrow // HEAD_DIM

    def unfold(core):
        for p in range(2):
            for a in range(parts):
                d = a if a in (0, 3) or (core ^ p) == 0 else 3 - a
                low, high = d * narrow, (d + 1) * narrow
                for s in range(4):
                    z = (meta[1] + s) % 4
                    k = core ^ p
                    ref = arrays[p][a]
                    wq[z, low:high, k * half : (k + 1) * half] = ref[s, :narrow, :half]
                    wo_parts[me ^ d, z, :, k * outer : (k + 1) * outer] = ref[s, :narrow, half:]
                    if a == 0:
                        inb[2 * z + k] = ref[s, narrow:, :].astype(F32)[8:9]
                if p == 0:
                    small = arrays[p][a][0, narrow:, :].astype(F32)
                    vecs[:, low:high] = small[:, :narrow]
                    rest = small[7:8, : wide - small.shape[1]]
                    shifts[me ^ d] = jnp.concatenate([small[6:7], rest], 1)

    pl.when(meta[2] == 0)(partial(unfold, 0))
    pl.when(meta[2] == 1)(partial(unfold, 1))
    for t in range(parts):
        for d in range(parts):
            wo[t, :, d * narrow : (d + 1) * narrow] = wo_parts[t, me ^ d]
    tokens = turned(meta[2], *x_refs)
    for d in range(parts):
        e = me ^ d
        table = jnp.where(e % 2 == 0, sines[...], cosines[...])
        high = table.astype(BF16)
        rest = table - high.astype(F32)
        middle = rest.astype(BF16)
        low = (rest - middle.astype(F32)).astype(BF16)
        stacked = jnp.concatenate([high, middle, low], 0)
        depth = table.shape[0]
        for i in range(images):
            patch = patches[pl.ds(me * images + i, 1), :rows]
            row = (patch * 4682) >> 16
            spot = jnp.where(e < 2, row, patch - row * GRID)
            hot = jnp.where(iota((depth, rows), 0) == spot, 1.0, 0.0).astype(BF16)
            placed = dot(jnp.concatenate([hot, hot, hot], 0), stacked, TN)
            x0[i * rows : (i + 1) * rows, d * narrow : (d + 1) * narrow] = (
                tokens[d][i * rows : (i + 1) * rows, :narrow].astype(F32) + placed
            )
    xhat, _ = norm_parts(x0[...])
    h1 = (xhat * vecs[0:1] + vecs[1:2]).astype(BF16)
    h1_out[...] = h1
    for z in range(parts):
        qkv_out[z] = (dot(h1, wq[z], NN) + shifts[z]).astype(BF16)
    factor = HEAD_DIM ** (-0.5)
    each = [(z, i) for z in range(parts) for i in range(heads)]
    for b in range(images):
        seen = iota((rows, rows), 0) < counts[me * images + b]
        span = slice(b * rows, (b + 1) * rows)
        scores, mixed = [], []
        for z, i in each:
            query, key = (head_part(qkv_out, z, span, i, part) for part in (0, 1))
            scores.append(jnp.where(seen, dot(key, query, NT) * factor, NEGATIVE))
        for n, score in enumerate(scores):
            weights = jnp.exp(score - jnp.max(score, 0, keepdims=True))
            scale = 1.0 / jnp.sum(weights, 0, keepdims=True)
            p_out[n, b] = (weights * scale).astype(BF16)
        for n, (z, i) in enumerate(each):
            value = head_part(qkv_out, z, span, i, 2)
            mixed.append(dot(p_out[n, b], value, TN).astype(BF16))
        for z in range(parts):
            together = jnp.concatenate(mixed[z * heads : (z + 1) * heads], 1)
            o_out[span, z * narrow : (z + 1) * narrow] = together
    attn = dot(o_out[...], jnp.concatenate([wo[z] for z in range(parts)], 0), NN)
    x1_out[...] = x0[...] + attn + vecs[4:5]


def hidden_step(p, meta, h2, dy, inb, refs, first):
    narrow = refs[0].shape[1] // 2
    swap = (meta[2] ^ p) == 1
    w_in = whole_block(refs, slice(0, narrow), swap)
    w_back = whole_block(refs, slice(narrow, 2 * narrow), swap)
    biases = []
    for s in range(refs[0].shape[0]):
        z, k = column_of(meta, p, first + s)
        biases.append(inb[2 * z + k])
    hidden = dot(h2, w_in, NN) + jnp.concatenate(biases, 1)
    gate = 0.5 + 0.5 * lax.erf(hidden * (0.5**0.5))
    active = (hidden * gate).astype(BF16)
    slope = gate + hidden * jnp.exp(-0.5 * hidden * hidden) * 0.3989422804014327
    low = (dot(dy, w_back, NN) * slope).astype(BF16)
    return active, low, dot(active, w_back, NT), dot(low, w_in, NT)


def store_bias(dinb, low):
    total = colsum(low.astype(F32))
    width = dinb.shape[-1]
    for s in range(dinb.shape[0]):
        dinb[s] = total[:, s * width : (s + 1) * width]


def store_blocks(out, core, h2, dy, active, low):
    narrow, width = out.shape[2] // 2, out.shape[3]
    d_in = dot(h2, low, TN).astype(BF16)
    d_back = dot(dy, active, TN).astype(BF16)
    for d in range(4):
        q = place(d, core)
        for s in range(out.shape[1]):
            part = (slice(d * narrow, (d + 1) * narrow), slice(s * width, (s + 1) * width))
            out[q, s, :narrow] = d_in[part]
            out[q, s, narrow:] = d_back[part]


def hidden_first_kernel(meta, *refs):
    x1, y_refs, (vecs, inb), own, other = refs[0], refs[1:4], refs[4:6], refs[6:10], refs[10:14]
    sent, kept, sent_dinb, kept_dinb, h2s, dys, y_total, dh_total = refs[14:]
    narrow = y_refs[0].shape[1] // 2
    for d, part in enumerate(turned(meta[2], *y_refs)):
        dys[:, d * narrow : (d + 1) * narrow] = part[:, narrow:]
    xhat, _ = norm_parts(x1[...])
    h2s[...] = (xhat * vecs[2:3] + vecs[3:4]).astype(BF16)
    h2, dy = h2s[...], dys[...]
    for p, arrays, out, dinb in ((1, other, sent, sent_dinb), (0, own, kept, kept_dinb)):
        active, low, y_part, dh_part = hidden_step(p, meta, h2, dy, inb, arrays, 0)
        y_total[...] = y_part if p else y_total[...] + y_part
        dh_total[...] = dh_part if p else dh_total[...] + dh_part
        store_bias(dinb, low)
        store_blocks(out, meta[2] ^ p, h2, dy, active, low)


def hidden_a_kernel(meta, h2s, dys, y_first, dh_first, inb, *refs):
    arrays = refs[:4]
    sent, dinb, y_total, dh_total = refs[4:]
    h2, dy = h2s[...], dys[...]
    active, low, y_part, dh_part = hidden_step(1, meta, h2, dy, inb, arrays, 2)
    y_total[...] = y_first[...] + y_part
    dh_total[...] = dh_first[...] + dh_part
    store_bias(dinb, low)
    store_blocks(sent, 1 - meta[2], h2, dy, active, low)


def hidden_b_kernel(meta, x1, h2s, dys, y_first, dh_first, vecs, inb, arrived, *refs):
    arrays, (kept, sent, dinb), turn = refs[:4], refs[4:7], refs[7:10]
    dx1, da, vec_grads, d_in, d_back = refs[10:]
    h2, dy = h2s[...], dys[...]
    active, low, y_part, dh_part = hidden_step(0, meta, h2, dy, inb, arrays, 2)
    store_bias(dinb, low)
    narrow, width = kept.shape[2] // 2, kept.shape[3]
    d_in[...] = dot(h2, low, TN)
    d_back[...] = dot(dy, active, TN)
    for q in range(4):
        start = place(q, meta[2]) * narrow
        span = pl.ds(pl.multiple_of(start, narrow) if q in (1, 2) else start, narrow)
        into = kept if q < 2 else sent
        for s in range(2):
            columns = slice(s * width, (s + 1) * width)
            part = d_in[span, columns] + arrived[q, s, :narrow].astype(F32)
            into[q % 2, s, :narrow] = part.astype(BF16)
            part = d_back[span, columns] + arrived[q, s, narrow:].astype(F32)
            into[q % 2, s, narrow:] = part.astype(BF16)
    values = x1[...]
    store_halves(meta[2], *turn, values + y_first[...] + y_part + vecs[5:6])
    xhat, factor = norm_parts(values)
    grad = dh_first[...] + dh_part
    dy_wide = dy.astype(F32)
    total = dy_wide + norm_back(grad, xhat, factor, vecs[2:3])
    dx1[...] = total
    narrowed = total.astype(BF16)
    da[...] = narrowed
    vec_grads[0:1] = colsum(grad * xhat)
    vec_grads[1:2] = colsum(grad)
    vec_grads[2:3] = colsum(narrowed.astype(F32))
    vec_grads[3:4] = colsum(dy_wide)
    vec_grads[4:8] = jnp.zeros_like(vec_grads[4:8])


def attend_back_kernel(images, rows, meta, da, o_ref, qkv, p_ref, wo, h1, *refs):
    dqkv, halves, dwo, dshift, sent, do_ref, dw_ref = refs
    parts, narrow = wo.shape[0], wo.shape[1]
    heads = narrow // HEAD_DIM
    factor = HEAD_DIM ** (-0.5)
    grad = da[...]
    outer = narrow // 2
    for z in range(parts):
        do_ref[z] = dot(grad, wo[z], NT).astype(BF16)
    each = [(z, i) for z in range(parts) for i in range(heads)]
    for b in range(images):
        span = slice(b * rows, (b + 1) * rows)
        grad_heads, grad_scores, grads = [], [], []
        for z, i in each:
            grad_head = do_ref[z, span, i * HEAD_DIM : (i + 1) * HEAD_DIM]
            grad_heads.append(grad_head)
            grad_scores.append(dot(head_part(qkv, z, span, i, 2), grad_head, NT))
        for n in range(len(each)):
            chance = p_ref[n, b].astype(F32)
            inner = jnp.sum(chance * grad_scores[n], 0, keepdims=True)
            grad_scores[n] = (chance * (grad_scores[n] - inner)).astype(BF16)
        for n, (z, i) in enumerate(each):
            query, key = (head_part(qkv, z, span, i, part) for part in (0, 1))
            grads.append((dot(grad_scores[n], key, TN) * factor).astype(BF16))
            grads.append((dot(grad_scores[n], query, NN) * factor).astype(BF16))
            grads.append(dot(p_ref[n, b], grad_heads[n], NN).astype(BF16))
        for z in range(parts):
            together = grads[3 * z * heads : 3 * (z + 1) * heads]
            dqkv[z, span, :] = jnp.concatenate(together, 1)
    half = dqkv.shape[2] // 2
    for z in range(parts):
        dshift[z] = colsum(dqkv[z].astype(F32))
        for k in range(2):
            halves[z, k] = dqkv[z, :, k * half : (k + 1) * half]
        dw = dot(o_ref[:, z * narrow : (z + 1) * narrow], grad, TN)
        for d in range(parts):
            for k in range(2):
                at = d * narrow + k * outer
                dwo[z, d, k] = dw[:, at : at + outer]

    def store(q, s, block):
        sent[q, s] = block.astype(BF16)

    first_grad(1, meta, h1, halves, dwo, dw_ref, store)


def first_back_kernel(
    meta, x0, dqkv, wq, dx1, vecs, vec_grads, dshift, sent_dinb, sent_rest, kept_dinb, kept_rest, *refs
):
    turn, (sent, kept, rows_out) = refs[:3], refs[3:]
    me = meta[0]
    parts, narrow = dqkv.shape[0], dqkv.shape[2] // 3
    width = sent.shape[3]
    grad = dot(dqkv[0], wq[0], NT)
    for z in range(1, parts):
        grad += dot(dqkv[z], wq[z], NT)
    xhat, factor = norm_parts(x0[...])
    store_halves(meta[2], *turn, dx1[...] + norm_back(grad, xhat, factor, vecs[0:1]))
    rows_out[0:1] = colsum(grad * xhat)
    rows_out[1:2] = colsum(grad)
    rows_out[2:6] = vec_grads[0:4]
    gap = jnp.zeros((6, width - narrow), F32)
    tail = jnp.zeros((VEC_ROWS - 9, width), F32)
    for d in range(parts):
        six = jnp.concatenate([rows_out[0:6, d * narrow : (d + 1) * narrow], gap], 1)
        shift = dshift[me ^ d]
        second = jnp.concatenate([shift[:, width:], gap[0:1, : 2 * width - shift.shape[1]]], 1)
        for s in range(4):
            for p, first, rest, out in (
                (1, sent_dinb, sent_rest, sent),
                (0, kept_dinb, kept_rest, kept),
            ):
                bias = first[s] if s < 2 else rest[s - 2]
                lines = [six, shift[:, :width], second, bias, tail]
                out[place(d, meta[2] ^ p), s] = jnp.concatenate(lines, 0).astype(BF16)


def first_grad(p, meta, h1, halves, dwo, dw, store):
    me = meta[0]
    narrow = dwo.shape[3]
    feature = h1[...]
    for s in range(4):
        z, k = column_of(meta, p, s)
        dw[...] = dot(feature, halves[z, k], TN)
        for q in range(4):
            d = place(q, meta[2] ^ p)
            start = d * narrow
            span = pl.ds(pl.multiple_of(start, narrow) if q in (1, 2) else start, narrow)
            store(q, s, jnp.concatenate([dw[span, :], dwo[me ^ d, z ^ me, k]], 1))


def first_kept_kernel(meta, h1, halves, dwo, below, arrived, arrived_below, kept, sent, dw):
    narrow = dwo.shape[3]

    def store(q, s, block):
        into = kept if q < 2 else sent
        into[q % 2, s, :narrow] = (block + arrived[q, s].astype(F32)).astype(BF16)
        into[q % 2, s, narrow:] = add(below[q, s], arrived_below[q, s])

    first_grad(0, meta, h1, halves, dwo, dw, store)


def finish_second_kernel(*refs):
    pieces, (d_in, d_back) = refs[:4], refs[4:]
    narrow = d_in.shape[0]
    for rows, out in ((slice(0, narrow), d_in), (slice(narrow, 2 * narrow), d_back)):
        total = pieces[0][rows].astype(F32)
        for piece in pieces[1:]:
            total += piece[rows].astype(F32)
        out[...] = total


def finish_kernel(*refs):
    pieces, (qkv, out, hidden_bias, query, value), vectors = refs[:4], refs[4:9], refs[9:]
    narrow, half = qkv.shape
    total = pieces[0][...].astype(F32)
    for piece in pieces[1:]:
        total += piece[...].astype(F32)
    qkv[...] = total[:narrow, :half]
    out[...] = total[:narrow, half:]
    for i, ref in enumerate(vectors):
        ref[...] = total[narrow + i : narrow + i + 1, :narrow].reshape(ref.shape)
    shift = jnp.concatenate([total[narrow + 6 : narrow + 7], total[narrow + 7 : narrow + 8]], 1)
    heads = range(narrow // HEAD_DIM)
    for ref, part in ((query, 0), (value, 2)):
        pieces = [shift[:, (3 * i + part) * HEAD_DIM :][:, :HEAD_DIM] for i in heads]
        ref[...] = jnp.concatenate(pieces, 1).reshape(ref.shape)
    hidden_bias[...] = total[narrow + 8 : narrow + 9].reshape(hidden_bias.shape)


def call(kernel, outs, operands, scratch=(), name=None):
    specs = []
    for value in operands:
        specs.append(SMEM if value.dtype == jnp.int32 and value.ndim == 1 else VMEM)
    return pl.pallas_call(
        kernel,
        out_shape=outs,
        in_specs=specs,
        out_specs=jax.tree.map(lambda _: VMEM, outs),
        scratch_shapes=scratch,
        compiler_params=PARAMS,
        name=name,
    )(*operands)


def shaped(dtype, *shape):
    return jax.ShapeDtypeStruct(shape, dtype)


def exchange(block, d):
    size = lax.axis_size("ea")
    return block if d == 0 else lax.ppermute(block, "ea", [(e, e ^ d) for e in range(size)])


class Wires:
    def __init__(self, parts, columns):
        self.parts, self.chips = parts, columns // 2

    def over_z(self, blocks, back=False, slots=(1, 2, 3)):
        pulled = [blocks[0]]
        for s in slots:
            pairs = []
            for h in range(2 * self.chips):
                far = (h + 2 * s) % (2 * self.chips)
                pairs.append((h, far) if back else (far, h))
            pulled.append(lax.ppermute(blocks[s], "ha", pairs))
        return pulled

    def turn(self, pair):
        if 2 * self.chips == BLOCKS:
            return self.stage(pair, 0)
        one = exchange(pair[0], 1)
        return jnp.stack([one, exchange(pair[1], 1)])

    def turn_again(self, *pairs):
        both = jnp.stack([block for single, first in pairs for block in (single, first[1])])
        return self.stage(both, 1) if 2 * self.chips == BLOCKS else exchange(both, 2)

    def swap(self, block):
        return lax.ppermute(block, "ha", [(h, h ^ 1) for h in range(2 * self.chips)])

    def stage(self, block, second):
        pairs = []
        columns = 2 * self.chips
        for e in range(self.parts):
            for h in range(columns):
                d = 1 + ((h % 2) ^ second)
                pairs.append((e * columns + h, (e ^ d) * columns + h))
        return lax.ppermute(block, ("ea", "ha"), pairs)

    def spread(self, mine, behind=(), swap_behind=()):
        one = self.stage(mine, 0)
        two = self.stage(mine, 1)
        mine, one, two = after((mine, one, two), *behind)
        three = self.stage(one, 1)
        mine, one, two = after((mine, one, two), *swap_behind)
        own = (mine, one, two, three)
        return own, tuple(self.swap(block) for block in own)


def after(value, *others):
    return lax.optimization_barrier((value, others))[0]


def add(*terms):
    return sum(term.astype(F32) for term in terms).astype(BF16)


def vector_rows(vectors, shift, bias):
    width = bias.shape[-1]
    rows = [jnp.pad(v, (0, width - v.shape[0])) for v in vectors]
    rows += [shift[:width], jnp.pad(shift[width:], (0, 2 * width - shift.shape[0])), bias]
    return jnp.stack(rows + [jnp.zeros_like(bias)] * (VEC_ROWS - len(rows)))


def half_call(half, kernel, outs, operands, arrays, scratch, name):
    block = pl.BlockSpec((2, *arrays[0].shape[1:]), lambda i: (half, 0, 0))
    return pl.pallas_call(
        kernel,
        grid=(1,),
        out_shape=outs,
        in_specs=[SMEM] + [whole_spec(*v.shape) for v in operands[1:]] + [block] * len(arrays),
        out_specs=jax.tree.map(lambda out: whole_spec(*out.shape), outs),
        scratch_shapes=scratch,
        compiler_params=PARAMS,
        name=name,
    )(*operands, *arrays)


def whole_spec(*shape):
    return pl.BlockSpec(shape, lambda i: (0,) * len(shape))


def shards(
    tokens,
    image_counts,
    kept_patches,
    norm1_gain,
    norm1_bias,
    qkv_weight,
    query_bias,
    value_bias,
    out_weight,
    out_bias,
    norm2_gain,
    norm2_bias,
    in_weight,
    in_bias,
    back_weight,
    back_bias,
    cotangent,
):
    parts = lax.axis_size("ea")
    columns = lax.axis_size("ha")
    me = lax.axis_index("ea")
    mine = lax.axis_index("ha")
    direct = columns == BLOCKS
    wires = Wires(parts, columns)
    if direct:
        meta = jnp.stack([me, mine // 2, mine % 2]).astype(jnp.int32)
    else:
        meta = jnp.stack([me, 0 * mine, 0 * mine]).astype(jnp.int32)
    narrow, slots = tokens.shape
    full = narrow * parts
    images = image_counts.shape[0] // parts
    most = kept_patches.shape[1]
    rows = -(-most // 16) * 16
    count = images * rows
    window = min(slots, (images * most + 127 + 127) // 128 * 128)
    heads = full // HEAD_DIM
    group_heads = narrow // HEAD_DIM
    width = in_weight.shape[1] * columns // BLOCKS
    half = 3 * narrow // 2

    vectors = (norm1_gain, norm1_bias, norm2_gain, norm2_bias, out_bias, back_bias)
    if direct:
        first, second = call(
            shard_kernel,
            (shaped(BF16, narrow + VEC_ROWS, width), shaped(BF16, 2 * narrow, width)),
            (qkv_weight, out_weight, in_weight, back_weight.T, in_bias, query_bias, value_bias)
            + vectors,
            name="shard",
        )

    turn_shapes = lambda r, c: (shaped(BF16, r, c), shaped(BF16, 2, r, c), shaped(BF16, r, c))
    packed = call(
        partial(pack_kernel, images, rows, window),
        turn_shapes(count, 2 * narrow),
        (meta, image_counts, tokens, cotangent),
        (pltpu.SMEM((image_counts.shape[0],), jnp.int32), pltpu.VMEM((count, window), BF16)),
        "pack",
    )

    if direct:
        turned_once = wires.turn(packed[1])
        z_first = wires.over_z([first] * 4)
        turned_once = after(turned_once, *z_first[1:])
        xs = (packed[0], turned_once, wires.turn_again((packed[2], turned_once)))
        z_second = wires.over_z([after(second, *z_first)] * 4)
        g1 = wires.spread(jnp.stack(z_first), (), (*z_second, xs[2]))
        z_second = jnp.stack(after(z_second, g1[0][1]))
        xs = after(xs, z_second)
    else:
        turned_once = wires.turn(packed[1])
        xs = (packed[0], turned_once, wires.turn_again((packed[2], turned_once)))
        pairs = jnp.zeros((group_heads, HEAD_DIM), BF16)
        by_head = lambda bias: bias.reshape(group_heads, HEAD_DIM)
        shift = jnp.stack([by_head(query_bias), pairs, by_head(value_bias)], 1).reshape(-1)

        def whole(weight):
            wide = lax.all_gather(weight, "ha", axis=1, tiled=True)
            blocks = wide.reshape(narrow, BLOCKS, -1).transpose(1, 0, 2)
            return lax.all_gather(blocks, "ea")

        def arrange(blocks):
            sides = []
            for p in range(2):
                side = []
                for a in range(parts):
                    d = a if p == 0 or a in (0, 3) else 3 - a
                    row = lax.dynamic_index_in_dim(blocks, me ^ d, 0, False)
                    side.append(jnp.stack([row[2 * s + p] for s in range(4)]))
                sides.append(tuple(side))
            return sides

        biases = lax.all_gather(in_bias, "ha", tiled=True).reshape(BLOCKS, -1)
        below = jax.vmap(lambda bias: vector_rows(vectors, shift, bias))(biases)
        g1 = jnp.concatenate([whole(qkv_weight), whole(out_weight)], 3)
        g1 = jnp.concatenate([g1, lax.all_gather(below, "ea")], 2)
        g1 = arrange(g1)
        g2 = arrange(jnp.concatenate([whole(in_weight), whole(back_weight.T)], 2))

    omega = 1.0 / 10000.0 ** (jnp.arange(narrow, dtype=F32) / narrow)
    angles = jnp.arange(16, dtype=F32)[:, None] * omega[None, :]
    patches = jnp.pad(kept_patches, ((0, 0), (0, 128 - most)))

    x1, x0, h1, qkv, chances, mixed, vecs, inb, wq, wo = call(
        partial(attend_kernel, images, rows),
        (
            shaped(F32, count, full),
            shaped(F32, count, full),
            shaped(BF16, count, full),
            shaped(BF16, parts, count, 3 * narrow),
            shaped(BF16, heads, images, rows, rows),
            shaped(BF16, count, full),
            shaped(F32, VEC_ROWS, full),
            shaped(F32, BLOCKS, 1, width),
            shaped(BF16, parts, full, 3 * narrow),
            shaped(BF16, parts, narrow, full),
        ),
        (meta, image_counts, *xs, patches, jnp.sin(angles), jnp.cos(angles), *g1[0], *g1[1]),
        (
            pltpu.VMEM((parts, 1, 3 * narrow), F32),
            pltpu.VMEM((parts, parts, narrow, narrow), BF16),
        ),
        "attend",
    )

    if direct:
        g2 = wires.spread(z_second, (x1,))
    far_z = lambda block, s: wires.over_z([block] * 4, True, (s,))[1]
    four = shaped(BF16, 4, 2, 2 * narrow, width)
    two = shaped(BF16, 2, 2, 2 * narrow, width)
    pair_bias = shaped(F32, 2, 1, width)
    wide_low, wide = shaped(BF16, count, full), shaped(F32, count, full)
    sent2, kept2, dinb_sent, dinb_kept, h2, dy, y_first, dh_first = half_call(
        0,
        hidden_first_kernel,
        (four, four, pair_bias, pair_bias, wide_low, wide_low, wide, wide),
        (meta, x1, *xs, vecs, inb),
        (*g2[0], *g2[1]),
        (),
        "hidden_first",
    )
    arrived2 = wires.swap(sent2) if direct else jnp.zeros_like(sent2)
    sent3, dinb_a, y_first, dh_first = half_call(
        1,
        hidden_a_kernel,
        (four, pair_bias, wide, wide),
        (meta, h2, dy, y_first, dh_first, inb),
        g2[1],
        (),
        "hidden_a",
    )
    arrived3 = wires.swap(sent3) if direct else jnp.zeros_like(sent3)
    arrived2 = after(arrived2, y_first)
    passed2 = add(kept2[2:], arrived2[2:])
    if direct:
        arrived_pass2 = wires.stage(passed2, 1)
    kept3, passed3, dinb_b, *outs, dx1, da, vec_grads = half_call(
        1,
        hidden_b_kernel,
        (two, two, pair_bias) + turn_shapes(count // 2, 2 * narrow) + (wide, wide_low, shaped(F32, 8, full)),
        (meta, x1, after(h2, passed2), dy, y_first, dh_first, vecs, inb, arrived3),
        g2[0],
        (pltpu.VMEM((full, 2 * width), F32), pltpu.VMEM((full, 2 * width), F32)),
        "hidden_b",
    )
    if direct:
        arrived = after(arrived_pass2, da)
        once2 = add(kept2[0], arrived2[0], arrived[0])
        next2 = add(kept2[1], arrived2[1], arrived[1])
        arrived_next2 = wires.stage(next2, 0)
        arrived_pass3 = wires.stage(after(passed3, next2), 1)
        da = after(da, once2, next2)
    dqkv, halves, dwo, dshift, sent1 = call(
        partial(attend_back_kernel, images, rows),
        (
            shaped(BF16, parts, count, 3 * narrow),
            shaped(BF16, parts, 2, count, half),
            shaped(F32, parts, parts, 2, narrow, narrow // 2),
            shaped(F32, parts, 1, 3 * narrow),
            shaped(BF16, 4, 4, narrow, width),
        ),
        (meta, da, mixed, qkv, chances, wo, h1),
        (pltpu.VMEM((parts, count, narrow), BF16), pltpu.VMEM((full, half), F32)),
        "attend_back",
    )
    if direct:
        arrived = after(arrived_pass3, dqkv)
        once3, next3 = add(kept3[0], arrived[0]), add(kept3[1], arrived[1])
        next3, sent1, x0 = after((next3, sent1, x0), once3)
        arrived_next3 = wires.stage(next3, 0)
        arrived1 = wires.swap(sent1)
    outs[1] = wires.turn(after(outs[1], once3 if direct else dqkv))
    *gx, sent_below, kept_below = call(
        first_back_kernel,
        turn_shapes(count // 2, 2 * narrow)
        + (shaped(BF16, 4, 4, VEC_ROWS, width),) * 2,
        (meta, x0, dqkv, wq, dx1, vecs, vec_grads, dshift, dinb_sent, dinb_a, dinb_kept, dinb_b),
        (pltpu.VMEM((8, full), F32),),
        name="first_back",
    )
    if direct:
        arrived_below = wires.swap(sent_below)
        total2 = add(once2, after(arrived_next2, gx[0]))
        h1 = after(h1, total2, outs[1])
    else:
        arrived1, arrived_below = jnp.zeros_like(sent1), jnp.zeros_like(sent_below)
    kept1, passed1 = call(
        first_kept_kernel,
        (shaped(BF16, 2, 4, narrow + VEC_ROWS, width),) * 2,
        (meta, h1, halves, dwo, kept_below, arrived1, arrived_below),
        (pltpu.VMEM((full, half), F32),),
        "first_kept",
    )
    gx[1] = wires.turn(gx[1])
    if direct:
        arrived = wires.stage(passed1, 1)
        total3 = add(once3, after(arrived_next3, kept1))
        far = [far_z(total2[1], 1), far_z(total3[0], 2), far_z(total3[1], 3)]
        grad_in, grad_back = call(
            finish_second_kernel,
            (shaped(F32, narrow, width),) * 2,
            (total2[0], *far),
            name="finish_second",
        )
        arrived = after(arrived, far[1], gx[1])
        once1, next1 = add(kept1[0], arrived[0]), add(kept1[1], arrived[1])
        total = add(once1, wires.stage(next1, 0))
        z_first = wires.over_z([total[s] for s in range(4)], back=True)
        gx[1] = after(gx[1], next1)
    second = wires.turn_again((outs[2], outs[1]), (gx[2], gx[1]))

    output, grad_tokens = call(
        partial(unpack_kernel, images, rows, window),
        (shaped(BF16, narrow, slots), shaped(F32, narrow, slots)),
        (meta, image_counts, *outs[:2], *gx[:2], second),
        (
            pltpu.SMEM((image_counts.shape[0],), jnp.int32),
            pltpu.VMEM((count, window), BF16),
            pltpu.VMEM((narrow, slots), F32),
            pltpu.VMEM((narrow, slots), F32),
        ),
        "unpack",
    )

    if direct:
        line = shaped(F32, narrow)
        grad_qkv, grad_out, grad_in_bias, grad_query, grad_value, *small = call(
            finish_kernel,
            (shaped(F32, narrow, half), shaped(F32, narrow, narrow // 2), shaped(F32, width))
            + (line,) * 8,
            z_first,
            name="finish",
        )
    else:

        def spread(sent, kept, passed):
            later = jnp.concatenate([kept, passed], 0)
            tall = []
            for e in range(parts):
                d = me ^ e
                row = [None] * BLOCKS
                for p, side in ((1, sent), (0, later)):
                    q = jnp.where((d == 0) | (d == 3) | (p == 0), d, 3 - d)
                    four = lax.dynamic_index_in_dim(side, q, 0, False)
                    for s in range(4):
                        row[2 * s + p] = four[s]
                tall.append(jnp.stack(row))
            return jnp.stack(tall).astype(F32)

        def scatter(blocks):
            flat = lax.psum_scatter(blocks, "ea").transpose(1, 0, 2).reshape(narrow, -1)
            return lax.psum_scatter(flat, "ha", scatter_dimension=1, tiled=True)

        sent1 = jnp.concatenate([sent1, sent_below], 2)
        sent2, kept2 = jnp.concatenate([sent2, sent3], 1), jnp.concatenate([kept2[:2], kept3], 1)
        d2 = spread(sent2, kept2, jnp.concatenate([passed2, passed3], 1))
        d1 = spread(sent1, kept1, passed1)
        grad_in, grad_back = scatter(d2[:, :, :narrow]), scatter(d2[:, :, narrow:])
        grad_qkv, grad_out = scatter(d1[:, :, :narrow, :half]), scatter(d1[:, :, :narrow, half:])
        small = lax.psum(d1[:, :, narrow:], ("ea", "ha"))
        size = in_bias.shape[0]
        grad_in_bias = lax.dynamic_slice_in_dim(small[0, :, 8].reshape(-1), mine * size, size, 0)
        small = lax.dynamic_index_in_dim(small[:, 0], me, 0, False)
        shift = jnp.concatenate([small[6], small[7]])[: 3 * narrow]
        shift = shift.reshape(group_heads, 3, HEAD_DIM)
        grad_query, grad_value = shift[:, 0].reshape(-1), shift[:, 2].reshape(-1)
        small = small[:, :narrow]
    return (
        output,
        grad_tokens,
        small[0],
        small[1],
        grad_qkv,
        grad_query,
        grad_value,
        grad_out,
        small[4],
        small[2],
        small[3],
        grad_in,
        grad_in_bias,
        grad_back.T,
        small[5],
    )


def solution(mesh):
    return jax.shard_map(
        shards,
        mesh=mesh,
        in_specs=(
            P("ea", "ha"),
            P("ha"),
            P("ha", None),
            P("ea"),
            P("ea"),
            P("ea", "ha"),
            P("ea"),
            P("ea"),
            P("ea", "ha"),
            P("ea"),
            P("ea"),
            P("ea"),
            P("ea", "ha"),
            P("ha"),
            P("ha", "ea"),
            P("ea"),
            P("ea", "ha"),
        ),
        out_specs=(
            P("ea", "ha"),
            P("ea", "ha"),
            P("ea"),
            P("ea"),
            P("ea", "ha"),
            P("ea"),
            P("ea"),
            P("ea", "ha"),
            P("ea"),
            P("ea"),
            P("ea"),
            P("ea", "ha"),
            P("ha"),
            P("ha", "ea"),
            P("ea"),
        ),
        check_vma=False,
    )
```

```python
from functools import partial

import jax
import jax.numpy as jnp
from jax import lax
from jax.experimental import pallas as pl
from jax.experimental.pallas import tpu as pltpu
from jax.sharding import PartitionSpec as P

HEAD_DIM = 64
GRID = 14
EPSILON = 1e-06
NEGATIVE = -1e30
BLOCKS = 8
VEC_ROWS = 16
NN = (((1,), (0,)), ((), ()))
NT = (((1,), (1,)), ((), ()))
TN = (((0,), (0,)), ((), ()))
F32 = jnp.float32
BF16 = jnp.bfloat16
SMEM = pl.BlockSpec(memory_space=pltpu.SMEM)
VMEM = pl.BlockSpec(memory_space=pltpu.VMEM)
PARAMS = pltpu.CompilerParams(vmem_limit_bytes=56 * 1024 * 1024)


def dot(a, b, dims):
    return lax.dot_general(a, b, dims, preferred_element_type=F32)


def iota(shape, axis):
    return lax.broadcasted_iota(jnp.int32, shape, axis)


def prefix(counts, starts):
    total = jnp.int32(0)
    for i in range(counts.shape[0]):
        starts[i] = total
        total = total + counts[i]


def select_rows(sel, counts, starts, part, images, rows, window, slots):
    first = starts[part * images]
    base = jnp.minimum(first // 128, (slots - window) // 128) * 128
    base = pl.multiple_of(base, 128)
    row = iota((rows, window), 0)
    gap = iota((rows, window), 1) - row
    for i in range(images):
        image = part * images + i
        hit = (gap == starts[image] - base) & (row < counts[image])
        sel[i * rows : (i + 1) * rows, :] = jnp.where(hit, 1.0, 0.0).astype(BF16)
    return base


def pack_kernel(images, rows, window, meta, counts, tokens, cotangent, *refs):
    (mine, pair, single), (starts, sel, parts) = refs[:3], refs[3:]
    prefix(counts, starts)

    def pack_part(a, carry):
        part = meta[0] ^ place(a, meta[2])
        base = select_rows(sel, counts, starts, part, images, rows, window, tokens.shape[1])
        span = pl.ds(base, window)
        both = jnp.concatenate([tokens[:, span], cotangent[:, span]], 0)
        parts[a] = dot(sel[...], both, NT).astype(BF16)
        return carry

    lax.fori_loop(0, 4, pack_part, 0)
    mine[...] = parts[0]
    pair[0] = parts[1]
    single[...] = parts[2]
    pair[1] = parts[3]


def shard_kernel(qkv, out, into, back, hidden_bias, query, value, *refs):
    vectors, (first, second) = refs[:-2], refs[-2:]
    narrow, half = qkv.shape
    width = first.shape[1]
    first[:narrow, :half] = qkv[...]
    first[:narrow, half:] = out[...]
    empty = jnp.zeros((1, width), F32)
    wide = lambda ref: ref[...].astype(F32).reshape(1, -1)
    rows = [jnp.concatenate([wide(ref), empty[:, narrow:]], 1) for ref in vectors]
    query, value = wide(query), wide(value)
    shift = []
    for i in range(narrow // HEAD_DIM):
        at = slice(i * HEAD_DIM, (i + 1) * HEAD_DIM)
        shift += [query[:, at], empty[:, :HEAD_DIM], value[:, at]]
    shift = jnp.concatenate(shift + [empty[:, : 2 * width - 2 * half]], 1)
    rows += [shift[:, :width], shift[:, width:], wide(hidden_bias)]
    rows.append(jnp.zeros((VEC_ROWS - len(rows), width), F32))
    first[narrow:, :] = jnp.concatenate(rows, 0).astype(BF16)
    second[:narrow, :] = into[...]
    second[narrow:, :] = back[...]


def unpack_kernel(images, rows, window, meta, counts, *refs):
    outs, grads, second = refs[:2], refs[2:4], refs[4]
    output, grad, starts, sel, total, parts = refs[5:]
    narrow, slots = output.shape
    prefix(counts, starts)
    total[...] = jnp.zeros_like(total)
    for a in range(4):
        for i, pieces in enumerate((outs, grads)):
            pair = pieces[0][...] if a == 0 else pieces[1][0] if a == 1 else second[2 * i + a - 2]
            tall = jnp.concatenate([pair[:, :narrow], pair[:, narrow:]], 0)
            parts[a, :, i * narrow : (i + 1) * narrow] = tall

    def unpack_part(a, carry):
        part = meta[0] ^ place(a, meta[2])
        base = select_rows(sel, counts, starts, part, images, rows, window, slots)
        total[:, pl.ds(base, window)] += dot(parts[a], sel[...], TN)
        return carry

    lax.fori_loop(0, 4, unpack_part, 0)
    output[...] = total[:narrow].astype(output.dtype)
    grad[...] = total[narrow:]


def store_halves(core, mine, pair, single, values):
    low, narrow = mine.shape[0], mine.shape[1] // 2
    parts = []
    for d in range(4):
        span = slice(d * narrow, (d + 1) * narrow)
        both = [values[:low, span], values[low:, span]]
        parts.append(jnp.concatenate(both, 1).astype(mine.dtype))
    mine[...] = parts[0]
    pair[0] = jnp.where(core == 0, parts[1], parts[2])
    single[...] = jnp.where(core == 0, parts[2], parts[1])
    pair[1] = parts[3]


def turned(core, mine, first, second):
    one, two = first[0], second[0]
    swap = core == 1
    return [mine[...], jnp.where(swap, two, one), jnp.where(swap, one, two), second[1]]


def norm_parts(values):
    center = jnp.mean(values, 1, keepdims=True)
    centred = values - center
    factor = lax.rsqrt(jnp.mean(centred * centred, 1, keepdims=True) + EPSILON)
    return centred * factor, factor


def norm_back(grad, xhat, factor, gain):
    scaled = grad * gain
    mean = jnp.mean(scaled, 1, keepdims=True)
    across = jnp.mean(scaled * xhat, 1, keepdims=True)
    return factor * (scaled - mean - xhat * across)


def colsum(values):
    return jnp.sum(values, 0, keepdims=True)


def place(d, core):
    if isinstance(d, int):
        return d if d in (0, 3) else jnp.where(core == 0, d, 3 - d)
    return jnp.where((d == 0) | (d == 3) | (core == 0), d, 3 - d)


def column_of(meta, p, s):
    return (meta[1] + s) % 4, meta[2] ^ p


def whole_block(refs, rows, swap):
    columns = []
    for s in range(refs[0].shape[0]):
        one, two = refs[1][s, rows], refs[2][s, rows]
        one, two = jnp.where(swap, two, one), jnp.where(swap, one, two)
        columns.append(jnp.concatenate([refs[0][s, rows], one, two, refs[3][s, rows]], 0))
    return jnp.concatenate(columns, 1)


def head_part(qkv, z, span, head, part):
    at = (3 * head + part) * HEAD_DIM
    return qkv[z, span, at : at + HEAD_DIM]


def attend_kernel(images, rows, meta, counts, *refs):
    x_refs, (patches, sines, cosines), arrays = refs[:3], refs[3:6], (refs[6:10], refs[10:14])
    x1_out, x0, h1_out, qkv_out, p_out, o_out, vecs, inb, wq, wo = refs[14:24]
    shifts, wo_parts = refs[24:]
    me = meta[0]
    parts, narrow = wo.shape[0], wo.shape[1]
    wide = 3 * narrow
    half = wide // 2
    outer = narrow // 2
    heads = narrow // HEAD_DIM

    def unfold(core):
        for p in range(2):
            for a in range(parts):
                d = a if a in (0, 3) or (core ^ p) == 0 else 3 - a
                low, high = d * narrow, (d + 1) * narrow
                for s in range(4):
                    z = (meta[1] + s) % 4
                    k = core ^ p
                    ref = arrays[p][a]
                    wq[z, low:high, k * half : (k + 1) * half] = ref[s, :narrow, :half]
                    wo_parts[me ^ d, z, :, k * outer : (k + 1) * outer] = ref[s, :narrow, half:]
                    if a == 0:
                        inb[2 * z + k] = ref[s, narrow:, :].astype(F32)[8:9]
                if p == 0:
                    small = arrays[p][a][0, narrow:, :].astype(F32)
                    vecs[:, low:high] = small[:, :narrow]
                    rest = small[7:8, : wide - small.shape[1]]
                    shifts[me ^ d] = jnp.concatenate([small[6:7], rest], 1)

    pl.when(meta[2] == 0)(partial(unfold, 0))
    pl.when(meta[2] == 1)(partial(unfold, 1))
    for t in range(parts):
        for d in range(parts):
            wo[t, :, d * narrow : (d + 1) * narrow] = wo_parts[t, me ^ d]
    tokens = turned(meta[2], *x_refs)
    for d in range(parts):
        e = me ^ d
        table = jnp.where(e % 2 == 0, sines[...], cosines[...])
        high = table.astype(BF16)
        rest = table - high.astype(F32)
        middle = rest.astype(BF16)
        low = (rest - middle.astype(F32)).astype(BF16)
        stacked = jnp.concatenate([high, middle, low], 0)
        depth = table.shape[0]
        for i in range(images):
            patch = patches[pl.ds(me * images + i, 1), :rows]
            row = (patch * 4682) >> 16
            spot = jnp.where(e < 2, row, patch - row * GRID)
            hot = jnp.where(iota((depth, rows), 0) == spot, 1.0, 0.0).astype(BF16)
            placed = dot(jnp.concatenate([hot, hot, hot], 0), stacked, TN)
            x0[i * rows : (i + 1) * rows, d * narrow : (d + 1) * narrow] = (
                tokens[d][i * rows : (i + 1) * rows, :narrow].astype(F32) + placed
            )
    xhat, _ = norm_parts(x0[...])
    h1 = (xhat * vecs[0:1] + vecs[1:2]).astype(BF16)
    h1_out[...] = h1

    def project(z, carry):
        qkv_out[z] = (dot(h1, wq[z], NN) + shifts[z]).astype(BF16)
        return carry

    lax.fori_loop(0, parts, project, 0)
    factor = HEAD_DIM ** (-0.5)
    each = [(z, i) for z in range(parts) for i in range(heads)]
    def attend_image(b, carry):
        seen = iota((rows, rows), 0) < counts[me * images + b]
        span = pl.ds(pl.multiple_of(b * rows, 16), rows)
        scores, mixed = [], []
        for z, i in each:
            query, key = (head_part(qkv_out, z, span, i, part) for part in (0, 1))
            scores.append(jnp.where(seen, dot(key, query, NT) * factor, NEGATIVE))
        for n, score in enumerate(scores):
            weights = jnp.exp(score - jnp.max(score, 0, keepdims=True))
            scale = 1.0 / jnp.sum(weights, 0, keepdims=True)
            p_out[n, b] = (weights * scale).astype(BF16)
        for n, (z, i) in enumerate(each):
            value = head_part(qkv_out, z, span, i, 2)
            mixed.append(dot(p_out[n, b], value, TN).astype(BF16))
        for z in range(parts):
            together = jnp.concatenate(mixed[z * heads : (z + 1) * heads], 1)
            o_out[span, z * narrow : (z + 1) * narrow] = together
        return carry

    lax.fori_loop(0, images, attend_image, 0)
    attn = dot(o_out[...], jnp.concatenate([wo[z] for z in range(parts)], 0), NN)
    x1_out[...] = x0[...] + attn + vecs[4:5]


def hidden_step(p, meta, h2, dy, inb, refs, first):
    narrow = refs[0].shape[1] // 2
    swap = (meta[2] ^ p) == 1
    w_in = whole_block(refs, slice(0, narrow), swap)
    w_back = whole_block(refs, slice(narrow, 2 * narrow), swap)
    biases = []
    for s in range(refs[0].shape[0]):
        z, k = column_of(meta, p, first + s)
        biases.append(inb[2 * z + k])
    hidden = dot(h2, w_in, NN) + jnp.concatenate(biases, 1)
    gate = 0.5 + 0.5 * lax.erf(hidden * (0.5**0.5))
    active = (hidden * gate).astype(BF16)
    slope = gate + hidden * jnp.exp(-0.5 * hidden * hidden) * 0.3989422804014327
    low = (dot(dy, w_back, NN) * slope).astype(BF16)
    return active, low, dot(active, w_back, NT), dot(low, w_in, NT)


def store_bias(dinb, low):
    total = colsum(low.astype(F32))
    width = dinb.shape[-1]
    for s in range(dinb.shape[0]):
        dinb[s] = total[:, s * width : (s + 1) * width]


def store_blocks(out, core, h2, dy, active, low):
    narrow, width = out.shape[2] // 2, out.shape[3]
    d_in = dot(h2, low, TN).astype(BF16)
    d_back = dot(dy, active, TN).astype(BF16)
    for d in range(4):
        q = place(d, core)
        for s in range(out.shape[1]):
            part = (slice(d * narrow, (d + 1) * narrow), slice(s * width, (s + 1) * width))
            out[q, s, :narrow] = d_in[part]
            out[q, s, narrow:] = d_back[part]


def hidden_first_kernel(meta, *refs):
    x1, y_refs, (vecs, inb), own, other = refs[0], refs[1:4], refs[4:6], refs[6:10], refs[10:14]
    sent, kept, sent_dinb, kept_dinb, h2s, dys, y_total, dh_total = refs[14:]
    narrow = y_refs[0].shape[1] // 2
    for d, part in enumerate(turned(meta[2], *y_refs)):
        dys[:, d * narrow : (d + 1) * narrow] = part[:, narrow:]
    xhat, _ = norm_parts(x1[...])
    h2s[...] = (xhat * vecs[2:3] + vecs[3:4]).astype(BF16)
    h2, dy = h2s[...], dys[...]
    for p, arrays, out, dinb in ((1, other, sent, sent_dinb), (0, own, kept, kept_dinb)):
        active, low, y_part, dh_part = hidden_step(p, meta, h2, dy, inb, arrays, 0)
        y_total[...] = y_part if p else y_total[...] + y_part
        dh_total[...] = dh_part if p else dh_total[...] + dh_part
        store_bias(dinb, low)
        store_blocks(out, meta[2] ^ p, h2, dy, active, low)


def hidden_a_kernel(meta, h2s, dys, y_first, dh_first, inb, *refs):
    arrays = refs[:4]
    sent, dinb, y_total, dh_total = refs[4:]
    h2, dy = h2s[...], dys[...]
    active, low, y_part, dh_part = hidden_step(1, meta, h2, dy, inb, arrays, 2)
    y_total[...] = y_first[...] + y_part
    dh_total[...] = dh_first[...] + dh_part
    store_bias(dinb, low)
    store_blocks(sent, 1 - meta[2], h2, dy, active, low)


def hidden_b_kernel(meta, x1, h2s, dys, y_first, dh_first, vecs, inb, arrived, *refs):
    arrays, (kept, sent, dinb), turn = refs[:4], refs[4:7], refs[7:10]
    dx1, da, vec_grads, d_in, d_back = refs[10:]
    h2, dy = h2s[...], dys[...]
    active, low, y_part, dh_part = hidden_step(0, meta, h2, dy, inb, arrays, 2)
    store_bias(dinb, low)
    narrow, width = kept.shape[2] // 2, kept.shape[3]
    d_in[...] = dot(h2, low, TN)
    d_back[...] = dot(dy, active, TN)
    for q in range(4):
        start = place(q, meta[2]) * narrow
        span = pl.ds(pl.multiple_of(start, narrow) if q in (1, 2) else start, narrow)
        into = kept if q < 2 else sent
        for s in range(2):
            columns = slice(s * width, (s + 1) * width)
            part = d_in[span, columns] + arrived[q, s, :narrow].astype(F32)
            into[q % 2, s, :narrow] = part.astype(BF16)
            part = d_back[span, columns] + arrived[q, s, narrow:].astype(F32)
            into[q % 2, s, narrow:] = part.astype(BF16)
    values = x1[...]
    store_halves(meta[2], *turn, values + y_first[...] + y_part + vecs[5:6])
    xhat, factor = norm_parts(values)
    grad = dh_first[...] + dh_part
    dy_wide = dy.astype(F32)
    total = dy_wide + norm_back(grad, xhat, factor, vecs[2:3])
    dx1[...] = total
    narrowed = total.astype(BF16)
    da[...] = narrowed
    vec_grads[0:1] = colsum(grad * xhat)
    vec_grads[1:2] = colsum(grad)
    vec_grads[2:3] = colsum(narrowed.astype(F32))
    vec_grads[3:4] = colsum(dy_wide)
    vec_grads[4:8] = jnp.zeros_like(vec_grads[4:8])


def attend_back_kernel(images, rows, meta, da, o_ref, qkv, p_ref, wo, h1, *refs):
    dqkv, halves, dwo, dshift, sent, do_ref, dw_ref = refs
    parts, narrow = wo.shape[0], wo.shape[1]
    heads = narrow // HEAD_DIM
    factor = HEAD_DIM ** (-0.5)
    grad = da[...]
    outer = narrow // 2
    for z in range(parts):
        do_ref[z] = dot(grad, wo[z], NT).astype(BF16)
    each = [(z, i) for z in range(parts) for i in range(heads)]
    def attend_image(b, carry):
        span = pl.ds(pl.multiple_of(b * rows, 16), rows)
        grad_heads, grad_scores, grads = [], [], []
        for z, i in each:
            grad_head = do_ref[z, span, i * HEAD_DIM : (i + 1) * HEAD_DIM]
            grad_heads.append(grad_head)
            grad_scores.append(dot(head_part(qkv, z, span, i, 2), grad_head, NT))
        for n in range(len(each)):
            chance = p_ref[n, b].astype(F32)
            inner = jnp.sum(chance * grad_scores[n], 0, keepdims=True)
            grad_scores[n] = (chance * (grad_scores[n] - inner)).astype(BF16)
        for n, (z, i) in enumerate(each):
            query, key = (head_part(qkv, z, span, i, part) for part in (0, 1))
            grads.append((dot(grad_scores[n], key, TN) * factor).astype(BF16))
            grads.append((dot(grad_scores[n], query, NN) * factor).astype(BF16))
            grads.append(dot(p_ref[n, b], grad_heads[n], NN).astype(BF16))
        for z in range(parts):
            together = grads[3 * z * heads : 3 * (z + 1) * heads]
            dqkv[z, span, :] = jnp.concatenate(together, 1)
        return carry

    lax.fori_loop(0, images, attend_image, 0)
    half = dqkv.shape[2] // 2
    for z in range(parts):
        dshift[z] = colsum(dqkv[z].astype(F32))
        for k in range(2):
            halves[z, k] = dqkv[z, :, k * half : (k + 1) * half]
        dw = dot(o_ref[:, z * narrow : (z + 1) * narrow], grad, TN)
        for d in range(parts):
            for k in range(2):
                at = d * narrow + k * outer
                dwo[z, d, k] = dw[:, at : at + outer]

    def store(q, s, block):
        sent[q, s] = block.astype(BF16)

    first_grad(1, meta, h1, halves, dwo, dw_ref, store)


def first_back_kernel(
    meta, x0, dqkv, wq, dx1, vecs, vec_grads, dshift, sent_dinb, sent_rest, kept_dinb, kept_rest, *refs
):
    turn, (sent, kept, rows_out) = refs[:3], refs[3:]
    me = meta[0]
    parts, narrow = dqkv.shape[0], dqkv.shape[2] // 3
    width = sent.shape[3]
    grad = dot(dqkv[0], wq[0], NT)
    for z in range(1, parts):
        grad += dot(dqkv[z], wq[z], NT)
    xhat, factor = norm_parts(x0[...])
    store_halves(meta[2], *turn, dx1[...] + norm_back(grad, xhat, factor, vecs[0:1]))
    rows_out[0:1] = colsum(grad * xhat)
    rows_out[1:2] = colsum(grad)
    rows_out[2:6] = vec_grads[0:4]
    gap = jnp.zeros((6, width - narrow), F32)
    tail = jnp.zeros((VEC_ROWS - 9, width), F32)
    for d in range(parts):
        six = jnp.concatenate([rows_out[0:6, d * narrow : (d + 1) * narrow], gap], 1)
        shift = dshift[me ^ d]
        second = jnp.concatenate([shift[:, width:], gap[0:1, : 2 * width - shift.shape[1]]], 1)
        for s in range(4):
            for p, first, rest, out in (
                (1, sent_dinb, sent_rest, sent),
                (0, kept_dinb, kept_rest, kept),
            ):
                bias = first[s] if s < 2 else rest[s - 2]
                lines = [six, shift[:, :width], second, bias, tail]
                out[place(d, meta[2] ^ p), s] = jnp.concatenate(lines, 0).astype(BF16)


def first_grad(p, meta, h1, halves, dwo, dw, store):
    me = meta[0]
    narrow = dwo.shape[3]
    feature = h1[...]

    def slot(s, carry):
        z, k = column_of(meta, p, s)
        dw[...] = dot(feature, halves[z, k], TN)
        for q in range(4):
            d = place(q, meta[2] ^ p)
            start = d * narrow
            span = pl.ds(pl.multiple_of(start, narrow) if q in (1, 2) else start, narrow)
            store(q, s, jnp.concatenate([dw[span, :], dwo[me ^ d, z ^ me, k]], 1))
        return carry

    lax.fori_loop(0, 4, slot, 0)


def first_kept_kernel(meta, h1, halves, dwo, arrived, kept, sent, dw):
    def store(q, s, block):
        into = kept if q < 2 else sent
        into[q % 2, s] = (block + arrived[q, s].astype(F32)).astype(BF16)

    first_grad(0, meta, h1, halves, dwo, dw, store)


def finish_second_kernel(*refs):
    pieces, (d_in, d_back) = refs[:4], refs[4:]
    narrow = d_in.shape[0]
    for rows, out in ((slice(0, narrow), d_in), (slice(narrow, 2 * narrow), d_back)):
        total = pieces[0][rows].astype(F32)
        for piece in pieces[1:]:
            total += piece[rows].astype(F32)
        out[...] = total


def finish_kernel(*refs):
    pieces, (qkv, out, hidden_bias, query, value), vectors = refs[:4], refs[4:9], refs[9:]
    narrow, half = qkv.shape
    total = pieces[0][...].astype(F32)
    for piece in pieces[1:]:
        total += piece[...].astype(F32)
    qkv[...] = total[:narrow, :half]
    out[...] = total[:narrow, half:]
    for i, ref in enumerate(vectors):
        ref[...] = total[narrow + i : narrow + i + 1, :narrow].reshape(ref.shape)
    shift = jnp.concatenate([total[narrow + 6 : narrow + 7], total[narrow + 7 : narrow + 8]], 1)
    heads = range(narrow // HEAD_DIM)
    for ref, part in ((query, 0), (value, 2)):
        pieces = [shift[:, (3 * i + part) * HEAD_DIM :][:, :HEAD_DIM] for i in heads]
        ref[...] = jnp.concatenate(pieces, 1).reshape(ref.shape)
    hidden_bias[...] = total[narrow + 8 : narrow + 9].reshape(hidden_bias.shape)


def call(kernel, outs, operands, scratch=(), name=None):
    specs = []
    for value in operands:
        specs.append(SMEM if value.dtype == jnp.int32 and value.ndim == 1 else VMEM)
    return pl.pallas_call(
        kernel,
        out_shape=outs,
        in_specs=specs,
        out_specs=jax.tree.map(lambda _: VMEM, outs),
        scratch_shapes=scratch,
        compiler_params=PARAMS,
        name=name,
    )(*operands)


def shaped(dtype, *shape):
    return jax.ShapeDtypeStruct(shape, dtype)


def exchange(block, d):
    size = lax.axis_size("ea")
    return block if d == 0 else lax.ppermute(block, "ea", [(e, e ^ d) for e in range(size)])


class Wires:
    def __init__(self, parts, columns):
        self.parts, self.chips = parts, columns // 2

    def over_z(self, blocks, back=False, slots=(1, 2, 3)):
        pulled = [blocks[0]]
        for s in slots:
            pairs = []
            for h in range(2 * self.chips):
                far = (h + 2 * s) % (2 * self.chips)
                pairs.append((h, far) if back else (far, h))
            pulled.append(lax.ppermute(blocks[s], "ha", pairs))
        return pulled

    def turn(self, pair):
        if 2 * self.chips == BLOCKS:
            return self.stage(pair, 0)
        one = exchange(pair[0], 1)
        return jnp.stack([one, exchange(pair[1], 1)])

    def turn_again(self, *pairs):
        both = jnp.stack([block for single, first in pairs for block in (single, first[1])])
        return self.stage(both, 1) if 2 * self.chips == BLOCKS else exchange(both, 2)

    def swap(self, block):
        return lax.ppermute(block, "ha", [(h, h ^ 1) for h in range(2 * self.chips)])

    def stage(self, block, second):
        pairs = []
        columns = 2 * self.chips
        for e in range(self.parts):
            for h in range(columns):
                d = 1 + ((h % 2) ^ second)
                pairs.append((e * columns + h, (e ^ d) * columns + h))
        return lax.ppermute(block, ("ea", "ha"), pairs)

    def spread(self, mine, behind=(), swap_behind=(), one=None):
        one = self.stage(mine, 0) if one is None else one
        two = self.stage(mine, 1)
        mine, one, two = after((mine, one, two), *behind)
        three = self.stage(one, 1)
        mine, one, two = after((mine, one, two), *swap_behind)
        own = (mine, one, two, three)
        return own, tuple(self.swap(block) for block in own)


def after(value, *others):
    return lax.optimization_barrier((value, others))[0]


def add(*terms):
    return sum(term.astype(F32) for term in terms).astype(BF16)


def vector_rows(vectors, shift, bias):
    width = bias.shape[-1]
    rows = [jnp.pad(v, (0, width - v.shape[0])) for v in vectors]
    rows += [shift[:width], jnp.pad(shift[width:], (0, 2 * width - shift.shape[0])), bias]
    return jnp.stack(rows + [jnp.zeros_like(bias)] * (VEC_ROWS - len(rows)))


def half_call(half, kernel, outs, operands, arrays, scratch, name):
    block = pl.BlockSpec((2, *arrays[0].shape[1:]), lambda i: (half, 0, 0))
    return pl.pallas_call(
        kernel,
        grid=(1,),
        out_shape=outs,
        in_specs=[SMEM] + [whole_spec(*v.shape) for v in operands[1:]] + [block] * len(arrays),
        out_specs=jax.tree.map(lambda out: whole_spec(*out.shape), outs),
        scratch_shapes=scratch,
        compiler_params=PARAMS,
        name=name,
    )(*operands, *arrays)


def whole_spec(*shape):
    return pl.BlockSpec(shape, lambda i: (0,) * len(shape))


def shards(
    tokens,
    image_counts,
    kept_patches,
    norm1_gain,
    norm1_bias,
    qkv_weight,
    query_bias,
    value_bias,
    out_weight,
    out_bias,
    norm2_gain,
    norm2_bias,
    in_weight,
    in_bias,
    back_weight,
    back_bias,
    cotangent,
):
    parts = lax.axis_size("ea")
    columns = lax.axis_size("ha")
    me = lax.axis_index("ea")
    mine = lax.axis_index("ha")
    direct = columns == BLOCKS
    wires = Wires(parts, columns)
    if direct:
        meta = jnp.stack([me, mine // 2, mine % 2]).astype(jnp.int32)
    else:
        meta = jnp.stack([me, 0 * mine, 0 * mine]).astype(jnp.int32)
    narrow, slots = tokens.shape
    full = narrow * parts
    images = image_counts.shape[0] // parts
    most = kept_patches.shape[1]
    rows = -(-most // 16) * 16
    count = images * rows
    window = min(slots, (images * most + 127 + 127) // 128 * 128)
    heads = full // HEAD_DIM
    group_heads = narrow // HEAD_DIM
    width = in_weight.shape[1] * columns // BLOCKS
    half = 3 * narrow // 2

    vectors = (norm1_gain, norm1_bias, norm2_gain, norm2_bias, out_bias, back_bias)
    if direct:
        first, second = call(
            shard_kernel,
            (shaped(BF16, narrow + VEC_ROWS, width), shaped(BF16, 2 * narrow, width)),
            (qkv_weight, out_weight, in_weight, back_weight.T, in_bias, query_bias, value_bias)
            + vectors,
            name="shard",
        )

    turn_shapes = lambda r, c: (shaped(BF16, r, c), shaped(BF16, 2, r, c), shaped(BF16, r, c))
    packed = call(
        partial(pack_kernel, images, rows, window),
        turn_shapes(count, 2 * narrow),
        (meta, image_counts, tokens, cotangent),
        (
            pltpu.SMEM((image_counts.shape[0],), jnp.int32),
            pltpu.VMEM((count, window), BF16),
            pltpu.VMEM((parts, count, 2 * narrow), BF16),
        ),
        "pack",
    )

    if direct:
        turned_once = wires.turn(packed[1])
        z_first = wires.over_z([first] * 4)
        turned_once = after(turned_once, *z_first[1:])
        xs = (packed[0], turned_once, wires.turn_again((packed[2], turned_once)))
        z_second = wires.over_z([after(second, *z_first)] * 4)
        g1 = wires.spread(jnp.stack(z_first), (), z_second)
        z_second = jnp.stack(after(z_second, g1[0][1]))
        xs = after(xs, z_second)
    else:
        turned_once = wires.turn(packed[1])
        xs = (packed[0], turned_once, wires.turn_again((packed[2], turned_once)))
        pairs = jnp.zeros((group_heads, HEAD_DIM), BF16)
        by_head = lambda bias: bias.reshape(group_heads, HEAD_DIM)
        shift = jnp.stack([by_head(query_bias), pairs, by_head(value_bias)], 1).reshape(-1)

        def whole(weight):
            wide = lax.all_gather(weight, "ha", axis=1, tiled=True)
            blocks = wide.reshape(narrow, BLOCKS, -1).transpose(1, 0, 2)
            return lax.all_gather(blocks, "ea")

        def arrange(blocks):
            sides = []
            for p in range(2):
                side = []
                for a in range(parts):
                    d = a if p == 0 or a in (0, 3) else 3 - a
                    row = lax.dynamic_index_in_dim(blocks, me ^ d, 0, False)
                    side.append(jnp.stack([row[2 * s + p] for s in range(4)]))
                sides.append(tuple(side))
            return sides

        biases = lax.all_gather(in_bias, "ha", tiled=True).reshape(BLOCKS, -1)
        below = jax.vmap(lambda bias: vector_rows(vectors, shift, bias))(biases)
        g1 = jnp.concatenate([whole(qkv_weight), whole(out_weight)], 3)
        g1 = jnp.concatenate([g1, lax.all_gather(below, "ea")], 2)
        g1 = arrange(g1)
        g2 = arrange(jnp.concatenate([whole(in_weight), whole(back_weight.T)], 2))

    omega = 1.0 / 10000.0 ** (jnp.arange(narrow, dtype=F32) / narrow)
    angles = jnp.arange(16, dtype=F32)[:, None] * omega[None, :]
    patches = jnp.pad(kept_patches, ((0, 0), (0, 128 - most)))

    x1, x0, h1, qkv, chances, mixed, vecs, inb, wq, wo = call(
        partial(attend_kernel, images, rows),
        (
            shaped(F32, count, full),
            shaped(F32, count, full),
            shaped(BF16, count, full),
            shaped(BF16, parts, count, 3 * narrow),
            shaped(BF16, heads, images, rows, rows),
            shaped(BF16, count, full),
            shaped(F32, VEC_ROWS, full),
            shaped(F32, BLOCKS, 1, width),
            shaped(BF16, parts, full, 3 * narrow),
            shaped(BF16, parts, narrow, full),
        ),
        (meta, image_counts, *xs, patches, jnp.sin(angles), jnp.cos(angles), *g1[0], *g1[1]),
        (
            pltpu.VMEM((parts, 1, 3 * narrow), F32),
            pltpu.VMEM((parts, parts, narrow, narrow), BF16),
        ),
        "attend",
    )

    if direct:
        g2 = wires.spread(z_second, (x1,))
    far_z = lambda block, s: wires.over_z([block] * 4, True, (s,))[1]
    four = shaped(BF16, 4, 2, 2 * narrow, width)
    two = shaped(BF16, 2, 2, 2 * narrow, width)
    pair_bias = shaped(F32, 2, 1, width)
    wide_low, wide = shaped(BF16, count, full), shaped(F32, count, full)
    sent2, kept2, dinb_sent, dinb_kept, h2, dy, y_first, dh_first = half_call(
        0,
        hidden_first_kernel,
        (four, four, pair_bias, pair_bias, wide_low, wide_low, wide, wide),
        (meta, x1, *xs, vecs, inb),
        (*g2[0], *g2[1]),
        (),
        "hidden_first",
    )
    arrived2 = wires.swap(sent2) if direct else jnp.zeros_like(sent2)
    sent3, dinb_a, y_first, dh_first = half_call(
        1,
        hidden_a_kernel,
        (four, pair_bias, wide, wide),
        (meta, h2, dy, y_first, dh_first, inb),
        g2[1],
        (),
        "hidden_a",
    )
    arrived3 = wires.swap(sent3) if direct else jnp.zeros_like(sent3)
    arrived2 = after(arrived2, y_first)
    passed2 = add(kept2[2:], arrived2[2:])
    if direct:
        arrived_pass2 = wires.stage(passed2, 1)
    kept3, passed3, dinb_b, *outs, dx1, da, vec_grads = half_call(
        1,
        hidden_b_kernel,
        (two, two, pair_bias) + turn_shapes(count // 2, 2 * narrow) + (wide, wide_low, shaped(F32, 8, full)),
        (meta, x1, after(h2, passed2), dy, y_first, dh_first, vecs, inb, arrived3),
        g2[0],
        (pltpu.VMEM((full, 2 * width), F32), pltpu.VMEM((full, 2 * width), F32)),
        "hidden_b",
    )
    if direct:
        arrived = after(arrived_pass2, da)
        once2 = add(kept2[0], arrived2[0], arrived[0])
        next2 = add(kept2[1], arrived2[1], arrived[1])
        arrived_next2 = wires.stage(next2, 0)
        arrived_pass3 = wires.stage(after(passed3, next2), 1)
        da = after(da, once2, next2)
    dqkv, halves, dwo, dshift, sent1 = call(
        partial(attend_back_kernel, images, rows),
        (
            shaped(BF16, parts, count, 3 * narrow),
            shaped(BF16, parts, 2, count, half),
            shaped(F32, parts, parts, 2, narrow, narrow // 2),
            shaped(F32, parts, 1, 3 * narrow),
            shaped(BF16, 4, 4, narrow, width),
        ),
        (meta, da, mixed, qkv, chances, wo, h1),
        (pltpu.VMEM((parts, count, narrow), BF16), pltpu.VMEM((full, half), F32)),
        "attend_back",
    )
    if direct:
        arrived = after(arrived_pass3, dqkv)
        once3, next3 = add(kept3[0], arrived[0]), add(kept3[1], arrived[1])
        next3, sent1, h1 = after((next3, sent1, h1), once3)
        arrived1 = wires.swap(sent1)
    else:
        arrived1 = jnp.zeros_like(sent1)
    kept1, passed1 = call(
        first_kept_kernel,
        (shaped(BF16, 2, 4, narrow, width),) * 2,
        (meta, h1, halves, dwo, arrived1),
        (pltpu.VMEM((full, half), F32),),
        "first_kept",
    )
    if direct:
        arrived_pass1 = wires.stage(passed1, 1)
        total2 = add(once2, after(arrived_next2, kept1))
        arrived_next3 = wires.stage(next3, 0)
        x0 = after(x0, kept1, total2)
    outs[1] = wires.turn(after(outs[1], kept1))
    *gx, sent_below, kept_below = call(
        first_back_kernel,
        turn_shapes(count // 2, 2 * narrow)
        + (shaped(BF16, 4, 4, VEC_ROWS, width),) * 2,
        (meta, x0, dqkv, wq, dx1, vecs, vec_grads, dshift, dinb_sent, dinb_a, dinb_kept, dinb_b),
        (pltpu.VMEM((8, full), F32),),
        name="first_back",
    )
    gx[1] = wires.turn(gx[1])
    if direct:
        below = add(kept_below, wires.swap(sent_below))
        arrived_below = wires.stage(below[2:], 1)
        total3 = add(once3, after(arrived_next3, gx[0]))
        far = [far_z(total2[1], 1), far_z(total3[0], 2), far_z(total3[1], 3)]
        grad_in, grad_back = call(
            finish_second_kernel,
            (shaped(F32, narrow, width),) * 2,
            (total2[0], *far),
            name="finish_second",
        )
        arrived = after(arrived_pass1, gx[0], outs[1], far[1], gx[1])
        once1, next1 = add(kept1[0], arrived[0]), add(kept1[1], arrived[1])
        arrived_next1 = wires.stage(next1, 0)
        below_next = add(below[1], arrived_below[1])
        below_total = add(below[0], arrived_below[0], wires.stage(below_next, 0))
        total = jnp.concatenate([add(once1, arrived_next1), below_total], 1)
        z_first = wires.over_z([total[s] for s in range(4)], back=True)
        gx[1] = after(gx[1], next1)
    second = wires.turn_again((outs[2], outs[1]), (gx[2], gx[1]))

    output, grad_tokens = call(
        partial(unpack_kernel, images, rows, window),
        (shaped(BF16, narrow, slots), shaped(F32, narrow, slots)),
        (meta, image_counts, *outs[:2], *gx[:2], second),
        (
            pltpu.SMEM((image_counts.shape[0],), jnp.int32),
            pltpu.VMEM((count, window), BF16),
            pltpu.VMEM((2 * narrow, slots), F32),
            pltpu.VMEM((parts, count, 2 * narrow), BF16),
        ),
        "unpack",
    )

    if direct:
        line = shaped(F32, narrow)
        grad_qkv, grad_out, grad_in_bias, grad_query, grad_value, *small = call(
            finish_kernel,
            (shaped(F32, narrow, half), shaped(F32, narrow, narrow // 2), shaped(F32, width))
            + (line,) * 8,
            z_first,
            name="finish",
        )
    else:

        def spread(sent, kept, passed):
            later = jnp.concatenate([kept, passed], 0)
            tall = []
            for e in range(parts):
                d = me ^ e
                row = [None] * BLOCKS
                for p, side in ((1, sent), (0, later)):
                    q = jnp.where((d == 0) | (d == 3) | (p == 0), d, 3 - d)
                    four = lax.dynamic_index_in_dim(side, q, 0, False)
                    for s in range(4):
                        row[2 * s + p] = four[s]
                tall.append(jnp.stack(row))
            return jnp.stack(tall).astype(F32)

        def scatter(blocks):
            flat = lax.psum_scatter(blocks, "ea").transpose(1, 0, 2).reshape(narrow, -1)
            return lax.psum_scatter(flat, "ha", scatter_dimension=1, tiled=True)

        sent1 = jnp.concatenate([sent1, sent_below], 2)
        kept1 = jnp.concatenate([kept1, kept_below[:2]], 2)
        passed1 = jnp.concatenate([passed1, kept_below[2:]], 2)
        sent2, kept2 = jnp.concatenate([sent2, sent3], 1), jnp.concatenate([kept2[:2], kept3], 1)
        d2 = spread(sent2, kept2, jnp.concatenate([passed2, passed3], 1))
        d1 = spread(sent1, kept1, passed1)
        grad_in, grad_back = scatter(d2[:, :, :narrow]), scatter(d2[:, :, narrow:])
        grad_qkv, grad_out = scatter(d1[:, :, :narrow, :half]), scatter(d1[:, :, :narrow, half:])
        small = lax.psum(d1[:, :, narrow:], ("ea", "ha"))
        size = in_bias.shape[0]
        grad_in_bias = lax.dynamic_slice_in_dim(small[0, :, 8].reshape(-1), mine * size, size, 0)
        small = lax.dynamic_index_in_dim(small[:, 0], me, 0, False)
        shift = jnp.concatenate([small[6], small[7]])[: 3 * narrow]
        shift = shift.reshape(group_heads, 3, HEAD_DIM)
        grad_query, grad_value = shift[:, 0].reshape(-1), shift[:, 2].reshape(-1)
        small = small[:, :narrow]
    return (
        output,
        grad_tokens,
        small[0],
        small[1],
        grad_qkv,
        grad_query,
        grad_value,
        grad_out,
        small[4],
        small[2],
        small[3],
        grad_in,
        grad_in_bias,
        grad_back.T,
        small[5],
    )


def solution(mesh):
    return jax.shard_map(
        shards,
        mesh=mesh,
        in_specs=(
            P("ea", "ha"),
            P("ha"),
            P("ha", None),
            P("ea"),
            P("ea"),
            P("ea", "ha"),
            P("ea"),
            P("ea"),
            P("ea", "ha"),
            P("ea"),
            P("ea"),
            P("ea"),
            P("ea", "ha"),
            P("ha"),
            P("ha", "ea"),
            P("ea"),
            P("ea", "ha"),
        ),
        out_specs=(
            P("ea", "ha"),
            P("ea", "ha"),
            P("ea"),
            P("ea"),
            P("ea", "ha"),
            P("ea"),
            P("ea"),
            P("ea", "ha"),
            P("ea"),
            P("ea"),
            P("ea"),
            P("ea", "ha"),
            P("ha"),
            P("ha", "ea"),
            P("ea"),
        ),
        check_vma=False,
    )
```

```python
from functools import partial

import jax
import jax.numpy as jnp
from jax import lax
from jax.experimental import pallas as pl
from jax.experimental.pallas import tpu as pltpu
from jax.sharding import PartitionSpec as P

HEAD_DIM = 64
GRID = 14
EPSILON = 1e-06
NEGATIVE = -1e30
BLOCKS = 8
VEC_ROWS = 16
NN = (((1,), (0,)), ((), ()))
NT = (((1,), (1,)), ((), ()))
TN = (((0,), (0,)), ((), ()))
F32 = jnp.float32
BF16 = jnp.bfloat16
SMEM = pl.BlockSpec(memory_space=pltpu.SMEM)
VMEM = pl.BlockSpec(memory_space=pltpu.VMEM)
PARAMS = pltpu.CompilerParams(vmem_limit_bytes=56 * 1024 * 1024)


def dot(a, b, dims):
    return lax.dot_general(a, b, dims, preferred_element_type=F32)


def iota(shape, axis):
    return lax.broadcasted_iota(jnp.int32, shape, axis)


def prefix(counts, starts):
    total = jnp.int32(0)
    for i in range(counts.shape[0]):
        starts[i] = total
        total = total + counts[i]


def select_rows(sel, counts, starts, part, images, rows, window, slots):
    first = starts[part * images]
    base = jnp.minimum(first // 128, (slots - window) // 128) * 128
    base = pl.multiple_of(base, 128)
    row = iota((rows, window), 0)
    gap = iota((rows, window), 1) - row
    for i in range(images):
        image = part * images + i
        hit = (gap == starts[image] - base) & (row < counts[image])
        sel[i * rows : (i + 1) * rows, :] = jnp.where(hit, 1.0, 0.0).astype(BF16)
    return base


def pack_kernel(images, rows, window, meta, counts, tokens, cotangent, *refs):
    (mine, pair, single), (starts, sel) = refs[:3], refs[3:]
    prefix(counts, starts)
    for a in range(4):
        part = meta[0] ^ place(a, meta[2])
        base = select_rows(sel, counts, starts, part, images, rows, window, tokens.shape[1])
        span = pl.ds(base, window)
        both = jnp.concatenate([tokens[:, span], cotangent[:, span]], 0)
        block = dot(sel[...], both, NT).astype(BF16)
        if a in (0, 2):
            (single if a else mine)[...] = block
        else:
            pair[a // 2] = block


def shard_kernel(qkv, out, into, back, hidden_bias, query, value, *refs):
    vectors, (first, second) = refs[:-2], refs[-2:]
    narrow, half = qkv.shape
    width = first.shape[1]
    first[:narrow, :half] = qkv[...]
    first[:narrow, half:] = out[...]
    empty = jnp.zeros((1, width), F32)
    wide = lambda ref: ref[...].astype(F32).reshape(1, -1)
    rows = [jnp.concatenate([wide(ref), empty[:, narrow:]], 1) for ref in vectors]
    query, value = wide(query), wide(value)
    shift = []
    for i in range(narrow // HEAD_DIM):
        at = slice(i * HEAD_DIM, (i + 1) * HEAD_DIM)
        shift += [query[:, at], empty[:, :HEAD_DIM], value[:, at]]
    shift = jnp.concatenate(shift + [empty[:, : 2 * width - 2 * half]], 1)
    rows += [shift[:, :width], shift[:, width:], wide(hidden_bias)]
    rows.append(jnp.zeros((VEC_ROWS - len(rows), width), F32))
    first[narrow:, :] = jnp.concatenate(rows, 0).astype(BF16)
    second[:narrow, :] = into[...]
    second[narrow:, :] = back[...]


def unpack_kernel(images, rows, window, meta, counts, *refs):
    outs, grads, second = refs[:2], refs[2:4], refs[4]
    output, grad, starts, sel, total, grad_total = refs[5:]
    narrow, slots = output.shape
    prefix(counts, starts)
    total[...] = jnp.zeros_like(total)
    grad_total[...] = jnp.zeros_like(grad_total)
    for a in range(4):
        part = meta[0] ^ place(a, meta[2])
        base = select_rows(sel, counts, starts, part, images, rows, window, slots)
        span = pl.ds(base, window)
        for i, (refs, into) in enumerate(((outs, total), (grads, grad_total))):
            pair = refs[0][...] if a == 0 else refs[1][0] if a == 1 else second[2 * i + a - 2]
            tall = jnp.concatenate([pair[:, :narrow], pair[:, narrow:]], 0)
            into[:, span] += dot(tall, sel[...], TN)
    output[...] = total[...].astype(output.dtype)
    grad[...] = grad_total[...]


def store_halves(core, mine, pair, single, values):
    low, narrow = mine.shape[0], mine.shape[1] // 2
    parts = []
    for d in range(4):
        span = slice(d * narrow, (d + 1) * narrow)
        both = [values[:low, span], values[low:, span]]
        parts.append(jnp.concatenate(both, 1).astype(mine.dtype))
    mine[...] = parts[0]
    pair[0] = jnp.where(core == 0, parts[1], parts[2])
    single[...] = jnp.where(core == 0, parts[2], parts[1])
    pair[1] = parts[3]


def turned(core, mine, first, second):
    one, two = first[0], second[0]
    swap = core == 1
    return [mine[...], jnp.where(swap, two, one), jnp.where(swap, one, two), second[1]]


def norm_parts(values):
    center = jnp.mean(values, 1, keepdims=True)
    centred = values - center
    factor = lax.rsqrt(jnp.mean(centred * centred, 1, keepdims=True) + EPSILON)
    return centred * factor, factor


def norm_back(grad, xhat, factor, gain):
    scaled = grad * gain
    mean = jnp.mean(scaled, 1, keepdims=True)
    across = jnp.mean(scaled * xhat, 1, keepdims=True)
    return factor * (scaled - mean - xhat * across)


def colsum(values):
    return jnp.sum(values, 0, keepdims=True)


def place(d, core):
    return d if d in (0, 3) else jnp.where(core == 0, d, 3 - d)


def column_of(meta, p, s):
    return (meta[1] + s) % 4, meta[2] ^ p


def whole_block(refs, rows, swap):
    columns = []
    for s in range(refs[0].shape[0]):
        one, two = refs[1][s, rows], refs[2][s, rows]
        one, two = jnp.where(swap, two, one), jnp.where(swap, one, two)
        columns.append(jnp.concatenate([refs[0][s, rows], one, two, refs[3][s, rows]], 0))
    return jnp.concatenate(columns, 1)


def head_part(qkv, z, span, head, part):
    at = (3 * head + part) * HEAD_DIM
    return qkv[z, span, at : at + HEAD_DIM]


def attend_kernel(images, rows, meta, counts, *refs):
    x_refs, (patches, sines, cosines), arrays = refs[:3], refs[3:6], (refs[6:10], refs[10:14])
    x1_out, x0, h1_out, qkv_out, p_out, o_out, vecs, inb, wq, wo = refs[14:24]
    shifts, wo_parts = refs[24:]
    me = meta[0]
    parts, narrow = wo.shape[0], wo.shape[1]
    wide = 3 * narrow
    half = wide // 2
    outer = narrow // 2
    heads = narrow // HEAD_DIM

    def unfold(core):
        for p in range(2):
            for a in range(parts):
                d = a if a in (0, 3) or (core ^ p) == 0 else 3 - a
                low, high = d * narrow, (d + 1) * narrow
                for s in range(4):
                    z = (meta[1] + s) % 4
                    k = core ^ p
                    ref = arrays[p][a]
                    wq[z, low:high, k * half : (k + 1) * half] = ref[s, :narrow, :half]
                    wo_parts[me ^ d, z, :, k * outer : (k + 1) * outer] = ref[s, :narrow, half:]
                    if a == 0:
                        inb[2 * z + k] = ref[s, narrow:, :].astype(F32)[8:9]
                if p == 0:
                    small = arrays[p][a][0, narrow:, :].astype(F32)
                    vecs[:, low:high] = small[:, :narrow]
                    rest = small[7:8, : wide - small.shape[1]]
                    shifts[me ^ d] = jnp.concatenate([small[6:7], rest], 1)

    pl.when(meta[2] == 0)(partial(unfold, 0))
    pl.when(meta[2] == 1)(partial(unfold, 1))
    for t in range(parts):
        for d in range(parts):
            wo[t, :, d * narrow : (d + 1) * narrow] = wo_parts[t, me ^ d]
    tokens = turned(meta[2], *x_refs)
    for d in range(parts):
        e = me ^ d
        table = jnp.where(e % 2 == 0, sines[...], cosines[...])
        high = table.astype(BF16)
        rest = table - high.astype(F32)
        middle = rest.astype(BF16)
        low = (rest - middle.astype(F32)).astype(BF16)
        stacked = jnp.concatenate([high, middle, low], 0)
        depth = table.shape[0]
        for i in range(images):
            patch = patches[pl.ds(me * images + i, 1), :rows]
            row = (patch * 4682) >> 16
            spot = jnp.where(e < 2, row, patch - row * GRID)
            hot = jnp.where(iota((depth, rows), 0) == spot, 1.0, 0.0).astype(BF16)
            placed = dot(jnp.concatenate([hot, hot, hot], 0), stacked, TN)
            x0[i * rows : (i + 1) * rows, d * narrow : (d + 1) * narrow] = (
                tokens[d][i * rows : (i + 1) * rows, :narrow].astype(F32) + placed
            )
    xhat, _ = norm_parts(x0[...])
    h1 = (xhat * vecs[0:1] + vecs[1:2]).astype(BF16)
    h1_out[...] = h1
    for z in range(parts):
        qkv_out[z] = (dot(h1, wq[z], NN) + shifts[z]).astype(BF16)
    factor = HEAD_DIM ** (-0.5)
    each = [(z, i) for z in range(parts) for i in range(heads)]
    for b in range(images):
        seen = iota((rows, rows), 0) < counts[me * images + b]
        span = slice(b * rows, (b + 1) * rows)
        scores, mixed = [], []
        for z, i in each:
            query, key = (head_part(qkv_out, z, span, i, part) for part in (0, 1))
            scores.append(jnp.where(seen, dot(key, query, NT) * factor, NEGATIVE))
        for n, score in enumerate(scores):
            weights = jnp.exp(score - jnp.max(score, 0, keepdims=True))
            scale = 1.0 / jnp.sum(weights, 0, keepdims=True)
            p_out[n, b] = (weights * scale).astype(BF16)
        for n, (z, i) in enumerate(each):
            value = head_part(qkv_out, z, span, i, 2)
            mixed.append(dot(p_out[n, b], value, TN).astype(BF16))
        for z in range(parts):
            together = jnp.concatenate(mixed[z * heads : (z + 1) * heads], 1)
            o_out[span, z * narrow : (z + 1) * narrow] = together
    attn = dot(o_out[...], jnp.concatenate([wo[z] for z in range(parts)], 0), NN)
    x1_out[...] = x0[...] + attn + vecs[4:5]


def hidden_step(p, meta, h2, dy, inb, refs, first):
    narrow = refs[0].shape[1] // 2
    swap = (meta[2] ^ p) == 1
    w_in = whole_block(refs, slice(0, narrow), swap)
    w_back = whole_block(refs, slice(narrow, 2 * narrow), swap)
    biases = []
    for s in range(refs[0].shape[0]):
        z, k = column_of(meta, p, first + s)
        biases.append(inb[2 * z + k])
    hidden = dot(h2, w_in, NN) + jnp.concatenate(biases, 1)
    gate = 0.5 + 0.5 * lax.erf(hidden * (0.5**0.5))
    active = (hidden * gate).astype(BF16)
    slope = gate + hidden * jnp.exp(-0.5 * hidden * hidden) * 0.3989422804014327
    low = (dot(dy, w_back, NN) * slope).astype(BF16)
    return active, low, dot(active, w_back, NT), dot(low, w_in, NT)


def store_bias(dinb, low):
    total = colsum(low.astype(F32))
    width = dinb.shape[-1]
    for s in range(dinb.shape[0]):
        dinb[s] = total[:, s * width : (s + 1) * width]


def store_blocks(out, core, h2, dy, active, low):
    narrow, width = out.shape[2] // 2, out.shape[3]
    d_in = dot(h2, low, TN).astype(BF16)
    d_back = dot(dy, active, TN).astype(BF16)
    for d in range(4):
        q = place(d, core)
        for s in range(out.shape[1]):
            part = (slice(d * narrow, (d + 1) * narrow), slice(s * width, (s + 1) * width))
            out[q, s, :narrow] = d_in[part]
            out[q, s, narrow:] = d_back[part]


def hidden_first_kernel(meta, *refs):
    x1, y_refs, (vecs, inb), own, other = refs[0], refs[1:4], refs[4:6], refs[6:10], refs[10:14]
    sent, kept, sent_dinb, kept_dinb, h2s, dys, y_total, dh_total = refs[14:]
    narrow = y_refs[0].shape[1] // 2
    for d, part in enumerate(turned(meta[2], *y_refs)):
        dys[:, d * narrow : (d + 1) * narrow] = part[:, narrow:]
    xhat, _ = norm_parts(x1[...])
    h2s[...] = (xhat * vecs[2:3] + vecs[3:4]).astype(BF16)
    h2, dy = h2s[...], dys[...]
    for p, arrays, out, dinb in ((1, other, sent, sent_dinb), (0, own, kept, kept_dinb)):
        active, low, y_part, dh_part = hidden_step(p, meta, h2, dy, inb, arrays, 0)
        y_total[...] = y_part if p else y_total[...] + y_part
        dh_total[...] = dh_part if p else dh_total[...] + dh_part
        store_bias(dinb, low)
        store_blocks(out, meta[2] ^ p, h2, dy, active, low)


def hidden_a_kernel(meta, h2s, dys, y_first, dh_first, inb, *refs):
    arrays = refs[:4]
    sent, dinb, y_total, dh_total = refs[4:]
    h2, dy = h2s[...], dys[...]
    active, low, y_part, dh_part = hidden_step(1, meta, h2, dy, inb, arrays, 2)
    y_total[...] = y_first[...] + y_part
    dh_total[...] = dh_first[...] + dh_part
    store_bias(dinb, low)
    store_blocks(sent, 1 - meta[2], h2, dy, active, low)


def hidden_b_kernel(meta, x1, h2s, dys, y_first, dh_first, vecs, inb, arrived, *refs):
    arrays, (kept, sent, dinb), turn = refs[:4], refs[4:7], refs[7:10]
    dx1, da, vec_grads, d_in, d_back = refs[10:]
    h2, dy = h2s[...], dys[...]
    active, low, y_part, dh_part = hidden_step(0, meta, h2, dy, inb, arrays, 2)
    store_bias(dinb, low)
    narrow, width = kept.shape[2] // 2, kept.shape[3]
    d_in[...] = dot(h2, low, TN)
    d_back[...] = dot(dy, active, TN)
    for q in range(4):
        start = place(q, meta[2]) * narrow
        span = pl.ds(pl.multiple_of(start, narrow) if q in (1, 2) else start, narrow)
        into = kept if q < 2 else sent
        for s in range(2):
            columns = slice(s * width, (s + 1) * width)
            part = d_in[span, columns] + arrived[q, s, :narrow].astype(F32)
            into[q % 2, s, :narrow] = part.astype(BF16)
            part = d_back[span, columns] + arrived[q, s, narrow:].astype(F32)
            into[q % 2, s, narrow:] = part.astype(BF16)
    values = x1[...]
    store_halves(meta[2], *turn, values + y_first[...] + y_part + vecs[5:6])
    xhat, factor = norm_parts(values)
    grad = dh_first[...] + dh_part
    dy_wide = dy.astype(F32)
    total = dy_wide + norm_back(grad, xhat, factor, vecs[2:3])
    dx1[...] = total
    narrowed = total.astype(BF16)
    da[...] = narrowed
    vec_grads[0:1] = colsum(grad * xhat)
    vec_grads[1:2] = colsum(grad)
    vec_grads[2:3] = colsum(narrowed.astype(F32))
    vec_grads[3:4] = colsum(dy_wide)
    vec_grads[4:8] = jnp.zeros_like(vec_grads[4:8])


def attend_back_kernel(images, rows, meta, da, o_ref, qkv, p_ref, wo, h1, *refs):
    dqkv, halves, dwo, dshift, sent, do_ref, dw_ref = refs
    parts, narrow = wo.shape[0], wo.shape[1]
    heads = narrow // HEAD_DIM
    factor = HEAD_DIM ** (-0.5)
    grad = da[...]
    outer = narrow // 2
    for z in range(parts):
        do_ref[z] = dot(grad, wo[z], NT).astype(BF16)
    each = [(z, i) for z in range(parts) for i in range(heads)]
    for b in range(images):
        span = slice(b * rows, (b + 1) * rows)
        grad_heads, grad_scores, grads = [], [], []
        for z, i in each:
            grad_head = do_ref[z, span, i * HEAD_DIM : (i + 1) * HEAD_DIM]
            grad_heads.append(grad_head)
            grad_scores.append(dot(head_part(qkv, z, span, i, 2), grad_head, NT))
        for n in range(len(each)):
            chance = p_ref[n, b].astype(F32)
            inner = jnp.sum(chance * grad_scores[n], 0, keepdims=True)
            grad_scores[n] = (chance * (grad_scores[n] - inner)).astype(BF16)
        for n, (z, i) in enumerate(each):
            query, key = (head_part(qkv, z, span, i, part) for part in (0, 1))
            grads.append((dot(grad_scores[n], key, TN) * factor).astype(BF16))
            grads.append((dot(grad_scores[n], query, NN) * factor).astype(BF16))
            grads.append(dot(p_ref[n, b], grad_heads[n], NN).astype(BF16))
        for z in range(parts):
            together = grads[3 * z * heads : 3 * (z + 1) * heads]
            dqkv[z, span, :] = jnp.concatenate(together, 1)
    half = dqkv.shape[2] // 2
    for z in range(parts):
        dshift[z] = colsum(dqkv[z].astype(F32))
        for k in range(2):
            halves[z, k] = dqkv[z, :, k * half : (k + 1) * half]
        dw = dot(o_ref[:, z * narrow : (z + 1) * narrow], grad, TN)
        for d in range(parts):
            for k in range(2):
                at = d * narrow + k * outer
                dwo[z, d, k] = dw[:, at : at + outer]

    def store(q, s, block):
        sent[q, s] = block.astype(BF16)

    first_grad(1, meta, h1, halves, dwo, dw_ref, store)


def first_back_kernel(
    meta, x0, dqkv, wq, dx1, vecs, vec_grads, dshift, sent_dinb, sent_rest, kept_dinb, kept_rest, *refs
):
    turn, (sent, kept, rows_out) = refs[:3], refs[3:]
    me = meta[0]
    parts, narrow = dqkv.shape[0], dqkv.shape[2] // 3
    width = sent.shape[3]
    grad = dot(dqkv[0], wq[0], NT)
    for z in range(1, parts):
        grad += dot(dqkv[z], wq[z], NT)
    xhat, factor = norm_parts(x0[...])
    store_halves(meta[2], *turn, dx1[...] + norm_back(grad, xhat, factor, vecs[0:1]))
    rows_out[0:1] = colsum(grad * xhat)
    rows_out[1:2] = colsum(grad)
    rows_out[2:6] = vec_grads[0:4]
    gap = jnp.zeros((6, width - narrow), F32)
    tail = jnp.zeros((VEC_ROWS - 9, width), F32)
    for d in range(parts):
        six = jnp.concatenate([rows_out[0:6, d * narrow : (d + 1) * narrow], gap], 1)
        shift = dshift[me ^ d]
        second = jnp.concatenate([shift[:, width:], gap[0:1, : 2 * width - shift.shape[1]]], 1)
        for s in range(4):
            for p, first, rest, out in (
                (1, sent_dinb, sent_rest, sent),
                (0, kept_dinb, kept_rest, kept),
            ):
                bias = first[s] if s < 2 else rest[s - 2]
                lines = [six, shift[:, :width], second, bias, tail]
                out[place(d, meta[2] ^ p), s] = jnp.concatenate(lines, 0).astype(BF16)


def first_grad(p, meta, h1, halves, dwo, dw, store):
    me = meta[0]
    narrow = dwo.shape[3]
    feature = h1[...]
    for s in range(4):
        z, k = column_of(meta, p, s)
        dw[...] = dot(feature, halves[z, k], TN)
        for q in range(4):
            d = place(q, meta[2] ^ p)
            start = d * narrow
            span = pl.ds(pl.multiple_of(start, narrow) if q in (1, 2) else start, narrow)
            store(q, s, jnp.concatenate([dw[span, :], dwo[me ^ d, z ^ me, k]], 1))


def first_kept_kernel(meta, h1, halves, dwo, arrived, kept, sent, dw):
    def store(q, s, block):
        into = kept if q < 2 else sent
        into[q % 2, s] = (block + arrived[q, s].astype(F32)).astype(BF16)

    first_grad(0, meta, h1, halves, dwo, dw, store)


def finish_second_kernel(*refs):
    pieces, (d_in, d_back) = refs[:4], refs[4:]
    narrow = d_in.shape[0]
    for rows, out in ((slice(0, narrow), d_in), (slice(narrow, 2 * narrow), d_back)):
        total = pieces[0][rows].astype(F32)
        for piece in pieces[1:]:
            total += piece[rows].astype(F32)
        out[...] = total


def finish_kernel(*refs):
    pieces, (qkv, out, hidden_bias, query, value), vectors = refs[:4], refs[4:9], refs[9:]
    narrow, half = qkv.shape
    total = pieces[0][...].astype(F32)
    for piece in pieces[1:]:
        total += piece[...].astype(F32)
    qkv[...] = total[:narrow, :half]
    out[...] = total[:narrow, half:]
    for i, ref in enumerate(vectors):
        ref[...] = total[narrow + i : narrow + i + 1, :narrow].reshape(ref.shape)
    shift = jnp.concatenate([total[narrow + 6 : narrow + 7], total[narrow + 7 : narrow + 8]], 1)
    heads = range(narrow // HEAD_DIM)
    for ref, part in ((query, 0), (value, 2)):
        pieces = [shift[:, (3 * i + part) * HEAD_DIM :][:, :HEAD_DIM] for i in heads]
        ref[...] = jnp.concatenate(pieces, 1).reshape(ref.shape)
    hidden_bias[...] = total[narrow + 8 : narrow + 9].reshape(hidden_bias.shape)


def call(kernel, outs, operands, scratch=(), name=None):
    specs = []
    for value in operands:
        specs.append(SMEM if value.dtype == jnp.int32 and value.ndim == 1 else VMEM)
    return pl.pallas_call(
        kernel,
        out_shape=outs,
        in_specs=specs,
        out_specs=jax.tree.map(lambda _: VMEM, outs),
        scratch_shapes=scratch,
        compiler_params=PARAMS,
        name=name,
    )(*operands)


def shaped(dtype, *shape):
    return jax.ShapeDtypeStruct(shape, dtype)


def exchange(block, d):
    size = lax.axis_size("ea")
    return block if d == 0 else lax.ppermute(block, "ea", [(e, e ^ d) for e in range(size)])


class Wires:
    def __init__(self, parts, columns):
        self.parts, self.chips = parts, columns // 2

    def over_z(self, blocks, back=False, slots=(1, 2, 3)):
        pulled = [blocks[0]]
        for s in slots:
            pairs = []
            for h in range(2 * self.chips):
                far = (h + 2 * s) % (2 * self.chips)
                pairs.append((h, far) if back else (far, h))
            pulled.append(lax.ppermute(blocks[s], "ha", pairs))
        return pulled

    def turn(self, pair):
        if 2 * self.chips == BLOCKS:
            return self.stage(pair, 0)
        one = exchange(pair[0], 1)
        return jnp.stack([one, exchange(pair[1], 1)])

    def turn_again(self, *pairs):
        both = jnp.stack([block for single, first in pairs for block in (single, first[1])])
        return self.stage(both, 1) if 2 * self.chips == BLOCKS else exchange(both, 2)

    def swap(self, block):
        return lax.ppermute(block, "ha", [(h, h ^ 1) for h in range(2 * self.chips)])

    def stage(self, block, second):
        pairs = []
        columns = 2 * self.chips
        for e in range(self.parts):
            for h in range(columns):
                d = 1 + ((h % 2) ^ second)
                pairs.append((e * columns + h, (e ^ d) * columns + h))
        return lax.ppermute(block, ("ea", "ha"), pairs)

    def spread(self, mine, behind=(), swap_behind=(), one=None):
        one = self.stage(mine, 0) if one is None else one
        two = self.stage(mine, 1)
        mine, one, two = after((mine, one, two), *behind)
        three = self.stage(one, 1)
        mine, one, two = after((mine, one, two), *swap_behind)
        own = (mine, one, two, three)
        return own, tuple(self.swap(block) for block in own)


def after(value, *others):
    return lax.optimization_barrier((value, others))[0]


def add(*terms):
    return sum(term.astype(F32) for term in terms).astype(BF16)


def vector_rows(vectors, shift, bias):
    width = bias.shape[-1]
    rows = [jnp.pad(v, (0, width - v.shape[0])) for v in vectors]
    rows += [shift[:width], jnp.pad(shift[width:], (0, 2 * width - shift.shape[0])), bias]
    return jnp.stack(rows + [jnp.zeros_like(bias)] * (VEC_ROWS - len(rows)))


def half_call(half, kernel, outs, operands, arrays, scratch, name):
    block = pl.BlockSpec((2, *arrays[0].shape[1:]), lambda i: (half, 0, 0))
    return pl.pallas_call(
        kernel,
        grid=(1,),
        out_shape=outs,
        in_specs=[SMEM] + [whole_spec(*v.shape) for v in operands[1:]] + [block] * len(arrays),
        out_specs=jax.tree.map(lambda out: whole_spec(*out.shape), outs),
        scratch_shapes=scratch,
        compiler_params=PARAMS,
        name=name,
    )(*operands, *arrays)


def whole_spec(*shape):
    return pl.BlockSpec(shape, lambda i: (0,) * len(shape))


def shards(
    tokens,
    image_counts,
    kept_patches,
    norm1_gain,
    norm1_bias,
    qkv_weight,
    query_bias,
    value_bias,
    out_weight,
    out_bias,
    norm2_gain,
    norm2_bias,
    in_weight,
    in_bias,
    back_weight,
    back_bias,
    cotangent,
):
    parts = lax.axis_size("ea")
    columns = lax.axis_size("ha")
    me = lax.axis_index("ea")
    mine = lax.axis_index("ha")
    direct = columns == BLOCKS
    wires = Wires(parts, columns)
    if direct:
        meta = jnp.stack([me, mine // 2, mine % 2]).astype(jnp.int32)
    else:
        meta = jnp.stack([me, 0 * mine, 0 * mine]).astype(jnp.int32)
    narrow, slots = tokens.shape
    full = narrow * parts
    images = image_counts.shape[0] // parts
    most = kept_patches.shape[1]
    rows = -(-most // 16) * 16
    count = images * rows
    window = min(slots, (images * most + 127 + 127) // 128 * 128)
    heads = full // HEAD_DIM
    group_heads = narrow // HEAD_DIM
    width = in_weight.shape[1] * columns // BLOCKS
    half = 3 * narrow // 2

    vectors = (norm1_gain, norm1_bias, norm2_gain, norm2_bias, out_bias, back_bias)
    if direct:
        first, second = call(
            shard_kernel,
            (shaped(BF16, narrow + VEC_ROWS, width), shaped(BF16, 2 * narrow, width)),
            (qkv_weight, out_weight, in_weight, back_weight.T, in_bias, query_bias, value_bias)
            + vectors,
            name="shard",
        )

    turn_shapes = lambda r, c: (shaped(BF16, r, c), shaped(BF16, 2, r, c), shaped(BF16, r, c))
    packed = call(
        partial(pack_kernel, images, rows, window),
        turn_shapes(count, 2 * narrow),
        (meta, image_counts, tokens, cotangent),
        (pltpu.SMEM((image_counts.shape[0],), jnp.int32), pltpu.VMEM((count, window), BF16)),
        "pack",
    )

    if direct:
        turned_once = wires.turn(packed[1])
        z_first = wires.over_z([first] * 4)
        turned_once = after(turned_once, *z_first[1:])
        xs = (packed[0], turned_once, wires.turn_again((packed[2], turned_once)))
        z_second = wires.over_z([after(second, *z_first)] * 4)
        g1 = wires.spread(jnp.stack(z_first), (), z_second)
        z_second = jnp.stack(after(z_second, g1[0][1]))
        xs = after(xs, z_second)
    else:
        turned_once = wires.turn(packed[1])
        xs = (packed[0], turned_once, wires.turn_again((packed[2], turned_once)))
        pairs = jnp.zeros((group_heads, HEAD_DIM), BF16)
        by_head = lambda bias: bias.reshape(group_heads, HEAD_DIM)
        shift = jnp.stack([by_head(query_bias), pairs, by_head(value_bias)], 1).reshape(-1)

        def whole(weight):
            wide = lax.all_gather(weight, "ha", axis=1, tiled=True)
            blocks = wide.reshape(narrow, BLOCKS, -1).transpose(1, 0, 2)
            return lax.all_gather(blocks, "ea")

        def arrange(blocks):
            sides = []
            for p in range(2):
                side = []
                for a in range(parts):
                    d = a if p == 0 or a in (0, 3) else 3 - a
                    row = lax.dynamic_index_in_dim(blocks, me ^ d, 0, False)
                    side.append(jnp.stack([row[2 * s + p] for s in range(4)]))
                sides.append(tuple(side))
            return sides

        biases = lax.all_gather(in_bias, "ha", tiled=True).reshape(BLOCKS, -1)
        below = jax.vmap(lambda bias: vector_rows(vectors, shift, bias))(biases)
        g1 = jnp.concatenate([whole(qkv_weight), whole(out_weight)], 3)
        g1 = jnp.concatenate([g1, lax.all_gather(below, "ea")], 2)
        g1 = arrange(g1)
        g2 = arrange(jnp.concatenate([whole(in_weight), whole(back_weight.T)], 2))

    omega = 1.0 / 10000.0 ** (jnp.arange(narrow, dtype=F32) / narrow)
    angles = jnp.arange(16, dtype=F32)[:, None] * omega[None, :]
    patches = jnp.pad(kept_patches, ((0, 0), (0, 128 - most)))

    x1, x0, h1, qkv, chances, mixed, vecs, inb, wq, wo = call(
        partial(attend_kernel, images, rows),
        (
            shaped(F32, count, full),
            shaped(F32, count, full),
            shaped(BF16, count, full),
            shaped(BF16, parts, count, 3 * narrow),
            shaped(BF16, heads, images, rows, rows),
            shaped(BF16, count, full),
            shaped(F32, VEC_ROWS, full),
            shaped(F32, BLOCKS, 1, width),
            shaped(BF16, parts, full, 3 * narrow),
            shaped(BF16, parts, narrow, full),
        ),
        (meta, image_counts, *xs, patches, jnp.sin(angles), jnp.cos(angles), *g1[0], *g1[1]),
        (
            pltpu.VMEM((parts, 1, 3 * narrow), F32),
            pltpu.VMEM((parts, parts, narrow, narrow), BF16),
        ),
        "attend",
    )

    if direct:
        g2 = wires.spread(z_second, (x1,))
    far_z = lambda block, s: wires.over_z([block] * 4, True, (s,))[1]
    four = shaped(BF16, 4, 2, 2 * narrow, width)
    two = shaped(BF16, 2, 2, 2 * narrow, width)
    pair_bias = shaped(F32, 2, 1, width)
    wide_low, wide = shaped(BF16, count, full), shaped(F32, count, full)
    sent2, kept2, dinb_sent, dinb_kept, h2, dy, y_first, dh_first = half_call(
        0,
        hidden_first_kernel,
        (four, four, pair_bias, pair_bias, wide_low, wide_low, wide, wide),
        (meta, x1, *xs, vecs, inb),
        (*g2[0], *g2[1]),
        (),
        "hidden_first",
    )
    arrived2 = wires.swap(sent2) if direct else jnp.zeros_like(sent2)
    sent3, dinb_a, y_first, dh_first = half_call(
        1,
        hidden_a_kernel,
        (four, pair_bias, wide, wide),
        (meta, h2, dy, y_first, dh_first, inb),
        g2[1],
        (),
        "hidden_a",
    )
    arrived3 = wires.swap(sent3) if direct else jnp.zeros_like(sent3)
    arrived2 = after(arrived2, y_first)
    passed2 = add(kept2[2:], arrived2[2:])
    if direct:
        arrived_pass2 = wires.stage(passed2, 1)
    kept3, passed3, dinb_b, *outs, dx1, da, vec_grads = half_call(
        1,
        hidden_b_kernel,
        (two, two, pair_bias) + turn_shapes(count // 2, 2 * narrow) + (wide, wide_low, shaped(F32, 8, full)),
        (meta, x1, after(h2, passed2), dy, y_first, dh_first, vecs, inb, arrived3),
        g2[0],
        (pltpu.VMEM((full, 2 * width), F32), pltpu.VMEM((full, 2 * width), F32)),
        "hidden_b",
    )
    if direct:
        arrived = after(arrived_pass2, da)
        once2 = add(kept2[0], arrived2[0], arrived[0])
        next2 = add(kept2[1], arrived2[1], arrived[1])
        arrived_next2 = wires.stage(next2, 0)
        arrived_pass3 = wires.stage(after(passed3, next2), 1)
        da = after(da, once2, next2)
    dqkv, halves, dwo, dshift, sent1 = call(
        partial(attend_back_kernel, images, rows),
        (
            shaped(BF16, parts, count, 3 * narrow),
            shaped(BF16, parts, 2, count, half),
            shaped(F32, parts, parts, 2, narrow, narrow // 2),
            shaped(F32, parts, 1, 3 * narrow),
            shaped(BF16, 4, 4, narrow, width),
        ),
        (meta, da, mixed, qkv, chances, wo, h1),
        (pltpu.VMEM((parts, count, narrow), BF16), pltpu.VMEM((full, half), F32)),
        "attend_back",
    )
    if direct:
        arrived = after(arrived_pass3, dqkv)
        once3, next3 = add(kept3[0], arrived[0]), add(kept3[1], arrived[1])
        next3, sent1, h1 = after((next3, sent1, h1), once3)
        arrived1 = wires.swap(sent1)
    else:
        arrived1 = jnp.zeros_like(sent1)
    kept1, passed1 = call(
        first_kept_kernel,
        (shaped(BF16, 2, 4, narrow, width),) * 2,
        (meta, h1, halves, dwo, arrived1),
        (pltpu.VMEM((full, half), F32),),
        "first_kept",
    )
    if direct:
        arrived_pass1 = wires.stage(passed1, 1)
        total2 = add(once2, after(arrived_next2, kept1))
        arrived_next3 = wires.stage(next3, 0)
        x0 = after(x0, kept1, total2)
    outs[1] = wires.turn(after(outs[1], kept1))
    *gx, sent_below, kept_below = call(
        first_back_kernel,
        turn_shapes(count // 2, 2 * narrow)
        + (shaped(BF16, 4, 4, VEC_ROWS, width),) * 2,
        (meta, x0, dqkv, wq, dx1, vecs, vec_grads, dshift, dinb_sent, dinb_a, dinb_kept, dinb_b),
        (pltpu.VMEM((8, full), F32),),
        name="first_back",
    )
    gx[1] = wires.turn(gx[1])
    if direct:
        below = add(kept_below, wires.swap(sent_below))
        arrived_below = wires.stage(below[2:], 1)
        total3 = add(once3, after(arrived_next3, gx[0]))
        far = [far_z(total2[1], 1), far_z(total3[0], 2), far_z(total3[1], 3)]
        grad_in, grad_back = call(
            finish_second_kernel,
            (shaped(F32, narrow, width),) * 2,
            (total2[0], *far),
            name="finish_second",
        )
        arrived = after(arrived_pass1, gx[0], outs[1], far[1], gx[1])
        once1, next1 = add(kept1[0], arrived[0]), add(kept1[1], arrived[1])
        arrived_next1 = wires.stage(next1, 0)
        below_next = add(below[1], arrived_below[1])
        below_total = add(below[0], arrived_below[0], wires.stage(below_next, 0))
        total = jnp.concatenate([add(once1, arrived_next1), below_total], 1)
        z_first = wires.over_z([total[s] for s in range(4)], back=True)
        gx[1] = after(gx[1], next1)
    second = wires.turn_again((outs[2], outs[1]), (gx[2], gx[1]))

    output, grad_tokens = call(
        partial(unpack_kernel, images, rows, window),
        (shaped(BF16, narrow, slots), shaped(F32, narrow, slots)),
        (meta, image_counts, *outs[:2], *gx[:2], second),
        (
            pltpu.SMEM((image_counts.shape[0],), jnp.int32),
            pltpu.VMEM((count, window), BF16),
            pltpu.VMEM((narrow, slots), F32),
            pltpu.VMEM((narrow, slots), F32),
        ),
        "unpack",
    )

    if direct:
        line = shaped(F32, narrow)
        grad_qkv, grad_out, grad_in_bias, grad_query, grad_value, *small = call(
            finish_kernel,
            (shaped(F32, narrow, half), shaped(F32, narrow, narrow // 2), shaped(F32, width))
            + (line,) * 8,
            z_first,
            name="finish",
        )
    else:

        def spread(sent, kept, passed):
            later = jnp.concatenate([kept, passed], 0)
            tall = []
            for e in range(parts):
                d = me ^ e
                row = [None] * BLOCKS
                for p, side in ((1, sent), (0, later)):
                    q = jnp.where((d == 0) | (d == 3) | (p == 0), d, 3 - d)
                    four = lax.dynamic_index_in_dim(side, q, 0, False)
                    for s in range(4):
                        row[2 * s + p] = four[s]
                tall.append(jnp.stack(row))
            return jnp.stack(tall).astype(F32)

        def scatter(blocks):
            flat = lax.psum_scatter(blocks, "ea").transpose(1, 0, 2).reshape(narrow, -1)
            return lax.psum_scatter(flat, "ha", scatter_dimension=1, tiled=True)

        sent1 = jnp.concatenate([sent1, sent_below], 2)
        kept1 = jnp.concatenate([kept1, kept_below[:2]], 2)
        passed1 = jnp.concatenate([passed1, kept_below[2:]], 2)
        sent2, kept2 = jnp.concatenate([sent2, sent3], 1), jnp.concatenate([kept2[:2], kept3], 1)
        d2 = spread(sent2, kept2, jnp.concatenate([passed2, passed3], 1))
        d1 = spread(sent1, kept1, passed1)
        grad_in, grad_back = scatter(d2[:, :, :narrow]), scatter(d2[:, :, narrow:])
        grad_qkv, grad_out = scatter(d1[:, :, :narrow, :half]), scatter(d1[:, :, :narrow, half:])
        small = lax.psum(d1[:, :, narrow:], ("ea", "ha"))
        size = in_bias.shape[0]
        grad_in_bias = lax.dynamic_slice_in_dim(small[0, :, 8].reshape(-1), mine * size, size, 0)
        small = lax.dynamic_index_in_dim(small[:, 0], me, 0, False)
        shift = jnp.concatenate([small[6], small[7]])[: 3 * narrow]
        shift = shift.reshape(group_heads, 3, HEAD_DIM)
        grad_query, grad_value = shift[:, 0].reshape(-1), shift[:, 2].reshape(-1)
        small = small[:, :narrow]
    return (
        output,
        grad_tokens,
        small[0],
        small[1],
        grad_qkv,
        grad_query,
        grad_value,
        grad_out,
        small[4],
        small[2],
        small[3],
        grad_in,
        grad_in_bias,
        grad_back.T,
        small[5],
    )


def solution(mesh):
    return jax.shard_map(
        shards,
        mesh=mesh,
        in_specs=(
            P("ea", "ha"),
            P("ha"),
            P("ha", None),
            P("ea"),
            P("ea"),
            P("ea", "ha"),
            P("ea"),
            P("ea"),
            P("ea", "ha"),
            P("ea"),
            P("ea"),
            P("ea"),
            P("ea", "ha"),
            P("ha"),
            P("ha", "ea"),
            P("ea"),
            P("ea", "ha"),
        ),
        out_specs=(
            P("ea", "ha"),
            P("ea", "ha"),
            P("ea"),
            P("ea"),
            P("ea", "ha"),
            P("ea"),
            P("ea"),
            P("ea", "ha"),
            P("ea"),
            P("ea"),
            P("ea"),
            P("ea", "ha"),
            P("ha"),
            P("ha", "ea"),
            P("ea"),
        ),
        check_vma=False,
    )
```

```python
from functools import partial

import jax
import jax.numpy as jnp
from jax import lax
from jax.experimental import pallas as pl
from jax.experimental.pallas import tpu as pltpu
from jax.sharding import PartitionSpec as P

HEAD_DIM = 64
GRID = 14
EPSILON = 1e-06
NEGATIVE = -1e30
BLOCKS = 8
VEC_ROWS = 16
NN = (((1,), (0,)), ((), ()))
NT = (((1,), (1,)), ((), ()))
TN = (((0,), (0,)), ((), ()))
F32 = jnp.float32
BF16 = jnp.bfloat16
SMEM = pl.BlockSpec(memory_space=pltpu.SMEM)
VMEM = pl.BlockSpec(memory_space=pltpu.VMEM)
PARAMS = pltpu.CompilerParams(vmem_limit_bytes=56 * 1024 * 1024)


def dot(a, b, dims):
    return lax.dot_general(a, b, dims, preferred_element_type=F32)


def iota(shape, axis):
    return lax.broadcasted_iota(jnp.int32, shape, axis)


def prefix(counts, starts):
    total = jnp.int32(0)
    for i in range(counts.shape[0]):
        starts[i] = total
        total = total + counts[i]


def select_rows(sel, counts, starts, part, images, rows, window, slots):
    first = starts[part * images]
    base = jnp.minimum(first // 128, (slots - window) // 128) * 128
    base = pl.multiple_of(base, 128)
    row = iota((rows, window), 0)
    gap = iota((rows, window), 1) - row
    for i in range(images):
        image = part * images + i
        hit = (gap == starts[image] - base) & (row < counts[image])
        sel[i * rows : (i + 1) * rows, :] = jnp.where(hit, 1.0, 0.0).astype(BF16)
    return base


def pack_kernel(images, rows, window, meta, counts, tokens, cotangent, *refs):
    (mine, pair, single), (starts, sel) = refs[:3], refs[3:]
    prefix(counts, starts)
    for a in range(4):
        part = meta[0] ^ place(a, meta[2])
        base = select_rows(sel, counts, starts, part, images, rows, window, tokens.shape[1])
        span = pl.ds(base, window)
        both = jnp.concatenate([tokens[:, span], cotangent[:, span]], 0)
        block = dot(sel[...], both, NT).astype(BF16)
        if a in (0, 2):
            (single if a else mine)[...] = block
        else:
            pair[a // 2] = block


def shard_kernel(qkv, out, into, back, hidden_bias, query, value, *refs):
    vectors, (first, second) = refs[:-2], refs[-2:]
    narrow, half = qkv.shape
    width = first.shape[1]
    first[:narrow, :half] = qkv[...]
    first[:narrow, half:] = out[...]
    empty = jnp.zeros((1, width), F32)
    wide = lambda ref: ref[...].astype(F32).reshape(1, -1)
    rows = [jnp.concatenate([wide(ref), empty[:, narrow:]], 1) for ref in vectors]
    query, value = wide(query), wide(value)
    shift = []
    for i in range(narrow // HEAD_DIM):
        at = slice(i * HEAD_DIM, (i + 1) * HEAD_DIM)
        shift += [query[:, at], empty[:, :HEAD_DIM], value[:, at]]
    shift = jnp.concatenate(shift + [empty[:, : 2 * width - 2 * half]], 1)
    rows += [shift[:, :width], shift[:, width:], wide(hidden_bias)]
    rows.append(jnp.zeros((VEC_ROWS - len(rows), width), F32))
    first[narrow:, :] = jnp.concatenate(rows, 0).astype(BF16)
    second[:narrow, :] = into[...]
    second[narrow:, :] = back[...]


def unpack_kernel(images, rows, window, meta, counts, *refs):
    outs, grads, second = refs[:2], refs[2:4], refs[4]
    output, grad, starts, sel, total, grad_total = refs[5:]
    narrow, slots = output.shape
    prefix(counts, starts)
    total[...] = jnp.zeros_like(total)
    grad_total[...] = jnp.zeros_like(grad_total)
    for a in range(4):
        part = meta[0] ^ place(a, meta[2])
        base = select_rows(sel, counts, starts, part, images, rows, window, slots)
        span = pl.ds(base, window)
        for i, (refs, into) in enumerate(((outs, total), (grads, grad_total))):
            pair = refs[0][...] if a == 0 else refs[1][0] if a == 1 else second[2 * i + a - 2]
            tall = jnp.concatenate([pair[:, :narrow], pair[:, narrow:]], 0)
            into[:, span] += dot(tall, sel[...], TN)
    output[...] = total[...].astype(output.dtype)
    grad[...] = grad_total[...]


def store_halves(core, mine, pair, single, values):
    low, narrow = mine.shape[0], mine.shape[1] // 2
    parts = []
    for d in range(4):
        span = slice(d * narrow, (d + 1) * narrow)
        both = [values[:low, span], values[low:, span]]
        parts.append(jnp.concatenate(both, 1).astype(mine.dtype))
    mine[...] = parts[0]
    pair[0] = jnp.where(core == 0, parts[1], parts[2])
    single[...] = jnp.where(core == 0, parts[2], parts[1])
    pair[1] = parts[3]


def turned(core, mine, first, second):
    one, two = first[0], second[0]
    swap = core == 1
    return [mine[...], jnp.where(swap, two, one), jnp.where(swap, one, two), second[1]]


def norm_parts(values):
    center = jnp.mean(values, 1, keepdims=True)
    centred = values - center
    factor = lax.rsqrt(jnp.mean(centred * centred, 1, keepdims=True) + EPSILON)
    return centred * factor, factor


def norm_back(grad, xhat, factor, gain):
    scaled = grad * gain
    mean = jnp.mean(scaled, 1, keepdims=True)
    across = jnp.mean(scaled * xhat, 1, keepdims=True)
    return factor * (scaled - mean - xhat * across)


def colsum(values):
    return jnp.sum(values, 0, keepdims=True)


def place(d, core):
    return d if d in (0, 3) else jnp.where(core == 0, d, 3 - d)


def column_of(meta, p, s):
    return (meta[1] + s) % 4, meta[2] ^ p


def whole_block(refs, rows, swap):
    columns = []
    for s in range(refs[0].shape[0]):
        one, two = refs[1][s, rows], refs[2][s, rows]
        one, two = jnp.where(swap, two, one), jnp.where(swap, one, two)
        columns.append(jnp.concatenate([refs[0][s, rows], one, two, refs[3][s, rows]], 0))
    return jnp.concatenate(columns, 1)


def head_part(qkv, z, span, head, part):
    at = (3 * head + part) * HEAD_DIM
    return qkv[z, span, at : at + HEAD_DIM]


def attend_kernel(images, rows, meta, counts, *refs):
    x_refs, (patches, sines, cosines), arrays = refs[:3], refs[3:6], (refs[6:10], refs[10:14])
    x1_out, x0, h1_out, qkv_out, p_out, o_out, vecs, inb, wq, wo = refs[14:24]
    shifts, wo_parts = refs[24:]
    me = meta[0]
    parts, narrow = wo.shape[0], wo.shape[1]
    wide = 3 * narrow
    half = wide // 2
    outer = narrow // 2
    heads = narrow // HEAD_DIM

    def unfold(core):
        for p in range(2):
            for a in range(parts):
                d = a if a in (0, 3) or (core ^ p) == 0 else 3 - a
                low, high = d * narrow, (d + 1) * narrow
                for s in range(4):
                    z = (meta[1] + s) % 4
                    k = core ^ p
                    ref = arrays[p][a]
                    wq[z, low:high, k * half : (k + 1) * half] = ref[s, :narrow, :half]
                    wo_parts[me ^ d, z, :, k * outer : (k + 1) * outer] = ref[s, :narrow, half:]
                    if a == 0:
                        inb[2 * z + k] = ref[s, narrow:, :].astype(F32)[8:9]
                if p == 0:
                    small = arrays[p][a][0, narrow:, :].astype(F32)
                    vecs[:, low:high] = small[:, :narrow]
                    rest = small[7:8, : wide - small.shape[1]]
                    shifts[me ^ d] = jnp.concatenate([small[6:7], rest], 1)

    pl.when(meta[2] == 0)(partial(unfold, 0))
    pl.when(meta[2] == 1)(partial(unfold, 1))
    for t in range(parts):
        for d in range(parts):
            wo[t, :, d * narrow : (d + 1) * narrow] = wo_parts[t, me ^ d]
    tokens = turned(meta[2], *x_refs)
    for d in range(parts):
        e = me ^ d
        table = jnp.where(e % 2 == 0, sines[...], cosines[...])
        high = table.astype(BF16)
        rest = table - high.astype(F32)
        middle = rest.astype(BF16)
        low = (rest - middle.astype(F32)).astype(BF16)
        stacked = jnp.concatenate([high, middle, low], 0)
        depth = table.shape[0]
        for i in range(images):
            patch = patches[pl.ds(me * images + i, 1), :rows]
            row = (patch * 4682) >> 16
            spot = jnp.where(e < 2, row, patch - row * GRID)
            hot = jnp.where(iota((depth, rows), 0) == spot, 1.0, 0.0).astype(BF16)
            placed = dot(jnp.concatenate([hot, hot, hot], 0), stacked, TN)
            x0[i * rows : (i + 1) * rows, d * narrow : (d + 1) * narrow] = (
                tokens[d][i * rows : (i + 1) * rows, :narrow].astype(F32) + placed
            )
    xhat, _ = norm_parts(x0[...])
    h1 = (xhat * vecs[0:1] + vecs[1:2]).astype(BF16)
    h1_out[...] = h1
    for z in range(parts):
        qkv_out[z] = (dot(h1, wq[z], NN) + shifts[z]).astype(BF16)
    factor = HEAD_DIM ** (-0.5)
    each = [(z, i) for z in range(parts) for i in range(heads)]
    for b in range(images):
        seen = iota((rows, rows), 0) < counts[me * images + b]
        span = slice(b * rows, (b + 1) * rows)
        scores, mixed = [], []
        for z, i in each:
            query, key = (head_part(qkv_out, z, span, i, part) for part in (0, 1))
            scores.append(jnp.where(seen, dot(key, query, NT) * factor, NEGATIVE))
        for n, score in enumerate(scores):
            weights = jnp.exp(score - jnp.max(score, 0, keepdims=True))
            scale = 1.0 / jnp.sum(weights, 0, keepdims=True)
            p_out[n, b] = (weights * scale).astype(BF16)
        for n, (z, i) in enumerate(each):
            value = head_part(qkv_out, z, span, i, 2)
            mixed.append(dot(p_out[n, b], value, TN).astype(BF16))
        for z in range(parts):
            together = jnp.concatenate(mixed[z * heads : (z + 1) * heads], 1)
            o_out[span, z * narrow : (z + 1) * narrow] = together
    attn = dot(o_out[...], jnp.concatenate([wo[z] for z in range(parts)], 0), NN)
    x1_out[...] = x0[...] + attn + vecs[4:5]


def hidden_step(p, meta, h2, dy, inb, refs, first):
    narrow = refs[0].shape[1] // 2
    swap = (meta[2] ^ p) == 1
    w_in = whole_block(refs, slice(0, narrow), swap)
    w_back = whole_block(refs, slice(narrow, 2 * narrow), swap)
    biases = []
    for s in range(refs[0].shape[0]):
        z, k = column_of(meta, p, first + s)
        biases.append(inb[2 * z + k])
    hidden = dot(h2, w_in, NN) + jnp.concatenate(biases, 1)
    gate = 0.5 + 0.5 * lax.erf(hidden * (0.5**0.5))
    active = (hidden * gate).astype(BF16)
    slope = gate + hidden * jnp.exp(-0.5 * hidden * hidden) * 0.3989422804014327
    low = (dot(dy, w_back, NN) * slope).astype(BF16)
    return active, low, dot(active, w_back, NT), dot(low, w_in, NT)


def store_bias(dinb, low):
    total = colsum(low.astype(F32))
    width = dinb.shape[-1]
    for s in range(dinb.shape[0]):
        dinb[s] = total[:, s * width : (s + 1) * width]


def store_blocks(out, core, h2, dy, active, low):
    narrow, width = out.shape[2] // 2, out.shape[3]
    d_in = dot(h2, low, TN).astype(BF16)
    d_back = dot(dy, active, TN).astype(BF16)
    for d in range(4):
        q = place(d, core)
        for s in range(out.shape[1]):
            part = (slice(d * narrow, (d + 1) * narrow), slice(s * width, (s + 1) * width))
            out[q, s, :narrow] = d_in[part]
            out[q, s, narrow:] = d_back[part]


def hidden_first_kernel(meta, *refs):
    x1, y_refs, (vecs, inb), own, other = refs[0], refs[1:4], refs[4:6], refs[6:10], refs[10:14]
    sent, kept, sent_dinb, kept_dinb, h2s, dys, y_total, dh_total = refs[14:]
    narrow = y_refs[0].shape[1] // 2
    for d, part in enumerate(turned(meta[2], *y_refs)):
        dys[:, d * narrow : (d + 1) * narrow] = part[:, narrow:]
    xhat, _ = norm_parts(x1[...])
    h2s[...] = (xhat * vecs[2:3] + vecs[3:4]).astype(BF16)
    h2, dy = h2s[...], dys[...]
    for p, arrays, out, dinb in ((1, other, sent, sent_dinb), (0, own, kept, kept_dinb)):
        active, low, y_part, dh_part = hidden_step(p, meta, h2, dy, inb, arrays, 0)
        y_total[...] = y_part if p else y_total[...] + y_part
        dh_total[...] = dh_part if p else dh_total[...] + dh_part
        store_bias(dinb, low)
        store_blocks(out, meta[2] ^ p, h2, dy, active, low)


def hidden_a_kernel(meta, h2s, dys, y_first, dh_first, inb, *refs):
    arrays = refs[:4]
    sent, dinb, y_total, dh_total = refs[4:]
    h2, dy = h2s[...], dys[...]
    active, low, y_part, dh_part = hidden_step(1, meta, h2, dy, inb, arrays, 2)
    y_total[...] = y_first[...] + y_part
    dh_total[...] = dh_first[...] + dh_part
    store_bias(dinb, low)
    store_blocks(sent, 1 - meta[2], h2, dy, active, low)


def hidden_b_kernel(meta, x1, h2s, dys, y_first, dh_first, vecs, inb, arrived, *refs):
    arrays, (kept, sent, dinb), turn = refs[:4], refs[4:7], refs[7:10]
    dx1, da, vec_grads, d_in, d_back = refs[10:]
    h2, dy = h2s[...], dys[...]
    active, low, y_part, dh_part = hidden_step(0, meta, h2, dy, inb, arrays, 2)
    store_bias(dinb, low)
    narrow, width = kept.shape[2] // 2, kept.shape[3]
    d_in[...] = dot(h2, low, TN)
    d_back[...] = dot(dy, active, TN)
    for q in range(4):
        start = place(q, meta[2]) * narrow
        span = pl.ds(pl.multiple_of(start, narrow) if q in (1, 2) else start, narrow)
        into = kept if q < 2 else sent
        for s in range(2):
            columns = slice(s * width, (s + 1) * width)
            part = d_in[span, columns] + arrived[q, s, :narrow].astype(F32)
            into[q % 2, s, :narrow] = part.astype(BF16)
            part = d_back[span, columns] + arrived[q, s, narrow:].astype(F32)
            into[q % 2, s, narrow:] = part.astype(BF16)
    values = x1[...]
    store_halves(meta[2], *turn, values + y_first[...] + y_part + vecs[5:6])
    xhat, factor = norm_parts(values)
    grad = dh_first[...] + dh_part
    dy_wide = dy.astype(F32)
    total = dy_wide + norm_back(grad, xhat, factor, vecs[2:3])
    dx1[...] = total
    narrowed = total.astype(BF16)
    da[...] = narrowed
    vec_grads[0:1] = colsum(grad * xhat)
    vec_grads[1:2] = colsum(grad)
    vec_grads[2:3] = colsum(narrowed.astype(F32))
    vec_grads[3:4] = colsum(dy_wide)
    vec_grads[4:8] = jnp.zeros_like(vec_grads[4:8])


def attend_back_kernel(images, rows, meta, da, o_ref, qkv, p_ref, wo, h1, *refs):
    dqkv, halves, dwo, dshift, sent, do_ref, dw_ref = refs
    parts, narrow = wo.shape[0], wo.shape[1]
    heads = narrow // HEAD_DIM
    factor = HEAD_DIM ** (-0.5)
    grad = da[...]
    outer = narrow // 2
    for z in range(parts):
        do_ref[z] = dot(grad, wo[z], NT).astype(BF16)
    each = [(z, i) for z in range(parts) for i in range(heads)]
    for b in range(images):
        span = slice(b * rows, (b + 1) * rows)
        grad_heads, grad_scores, grads = [], [], []
        for z, i in each:
            grad_head = do_ref[z, span, i * HEAD_DIM : (i + 1) * HEAD_DIM]
            grad_heads.append(grad_head)
            grad_scores.append(dot(head_part(qkv, z, span, i, 2), grad_head, NT))
        for n in range(len(each)):
            chance = p_ref[n, b].astype(F32)
            inner = jnp.sum(chance * grad_scores[n], 0, keepdims=True)
            grad_scores[n] = (chance * (grad_scores[n] - inner)).astype(BF16)
        for n, (z, i) in enumerate(each):
            query, key = (head_part(qkv, z, span, i, part) for part in (0, 1))
            grads.append((dot(grad_scores[n], key, TN) * factor).astype(BF16))
            grads.append((dot(grad_scores[n], query, NN) * factor).astype(BF16))
            grads.append(dot(p_ref[n, b], grad_heads[n], NN).astype(BF16))
        for z in range(parts):
            together = grads[3 * z * heads : 3 * (z + 1) * heads]
            dqkv[z, span, :] = jnp.concatenate(together, 1)
    half = dqkv.shape[2] // 2
    for z in range(parts):
        dshift[z] = colsum(dqkv[z].astype(F32))
        for k in range(2):
            halves[z, k] = dqkv[z, :, k * half : (k + 1) * half]
        dw = dot(o_ref[:, z * narrow : (z + 1) * narrow], grad, TN)
        for d in range(parts):
            for k in range(2):
                at = d * narrow + k * outer
                dwo[z, d, k] = dw[:, at : at + outer].astype(BF16)

    def store(q, s, block):
        sent[q, s] = block.astype(BF16)

    first_grad(1, meta, h1, halves, dwo, dw_ref, store)


def first_back_kernel(
    meta, x0, dqkv, wq, dx1, vecs, vec_grads, dshift, sent_dinb, sent_rest, kept_dinb, kept_rest, *refs
):
    turn, (sent, kept, rows_out) = refs[:3], refs[3:]
    me = meta[0]
    parts, narrow = dqkv.shape[0], dqkv.shape[2] // 3
    width = sent.shape[3]
    grad = dot(dqkv[0], wq[0], NT)
    for z in range(1, parts):
        grad += dot(dqkv[z], wq[z], NT)
    xhat, factor = norm_parts(x0[...])
    store_halves(meta[2], *turn, dx1[...] + norm_back(grad, xhat, factor, vecs[0:1]))
    rows_out[0:1] = colsum(grad * xhat)
    rows_out[1:2] = colsum(grad)
    rows_out[2:6] = vec_grads[0:4]
    gap = jnp.zeros((6, width - narrow), F32)
    tail = jnp.zeros((VEC_ROWS - 9, width), F32)
    for d in range(parts):
        six = jnp.concatenate([rows_out[0:6, d * narrow : (d + 1) * narrow], gap], 1)
        shift = dshift[me ^ d]
        second = jnp.concatenate([shift[:, width:], gap[0:1, : 2 * width - shift.shape[1]]], 1)
        for s in range(4):
            for p, first, rest, out in (
                (1, sent_dinb, sent_rest, sent),
                (0, kept_dinb, kept_rest, kept),
            ):
                bias = first[s] if s < 2 else rest[s - 2]
                lines = [six, shift[:, :width], second, bias, tail]
                out[place(d, meta[2] ^ p), s] = jnp.concatenate(lines, 0).astype(BF16)


def first_grad(p, meta, h1, halves, dwo, dw, store):
    me = meta[0]
    narrow = dwo.shape[3]
    feature = h1[...]
    for s in range(4):
        z, k = column_of(meta, p, s)
        dw[...] = dot(feature, halves[z, k], TN)
        for q in range(4):
            d = place(q, meta[2] ^ p)
            start = d * narrow
            span = pl.ds(pl.multiple_of(start, narrow) if q in (1, 2) else start, narrow)
            store(q, s, jnp.concatenate([dw[span, :], dwo[me ^ d, z ^ me, k].astype(F32)], 1))


def first_kept_kernel(meta, h1, halves, dwo, arrived, kept, sent, dw):
    def store(q, s, block):
        into = kept if q < 2 else sent
        into[q % 2, s] = (block + arrived[q, s].astype(F32)).astype(BF16)

    first_grad(0, meta, h1, halves, dwo, dw, store)


def finish_second_kernel(*refs):
    pieces, (d_in, d_back) = refs[:4], refs[4:]
    narrow = d_in.shape[0]
    for rows, out in ((slice(0, narrow), d_in), (slice(narrow, 2 * narrow), d_back)):
        total = pieces[0][rows].astype(F32)
        for piece in pieces[1:]:
            total += piece[rows].astype(F32)
        out[...] = total


def finish_kernel(*refs):
    pieces, (qkv, out, hidden_bias, query, value), vectors = refs[:4], refs[4:9], refs[9:]
    narrow, half = qkv.shape
    total = pieces[0][...].astype(F32)
    for piece in pieces[1:]:
        total += piece[...].astype(F32)
    qkv[...] = total[:narrow, :half]
    out[...] = total[:narrow, half:]
    for i, ref in enumerate(vectors):
        ref[...] = total[narrow + i : narrow + i + 1, :narrow].reshape(ref.shape)
    shift = jnp.concatenate([total[narrow + 6 : narrow + 7], total[narrow + 7 : narrow + 8]], 1)
    heads = range(narrow // HEAD_DIM)
    for ref, part in ((query, 0), (value, 2)):
        pieces = [shift[:, (3 * i + part) * HEAD_DIM :][:, :HEAD_DIM] for i in heads]
        ref[...] = jnp.concatenate(pieces, 1).reshape(ref.shape)
    hidden_bias[...] = total[narrow + 8 : narrow + 9].reshape(hidden_bias.shape)


def call(kernel, outs, operands, scratch=(), name=None):
    specs = []
    for value in operands:
        specs.append(SMEM if value.dtype == jnp.int32 and value.ndim == 1 else VMEM)
    return pl.pallas_call(
        kernel,
        out_shape=outs,
        in_specs=specs,
        out_specs=jax.tree.map(lambda _: VMEM, outs),
        scratch_shapes=scratch,
        compiler_params=PARAMS,
        name=name,
    )(*operands)


def shaped(dtype, *shape):
    return jax.ShapeDtypeStruct(shape, dtype)


def exchange(block, d):
    size = lax.axis_size("ea")
    return block if d == 0 else lax.ppermute(block, "ea", [(e, e ^ d) for e in range(size)])


class Wires:
    def __init__(self, parts, columns):
        self.parts, self.chips = parts, columns // 2

    def over_z(self, blocks, back=False, slots=(1, 2, 3)):
        pulled = [blocks[0]]
        for s in slots:
            pairs = []
            for h in range(2 * self.chips):
                far = (h + 2 * s) % (2 * self.chips)
                pairs.append((h, far) if back else (far, h))
            pulled.append(lax.ppermute(blocks[s], "ha", pairs))
        return pulled

    def turn(self, pair):
        if 2 * self.chips == BLOCKS:
            return self.stage(pair, 0)
        one = exchange(pair[0], 1)
        return jnp.stack([one, exchange(pair[1], 1)])

    def turn_again(self, *pairs):
        both = jnp.stack([block for single, first in pairs for block in (single, first[1])])
        return self.stage(both, 1) if 2 * self.chips == BLOCKS else exchange(both, 2)

    def swap(self, block):
        return lax.ppermute(block, "ha", [(h, h ^ 1) for h in range(2 * self.chips)])

    def stage(self, block, second):
        pairs = []
        columns = 2 * self.chips
        for e in range(self.parts):
            for h in range(columns):
                d = 1 + ((h % 2) ^ second)
                pairs.append((e * columns + h, (e ^ d) * columns + h))
        return lax.ppermute(block, ("ea", "ha"), pairs)

    def spread(self, mine, behind=(), swap_behind=(), one=None):
        one = self.stage(mine, 0) if one is None else one
        two = self.stage(mine, 1)
        mine, one, two = after((mine, one, two), *behind)
        three = self.stage(one, 1)
        mine, one, two = after((mine, one, two), *swap_behind)
        own = (mine, one, two, three)
        return own, tuple(self.swap(block) for block in own)


def after(value, *others):
    return lax.optimization_barrier((value, others))[0]


def add(*terms):
    return sum(term.astype(F32) for term in terms).astype(BF16)


def vector_rows(vectors, shift, bias):
    width = bias.shape[-1]
    rows = [jnp.pad(v, (0, width - v.shape[0])) for v in vectors]
    rows += [shift[:width], jnp.pad(shift[width:], (0, 2 * width - shift.shape[0])), bias]
    return jnp.stack(rows + [jnp.zeros_like(bias)] * (VEC_ROWS - len(rows)))


def half_call(half, kernel, outs, operands, arrays, scratch, name):
    block = pl.BlockSpec((2, *arrays[0].shape[1:]), lambda i: (half, 0, 0))
    return pl.pallas_call(
        kernel,
        grid=(1,),
        out_shape=outs,
        in_specs=[SMEM] + [whole_spec(*v.shape) for v in operands[1:]] + [block] * len(arrays),
        out_specs=jax.tree.map(lambda out: whole_spec(*out.shape), outs),
        scratch_shapes=scratch,
        compiler_params=PARAMS,
        name=name,
    )(*operands, *arrays)


def whole_spec(*shape):
    return pl.BlockSpec(shape, lambda i: (0,) * len(shape))


def shards(
    tokens,
    image_counts,
    kept_patches,
    norm1_gain,
    norm1_bias,
    qkv_weight,
    query_bias,
    value_bias,
    out_weight,
    out_bias,
    norm2_gain,
    norm2_bias,
    in_weight,
    in_bias,
    back_weight,
    back_bias,
    cotangent,
):
    parts = lax.axis_size("ea")
    columns = lax.axis_size("ha")
    me = lax.axis_index("ea")
    mine = lax.axis_index("ha")
    direct = columns == BLOCKS
    wires = Wires(parts, columns)
    if direct:
        meta = jnp.stack([me, mine // 2, mine % 2]).astype(jnp.int32)
    else:
        meta = jnp.stack([me, 0 * mine, 0 * mine]).astype(jnp.int32)
    narrow, slots = tokens.shape
    full = narrow * parts
    images = image_counts.shape[0] // parts
    most = kept_patches.shape[1]
    rows = -(-most // 16) * 16
    count = images * rows
    window = min(slots, (images * most + 127 + 127) // 128 * 128)
    heads = full // HEAD_DIM
    group_heads = narrow // HEAD_DIM
    width = in_weight.shape[1] * columns // BLOCKS
    half = 3 * narrow // 2

    vectors = (norm1_gain, norm1_bias, norm2_gain, norm2_bias, out_bias, back_bias)
    if direct:
        first, second = call(
            shard_kernel,
            (shaped(BF16, narrow + VEC_ROWS, width), shaped(BF16, 2 * narrow, width)),
            (qkv_weight, out_weight, in_weight, back_weight.T, in_bias, query_bias, value_bias)
            + vectors,
            name="shard",
        )

    turn_shapes = lambda r, c: (shaped(BF16, r, c), shaped(BF16, 2, r, c), shaped(BF16, r, c))
    packed = call(
        partial(pack_kernel, images, rows, window),
        turn_shapes(count, 2 * narrow),
        (meta, image_counts, tokens, cotangent),
        (pltpu.SMEM((image_counts.shape[0],), jnp.int32), pltpu.VMEM((count, window), BF16)),
        "pack",
    )

    if direct:
        turned_once = wires.turn(packed[1])
        z_first = wires.over_z([first] * 4)
        turned_once = after(turned_once, *z_first[1:])
        xs = (packed[0], turned_once, wires.turn_again((packed[2], turned_once)))
        z_second = wires.over_z([after(second, *z_first)] * 4)
        g1 = wires.spread(jnp.stack(z_first), (), z_second)
        z_second = jnp.stack(after(z_second, g1[0][1]))
        xs = after(xs, z_second)
    else:
        turned_once = wires.turn(packed[1])
        xs = (packed[0], turned_once, wires.turn_again((packed[2], turned_once)))
        pairs = jnp.zeros((group_heads, HEAD_DIM), BF16)
        by_head = lambda bias: bias.reshape(group_heads, HEAD_DIM)
        shift = jnp.stack([by_head(query_bias), pairs, by_head(value_bias)], 1).reshape(-1)

        def whole(weight):
            wide = lax.all_gather(weight, "ha", axis=1, tiled=True)
            blocks = wide.reshape(narrow, BLOCKS, -1).transpose(1, 0, 2)
            return lax.all_gather(blocks, "ea")

        def arrange(blocks):
            sides = []
            for p in range(2):
                side = []
                for a in range(parts):
                    d = a if p == 0 or a in (0, 3) else 3 - a
                    row = lax.dynamic_index_in_dim(blocks, me ^ d, 0, False)
                    side.append(jnp.stack([row[2 * s + p] for s in range(4)]))
                sides.append(tuple(side))
            return sides

        biases = lax.all_gather(in_bias, "ha", tiled=True).reshape(BLOCKS, -1)
        below = jax.vmap(lambda bias: vector_rows(vectors, shift, bias))(biases)
        g1 = jnp.concatenate([whole(qkv_weight), whole(out_weight)], 3)
        g1 = jnp.concatenate([g1, lax.all_gather(below, "ea")], 2)
        g1 = arrange(g1)
        g2 = arrange(jnp.concatenate([whole(in_weight), whole(back_weight.T)], 2))

    omega = 1.0 / 10000.0 ** (jnp.arange(narrow, dtype=F32) / narrow)
    angles = jnp.arange(16, dtype=F32)[:, None] * omega[None, :]
    patches = jnp.pad(kept_patches, ((0, 0), (0, 128 - most)))

    x1, x0, h1, qkv, chances, mixed, vecs, inb, wq, wo = call(
        partial(attend_kernel, images, rows),
        (
            shaped(F32, count, full),
            shaped(F32, count, full),
            shaped(BF16, count, full),
            shaped(BF16, parts, count, 3 * narrow),
            shaped(BF16, heads, images, rows, rows),
            shaped(BF16, count, full),
            shaped(F32, VEC_ROWS, full),
            shaped(F32, BLOCKS, 1, width),
            shaped(BF16, parts, full, 3 * narrow),
            shaped(BF16, parts, narrow, full),
        ),
        (meta, image_counts, *xs, patches, jnp.sin(angles), jnp.cos(angles), *g1[0], *g1[1]),
        (
            pltpu.VMEM((parts, 1, 3 * narrow), F32),
            pltpu.VMEM((parts, parts, narrow, narrow), BF16),
        ),
        "attend",
    )

    if direct:
        g2 = wires.spread(z_second, (x1,))
    far_z = lambda block, s: wires.over_z([block] * 4, True, (s,))[1]
    four = shaped(BF16, 4, 2, 2 * narrow, width)
    two = shaped(BF16, 2, 2, 2 * narrow, width)
    pair_bias = shaped(F32, 2, 1, width)
    wide_low, wide = shaped(BF16, count, full), shaped(F32, count, full)
    sent2, kept2, dinb_sent, dinb_kept, h2, dy, y_first, dh_first = half_call(
        0,
        hidden_first_kernel,
        (four, four, pair_bias, pair_bias, wide_low, wide_low, wide, wide),
        (meta, x1, *xs, vecs, inb),
        (*g2[0], *g2[1]),
        (),
        "hidden_first",
    )
    arrived2 = wires.swap(sent2) if direct else jnp.zeros_like(sent2)
    sent3, dinb_a, y_first, dh_first = half_call(
        1,
        hidden_a_kernel,
        (four, pair_bias, wide, wide),
        (meta, h2, dy, y_first, dh_first, inb),
        g2[1],
        (),
        "hidden_a",
    )
    arrived3 = wires.swap(sent3) if direct else jnp.zeros_like(sent3)
    arrived2 = after(arrived2, y_first)
    passed2 = add(kept2[2:], arrived2[2:])
    if direct:
        arrived_pass2 = wires.stage(passed2, 1)
    kept3, passed3, dinb_b, *outs, dx1, da, vec_grads = half_call(
        1,
        hidden_b_kernel,
        (two, two, pair_bias) + turn_shapes(count // 2, 2 * narrow) + (wide, wide_low, shaped(F32, 8, full)),
        (meta, x1, after(h2, passed2), dy, y_first, dh_first, vecs, inb, arrived3),
        g2[0],
        (pltpu.VMEM((full, 2 * width), F32), pltpu.VMEM((full, 2 * width), F32)),
        "hidden_b",
    )
    if direct:
        arrived = after(arrived_pass2, da)
        once2 = add(kept2[0], arrived2[0], arrived[0])
        next2 = add(kept2[1], arrived2[1], arrived[1])
        arrived_next2 = wires.stage(next2, 0)
        arrived_pass3 = wires.stage(after(passed3, next2), 1)
        da = after(da, once2, next2)
    dqkv, halves, dwo, dshift, sent1 = call(
        partial(attend_back_kernel, images, rows),
        (
            shaped(BF16, parts, count, 3 * narrow),
            shaped(BF16, parts, 2, count, half),
            shaped(BF16, parts, parts, 2, narrow, narrow // 2),
            shaped(F32, parts, 1, 3 * narrow),
            shaped(BF16, 4, 4, narrow, width),
        ),
        (meta, da, mixed, qkv, chances, wo, h1),
        (pltpu.VMEM((parts, count, narrow), BF16), pltpu.VMEM((full, half), F32)),
        "attend_back",
    )
    if direct:
        arrived = after(arrived_pass3, dqkv)
        once3, next3 = add(kept3[0], arrived[0]), add(kept3[1], arrived[1])
        next3, sent1, h1 = after((next3, sent1, h1), once3)
        arrived1 = wires.swap(sent1)
    else:
        arrived1 = jnp.zeros_like(sent1)
    kept1, passed1 = call(
        first_kept_kernel,
        (shaped(BF16, 2, 4, narrow, width),) * 2,
        (meta, h1, halves, dwo, arrived1),
        (pltpu.VMEM((full, half), F32),),
        "first_kept",
    )
    if direct:
        arrived_pass1 = wires.stage(passed1, 1)
        total2 = add(once2, after(arrived_next2, kept1))
        arrived_next3 = wires.stage(next3, 0)
        x0 = after(x0, kept1, total2)
    outs[1] = wires.turn(after(outs[1], kept1))
    *gx, sent_below, kept_below = call(
        first_back_kernel,
        turn_shapes(count // 2, 2 * narrow)
        + (shaped(BF16, 4, 4, VEC_ROWS, width),) * 2,
        (meta, x0, dqkv, wq, dx1, vecs, vec_grads, dshift, dinb_sent, dinb_a, dinb_kept, dinb_b),
        (pltpu.VMEM((8, full), F32),),
        name="first_back",
    )
    gx[1] = wires.turn(gx[1])
    if direct:
        below = add(kept_below, wires.swap(sent_below))
        arrived_below = wires.stage(below[2:], 1)
        total3 = add(once3, after(arrived_next3, gx[0]))
        far = [far_z(total2[1], 1), far_z(total3[0], 2), far_z(total3[1], 3)]
        grad_in, grad_back = call(
            finish_second_kernel,
            (shaped(F32, narrow, width),) * 2,
            (total2[0], *far),
            name="finish_second",
        )
        arrived = after(arrived_pass1, gx[0], outs[1], far[1], gx[1])
        once1, next1 = add(kept1[0], arrived[0]), add(kept1[1], arrived[1])
        arrived_next1 = wires.stage(next1, 0)
        below_next = add(below[1], arrived_below[1])
        below_total = add(below[0], arrived_below[0], wires.stage(below_next, 0))
        total = jnp.concatenate([add(once1, arrived_next1), below_total], 1)
        z_first = wires.over_z([total[s] for s in range(4)], back=True)
        gx[1] = after(gx[1], next1)
    second = wires.turn_again((outs[2], outs[1]), (gx[2], gx[1]))

    output, grad_tokens = call(
        partial(unpack_kernel, images, rows, window),
        (shaped(BF16, narrow, slots), shaped(F32, narrow, slots)),
        (meta, image_counts, *outs[:2], *gx[:2], second),
        (
            pltpu.SMEM((image_counts.shape[0],), jnp.int32),
            pltpu.VMEM((count, window), BF16),
            pltpu.VMEM((narrow, slots), F32),
            pltpu.VMEM((narrow, slots), F32),
        ),
        "unpack",
    )

    if direct:
        line = shaped(F32, narrow)
        grad_qkv, grad_out, grad_in_bias, grad_query, grad_value, *small = call(
            finish_kernel,
            (shaped(F32, narrow, half), shaped(F32, narrow, narrow // 2), shaped(F32, width))
            + (line,) * 8,
            z_first,
            name="finish",
        )
    else:

        def spread(sent, kept, passed):
            later = jnp.concatenate([kept, passed], 0)
            tall = []
            for e in range(parts):
                d = me ^ e
                row = [None] * BLOCKS
                for p, side in ((1, sent), (0, later)):
                    q = jnp.where((d == 0) | (d == 3) | (p == 0), d, 3 - d)
                    four = lax.dynamic_index_in_dim(side, q, 0, False)
                    for s in range(4):
                        row[2 * s + p] = four[s]
                tall.append(jnp.stack(row))
            return jnp.stack(tall).astype(F32)

        def scatter(blocks):
            flat = lax.psum_scatter(blocks, "ea").transpose(1, 0, 2).reshape(narrow, -1)
            return lax.psum_scatter(flat, "ha", scatter_dimension=1, tiled=True)

        sent1 = jnp.concatenate([sent1, sent_below], 2)
        kept1 = jnp.concatenate([kept1, kept_below[:2]], 2)
        passed1 = jnp.concatenate([passed1, kept_below[2:]], 2)
        sent2, kept2 = jnp.concatenate([sent2, sent3], 1), jnp.concatenate([kept2[:2], kept3], 1)
        d2 = spread(sent2, kept2, jnp.concatenate([passed2, passed3], 1))
        d1 = spread(sent1, kept1, passed1)
        grad_in, grad_back = scatter(d2[:, :, :narrow]), scatter(d2[:, :, narrow:])
        grad_qkv, grad_out = scatter(d1[:, :, :narrow, :half]), scatter(d1[:, :, :narrow, half:])
        small = lax.psum(d1[:, :, narrow:], ("ea", "ha"))
        size = in_bias.shape[0]
        grad_in_bias = lax.dynamic_slice_in_dim(small[0, :, 8].reshape(-1), mine * size, size, 0)
        small = lax.dynamic_index_in_dim(small[:, 0], me, 0, False)
        shift = jnp.concatenate([small[6], small[7]])[: 3 * narrow]
        shift = shift.reshape(group_heads, 3, HEAD_DIM)
        grad_query, grad_value = shift[:, 0].reshape(-1), shift[:, 2].reshape(-1)
        small = small[:, :narrow]
    return (
        output,
        grad_tokens,
        small[0],
        small[1],
        grad_qkv,
        grad_query,
        grad_value,
        grad_out,
        small[4],
        small[2],
        small[3],
        grad_in,
        grad_in_bias,
        grad_back.T,
        small[5],
    )


def solution(mesh):
    return jax.shard_map(
        shards,
        mesh=mesh,
        in_specs=(
            P("ea", "ha"),
            P("ha"),
            P("ha", None),
            P("ea"),
            P("ea"),
            P("ea", "ha"),
            P("ea"),
            P("ea"),
            P("ea", "ha"),
            P("ea"),
            P("ea"),
            P("ea"),
            P("ea", "ha"),
            P("ha"),
            P("ha", "ea"),
            P("ea"),
            P("ea", "ha"),
        ),
        out_specs=(
            P("ea", "ha"),
            P("ea", "ha"),
            P("ea"),
            P("ea"),
            P("ea", "ha"),
            P("ea"),
            P("ea"),
            P("ea", "ha"),
            P("ea"),
            P("ea"),
            P("ea"),
            P("ea", "ha"),
            P("ha"),
            P("ha", "ea"),
            P("ea"),
        ),
        check_vma=False,
    )
```

```python
from functools import partial

import jax
import jax.numpy as jnp
from jax import lax
from jax.experimental import pallas as pl
from jax.experimental.pallas import tpu as pltpu
from jax.sharding import PartitionSpec as P

HEAD_DIM = 64
GRID = 14
EPSILON = 1e-06
NEGATIVE = -1e30
BLOCKS = 8
VEC_ROWS = 16
NN = (((1,), (0,)), ((), ()))
NT = (((1,), (1,)), ((), ()))
TN = (((0,), (0,)), ((), ()))
F32 = jnp.float32
BF16 = jnp.bfloat16
SMEM = pl.BlockSpec(memory_space=pltpu.SMEM)
VMEM = pl.BlockSpec(memory_space=pltpu.VMEM)
PARAMS = pltpu.CompilerParams(vmem_limit_bytes=56 * 1024 * 1024)


def dot(a, b, dims):
    return lax.dot_general(a, b, dims, preferred_element_type=F32)


def iota(shape, axis):
    return lax.broadcasted_iota(jnp.int32, shape, axis)


def prefix(counts, starts):
    total = jnp.int32(0)
    for i in range(counts.shape[0]):
        starts[i] = total
        total = total + counts[i]


def select_rows(sel, counts, starts, part, images, rows, window, slots):
    first = starts[part * images]
    base = jnp.minimum(first // 128, (slots - window) // 128) * 128
    base = pl.multiple_of(base, 128)
    row = iota((rows, window), 0)
    gap = iota((rows, window), 1) - row
    for i in range(images):
        image = part * images + i
        hit = (gap == starts[image] - base) & (row < counts[image])
        sel[i * rows : (i + 1) * rows, :] = jnp.where(hit, 1.0, 0.0).astype(BF16)
    return base


def pack_kernel(images, rows, window, meta, counts, tokens, cotangent, *refs):
    (mine, pair, single), (starts, sel) = refs[:3], refs[3:]
    prefix(counts, starts)
    for a in range(4):
        part = meta[0] ^ place(a, meta[2])
        base = select_rows(sel, counts, starts, part, images, rows, window, tokens.shape[1])
        span = pl.ds(base, window)
        both = jnp.concatenate([tokens[:, span], cotangent[:, span]], 0)
        block = dot(sel[...], both, NT).astype(BF16)
        if a in (0, 2):
            (single if a else mine)[...] = block
        else:
            pair[a // 2] = block


def shard_kernel(qkv, out, into, back, hidden_bias, query, value, *refs):
    vectors, (first, second) = refs[:-2], refs[-2:]
    narrow, half = qkv.shape
    width = first.shape[1]
    first[:narrow, :half] = qkv[...]
    first[:narrow, half:] = out[...]
    empty = jnp.zeros((1, width), F32)
    wide = lambda ref: ref[...].astype(F32).reshape(1, -1)
    rows = [jnp.concatenate([wide(ref), empty[:, narrow:]], 1) for ref in vectors]
    query, value = wide(query), wide(value)
    shift = []
    for i in range(narrow // HEAD_DIM):
        at = slice(i * HEAD_DIM, (i + 1) * HEAD_DIM)
        shift += [query[:, at], empty[:, :HEAD_DIM], value[:, at]]
    shift = jnp.concatenate(shift + [empty[:, : 2 * width - 2 * half]], 1)
    rows += [shift[:, :width], shift[:, width:], wide(hidden_bias)]
    rows.append(jnp.zeros((VEC_ROWS - len(rows), width), F32))
    first[narrow:, :] = jnp.concatenate(rows, 0).astype(BF16)
    second[:narrow, :] = into[...]
    second[narrow:, :] = back[...]


def unpack_kernel(images, rows, window, meta, counts, *refs):
    outs, grads, second = refs[:2], refs[2:4], refs[4]
    output, grad, starts, sel, total, grad_total = refs[5:]
    narrow, slots = output.shape
    prefix(counts, starts)
    total[...] = jnp.zeros_like(total)
    grad_total[...] = jnp.zeros_like(grad_total)
    for a in range(4):
        part = meta[0] ^ place(a, meta[2])
        base = select_rows(sel, counts, starts, part, images, rows, window, slots)
        span = pl.ds(base, window)
        for i, (refs, into) in enumerate(((outs, total), (grads, grad_total))):
            pair = refs[0][...] if a == 0 else refs[1][0] if a == 1 else second[2 * i + a - 2]
            tall = jnp.concatenate([pair[:, :narrow], pair[:, narrow:]], 0)
            into[:, span] += dot(tall, sel[...], TN)
    output[...] = total[...].astype(output.dtype)
    grad[...] = grad_total[...]


def store_halves(core, mine, pair, single, values):
    low, narrow = mine.shape[0], mine.shape[1] // 2
    parts = []
    for d in range(4):
        span = slice(d * narrow, (d + 1) * narrow)
        both = [values[:low, span], values[low:, span]]
        parts.append(jnp.concatenate(both, 1).astype(mine.dtype))
    mine[...] = parts[0]
    pair[0] = jnp.where(core == 0, parts[1], parts[2])
    single[...] = jnp.where(core == 0, parts[2], parts[1])
    pair[1] = parts[3]


def turned(core, mine, first, second):
    one, two = first[0], second[0]
    swap = core == 1
    return [mine[...], jnp.where(swap, two, one), jnp.where(swap, one, two), second[1]]


def norm_parts(values):
    center = jnp.mean(values, 1, keepdims=True)
    centred = values - center
    factor = lax.rsqrt(jnp.mean(centred * centred, 1, keepdims=True) + EPSILON)
    return centred * factor, factor


def norm_back(grad, xhat, factor, gain):
    scaled = grad * gain
    mean = jnp.mean(scaled, 1, keepdims=True)
    across = jnp.mean(scaled * xhat, 1, keepdims=True)
    return factor * (scaled - mean - xhat * across)


def colsum(values):
    return jnp.sum(values, 0, keepdims=True)


def place(d, core):
    return d if d in (0, 3) else jnp.where(core == 0, d, 3 - d)


def column_of(meta, p, s):
    return (meta[1] + s) % 4, meta[2] ^ p


def whole_block(refs, rows, swap):
    columns = []
    for s in range(refs[0].shape[0]):
        one, two = refs[1][s, rows], refs[2][s, rows]
        one, two = jnp.where(swap, two, one), jnp.where(swap, one, two)
        columns.append(jnp.concatenate([refs[0][s, rows], one, two, refs[3][s, rows]], 0))
    return jnp.concatenate(columns, 1)


def head_part(qkv, z, span, head, part):
    at = (3 * head + part) * HEAD_DIM
    return qkv[z, span, at : at + HEAD_DIM]


def attend_kernel(images, rows, meta, counts, *refs):
    x_refs, (patches, sines, cosines), arrays = refs[:3], refs[3:6], (refs[6:10], refs[10:14])
    x1_out, x0, h1_out, qkv_out, p_out, o_out, vecs, inb, wq, wo = refs[14:24]
    shifts, wo_parts = refs[24:]
    me = meta[0]
    parts, narrow = wo.shape[0], wo.shape[1]
    wide = 3 * narrow
    half = wide // 2
    outer = narrow // 2
    heads = narrow // HEAD_DIM

    def unfold(core):
        for p in range(2):
            for a in range(parts):
                d = a if a in (0, 3) or (core ^ p) == 0 else 3 - a
                low, high = d * narrow, (d + 1) * narrow
                for s in range(4):
                    z = (meta[1] + s) % 4
                    k = core ^ p
                    ref = arrays[p][a]
                    wq[z, low:high, k * half : (k + 1) * half] = ref[s, :narrow, :half]
                    wo_parts[me ^ d, z, :, k * outer : (k + 1) * outer] = ref[s, :narrow, half:]
                    if a == 0:
                        inb[2 * z + k] = ref[s, narrow:, :].astype(F32)[8:9]
                if p == 0:
                    small = arrays[p][a][0, narrow:, :].astype(F32)
                    vecs[:, low:high] = small[:, :narrow]
                    rest = small[7:8, : wide - small.shape[1]]
                    shifts[me ^ d] = jnp.concatenate([small[6:7], rest], 1)

    pl.when(meta[2] == 0)(partial(unfold, 0))
    pl.when(meta[2] == 1)(partial(unfold, 1))
    for t in range(parts):
        for d in range(parts):
            wo[t, :, d * narrow : (d + 1) * narrow] = wo_parts[t, me ^ d]
    tokens = turned(meta[2], *x_refs)
    for d in range(parts):
        e = me ^ d
        table = jnp.where(e % 2 == 0, sines[...], cosines[...])
        high = table.astype(BF16)
        rest = table - high.astype(F32)
        middle = rest.astype(BF16)
        low = (rest - middle.astype(F32)).astype(BF16)
        stacked = jnp.concatenate([high, middle, low], 0)
        depth = table.shape[0]
        for i in range(images):
            patch = patches[pl.ds(me * images + i, 1), :rows]
            row = (patch * 4682) >> 16
            spot = jnp.where(e < 2, row, patch - row * GRID)
            hot = jnp.where(iota((depth, rows), 0) == spot, 1.0, 0.0).astype(BF16)
            placed = dot(jnp.concatenate([hot, hot, hot], 0), stacked, TN)
            x0[i * rows : (i + 1) * rows, d * narrow : (d + 1) * narrow] = (
                tokens[d][i * rows : (i + 1) * rows, :narrow].astype(F32) + placed
            )
    xhat, _ = norm_parts(x0[...])
    h1 = (xhat * vecs[0:1] + vecs[1:2]).astype(BF16)
    h1_out[...] = h1
    for z in range(parts):
        qkv_out[z] = (dot(h1, wq[z], NN) + shifts[z]).astype(BF16)
    factor = HEAD_DIM ** (-0.5)
    each = [(z, i) for z in range(parts) for i in range(heads)]
    for b in range(images):
        seen = iota((rows, rows), 0) < counts[me * images + b]
        span = slice(b * rows, (b + 1) * rows)
        scores, mixed = [], []
        for z, i in each:
            query, key = (head_part(qkv_out, z, span, i, part) for part in (0, 1))
            scores.append(jnp.where(seen, dot(key, query, NT) * factor, NEGATIVE))
        for n, score in enumerate(scores):
            weights = jnp.exp(score - jnp.max(score, 0, keepdims=True))
            scale = 1.0 / jnp.sum(weights, 0, keepdims=True)
            p_out[n, b] = (weights * scale).astype(BF16)
        for n, (z, i) in enumerate(each):
            value = head_part(qkv_out, z, span, i, 2)
            mixed.append(dot(p_out[n, b], value, TN).astype(BF16))
        for z in range(parts):
            together = jnp.concatenate(mixed[z * heads : (z + 1) * heads], 1)
            o_out[span, z * narrow : (z + 1) * narrow] = together
    attn = dot(o_out[...], jnp.concatenate([wo[z] for z in range(parts)], 0), NN)
    x1_out[...] = x0[...] + attn + vecs[4:5]


def hidden_step(p, meta, h2, dy, inb, refs, first):
    narrow = refs[0].shape[1] // 2
    swap = (meta[2] ^ p) == 1
    w_in = whole_block(refs, slice(0, narrow), swap)
    w_back = whole_block(refs, slice(narrow, 2 * narrow), swap)
    biases = []
    for s in range(refs[0].shape[0]):
        z, k = column_of(meta, p, first + s)
        biases.append(inb[2 * z + k])
    hidden = dot(h2, w_in, NN) + jnp.concatenate(biases, 1)
    gate = 0.5 + 0.5 * lax.erf(hidden * (0.5**0.5))
    active = (hidden * gate).astype(BF16)
    slope = gate + hidden * jnp.exp(-0.5 * hidden * hidden) * 0.3989422804014327
    low = (dot(dy, w_back, NN) * slope).astype(BF16)
    return active, low, dot(active, w_back, NT), dot(low, w_in, NT)


def store_bias(dinb, low):
    total = colsum(low.astype(F32))
    width = dinb.shape[-1]
    for s in range(dinb.shape[0]):
        dinb[s] = total[:, s * width : (s + 1) * width]


def store_blocks(out, core, h2, dy, active, low):
    narrow, width = out.shape[2] // 2, out.shape[3]
    d_in = dot(h2, low, TN).astype(BF16)
    d_back = dot(dy, active, TN).astype(BF16)
    for d in range(4):
        q = place(d, core)
        for s in range(out.shape[1]):
            part = (slice(d * narrow, (d + 1) * narrow), slice(s * width, (s + 1) * width))
            out[q, s, :narrow] = d_in[part]
            out[q, s, narrow:] = d_back[part]


def hidden_first_kernel(meta, *refs):
    x1, y_refs, (vecs, inb), own, other = refs[0], refs[1:4], refs[4:6], refs[6:10], refs[10:14]
    sent, kept, sent_dinb, kept_dinb, h2s, dys, y_total, dh_total = refs[14:]
    narrow = y_refs[0].shape[1] // 2
    for d, part in enumerate(turned(meta[2], *y_refs)):
        dys[:, d * narrow : (d + 1) * narrow] = part[:, narrow:]
    xhat, _ = norm_parts(x1[...])
    h2s[...] = (xhat * vecs[2:3] + vecs[3:4]).astype(BF16)
    h2, dy = h2s[...], dys[...]
    for p, arrays, out, dinb in ((1, other, sent, sent_dinb), (0, own, kept, kept_dinb)):
        active, low, y_part, dh_part = hidden_step(p, meta, h2, dy, inb, arrays, 0)
        y_total[...] = y_part if p else y_total[...] + y_part
        dh_total[...] = dh_part if p else dh_total[...] + dh_part
        store_bias(dinb, low)
        store_blocks(out, meta[2] ^ p, h2, dy, active, low)


def hidden_a_kernel(meta, h2s, dys, y_first, dh_first, inb, *refs):
    arrays = refs[:4]
    sent, dinb, y_total, dh_total = refs[4:]
    h2, dy = h2s[...], dys[...]
    active, low, y_part, dh_part = hidden_step(1, meta, h2, dy, inb, arrays, 2)
    y_total[...] = y_first[...] + y_part
    dh_total[...] = dh_first[...] + dh_part
    store_bias(dinb, low)
    store_blocks(sent, 1 - meta[2], h2, dy, active, low)


def hidden_b_kernel(meta, x1, h2s, dys, y_first, dh_first, vecs, inb, arrived, *refs):
    arrays, (kept, sent, dinb), turn = refs[:4], refs[4:7], refs[7:10]
    dx1, da, vec_grads, d_in, d_back = refs[10:]
    h2, dy = h2s[...], dys[...]
    active, low, y_part, dh_part = hidden_step(0, meta, h2, dy, inb, arrays, 2)
    store_bias(dinb, low)
    narrow, width = kept.shape[2] // 2, kept.shape[3]
    d_in[...] = dot(h2, low, TN)
    d_back[...] = dot(dy, active, TN)
    for q in range(4):
        start = place(q, meta[2]) * narrow
        span = pl.ds(pl.multiple_of(start, narrow) if q in (1, 2) else start, narrow)
        into = kept if q < 2 else sent
        for s in range(2):
            columns = slice(s * width, (s + 1) * width)
            part = d_in[span, columns] + arrived[q, s, :narrow].astype(F32)
            into[q % 2, s, :narrow] = part.astype(BF16)
            part = d_back[span, columns] + arrived[q, s, narrow:].astype(F32)
            into[q % 2, s, narrow:] = part.astype(BF16)
    values = x1[...]
    store_halves(meta[2], *turn, values + y_first[...] + y_part + vecs[5:6])
    xhat, factor = norm_parts(values)
    grad = dh_first[...] + dh_part
    dy_wide = dy.astype(F32)
    total = dy_wide + norm_back(grad, xhat, factor, vecs[2:3])
    dx1[...] = total
    narrowed = total.astype(BF16)
    da[...] = narrowed
    vec_grads[0:1] = colsum(grad * xhat)
    vec_grads[1:2] = colsum(grad)
    vec_grads[2:3] = colsum(narrowed.astype(F32))
    vec_grads[3:4] = colsum(dy_wide)
    vec_grads[4:8] = jnp.zeros_like(vec_grads[4:8])


def attend_back_kernel(images, rows, meta, da, o_ref, qkv, p_ref, wo, h1, *refs):
    dqkv, halves, dwo, dshift, sent, do_ref, dw_ref = refs
    parts, narrow = wo.shape[0], wo.shape[1]
    heads = narrow // HEAD_DIM
    factor = HEAD_DIM ** (-0.5)
    grad = da[...]
    outer = narrow // 2
    for z in range(parts):
        do_ref[z] = dot(grad, wo[z], NT).astype(BF16)
    each = [(z, i) for z in range(parts) for i in range(heads)]
    for b in range(images):
        span = slice(b * rows, (b + 1) * rows)
        grad_heads, grad_scores, grads = [], [], []
        for z, i in each:
            grad_head = do_ref[z, span, i * HEAD_DIM : (i + 1) * HEAD_DIM]
            grad_heads.append(grad_head)
            grad_scores.append(dot(head_part(qkv, z, span, i, 2), grad_head, NT))
        for n in range(len(each)):
            chance = p_ref[n, b].astype(F32)
            inner = jnp.sum(chance * grad_scores[n], 0, keepdims=True)
            grad_scores[n] = (chance * (grad_scores[n] - inner)).astype(BF16)
        for n, (z, i) in enumerate(each):
            query, key = (head_part(qkv, z, span, i, part) for part in (0, 1))
            grads.append((dot(grad_scores[n], key, TN) * factor).astype(BF16))
            grads.append((dot(grad_scores[n], query, NN) * factor).astype(BF16))
            grads.append(dot(p_ref[n, b], grad_heads[n], NN).astype(BF16))
        for z in range(parts):
            together = grads[3 * z * heads : 3 * (z + 1) * heads]
            dqkv[z, span, :] = jnp.concatenate(together, 1)
    half = dqkv.shape[2] // 2
    for z in range(parts):
        dshift[z] = colsum(dqkv[z].astype(F32))
        for k in range(2):
            halves[z, k] = dqkv[z, :, k * half : (k + 1) * half]
        dw = dot(o_ref[:, z * narrow : (z + 1) * narrow], grad, TN)
        for d in range(parts):
            for k in range(2):
                at = d * narrow + k * outer
                dwo[z, d, k] = dw[:, at : at + outer].astype(BF16)

    def store(q, s, block):
        sent[q, s] = block.astype(BF16)

    first_grad(1, meta, h1, halves, dwo, dw_ref, store)


def first_back_kernel(
    meta, x0, dqkv, wq, dx1, vecs, vec_grads, dshift, sent_dinb, sent_rest, kept_dinb, kept_rest, *refs
):
    turn, (sent, kept, rows_out) = refs[:3], refs[3:]
    me = meta[0]
    parts, narrow = dqkv.shape[0], dqkv.shape[2] // 3
    width = sent.shape[3]
    grad = dot(dqkv[0], wq[0], NT)
    for z in range(1, parts):
        grad += dot(dqkv[z], wq[z], NT)
    xhat, factor = norm_parts(x0[...])
    store_halves(meta[2], *turn, dx1[...] + norm_back(grad, xhat, factor, vecs[0:1]))
    rows_out[0:1] = colsum(grad * xhat)
    rows_out[1:2] = colsum(grad)
    rows_out[2:6] = vec_grads[0:4]
    gap = jnp.zeros((6, width - narrow), F32)
    tail = jnp.zeros((VEC_ROWS - 9, width), F32)
    for d in range(parts):
        six = jnp.concatenate([rows_out[0:6, d * narrow : (d + 1) * narrow], gap], 1)
        shift = dshift[me ^ d]
        second = jnp.concatenate([shift[:, width:], gap[0:1, : 2 * width - shift.shape[1]]], 1)
        for s in range(4):
            for p, first, rest, out in (
                (1, sent_dinb, sent_rest, sent),
                (0, kept_dinb, kept_rest, kept),
            ):
                bias = first[s] if s < 2 else rest[s - 2]
                lines = [six, shift[:, :width], second, bias, tail]
                out[place(d, meta[2] ^ p), s] = jnp.concatenate(lines, 0).astype(BF16)


def first_grad(p, meta, h1, halves, dwo, dw, store):
    me = meta[0]
    narrow = dwo.shape[3]
    feature = h1[...]
    for s in range(4):
        z, k = column_of(meta, p, s)
        dw[...] = dot(feature, halves[z, k], TN)
        for q in range(4):
            d = place(q, meta[2] ^ p)
            start = d * narrow
            span = pl.ds(pl.multiple_of(start, narrow) if q in (1, 2) else start, narrow)
            store(q, s, jnp.concatenate([dw[span, :], dwo[me ^ d, z ^ me, k].astype(F32)], 1))


def first_kept_kernel(meta, h1, halves, dwo, arrived, kept, sent, dw):
    def store(q, s, block):
        into = kept if q < 2 else sent
        into[q % 2, s] = (block + arrived[q, s].astype(F32)).astype(BF16)

    first_grad(0, meta, h1, halves, dwo, dw, store)


def finish_second_kernel(*refs):
    pieces, (d_in, d_back) = refs[:4], refs[4:]
    narrow = d_in.shape[0]
    for rows, out in ((slice(0, narrow), d_in), (slice(narrow, 2 * narrow), d_back)):
        total = pieces[0][rows].astype(F32)
        for piece in pieces[1:]:
            total += piece[rows].astype(F32)
        out[...] = total


def finish_kernel(*refs):
    pieces, (qkv, out, hidden_bias, query, value), vectors = refs[:4], refs[4:9], refs[9:]
    narrow, half = qkv.shape
    total = pieces[0][...].astype(F32)
    for piece in pieces[1:]:
        total += piece[...].astype(F32)
    qkv[...] = total[:narrow, :half]
    out[...] = total[:narrow, half:]
    for i, ref in enumerate(vectors):
        ref[...] = total[narrow + i : narrow + i + 1, :narrow].reshape(ref.shape)
    shift = jnp.concatenate([total[narrow + 6 : narrow + 7], total[narrow + 7 : narrow + 8]], 1)
    heads = range(narrow // HEAD_DIM)
    for ref, part in ((query, 0), (value, 2)):
        pieces = [shift[:, (3 * i + part) * HEAD_DIM :][:, :HEAD_DIM] for i in heads]
        ref[...] = jnp.concatenate(pieces, 1).reshape(ref.shape)
    hidden_bias[...] = total[narrow + 8 : narrow + 9].reshape(hidden_bias.shape)


def call(kernel, outs, operands, scratch=(), name=None):
    specs = []
    for value in operands:
        specs.append(SMEM if value.dtype == jnp.int32 and value.ndim == 1 else VMEM)
    return pl.pallas_call(
        kernel,
        out_shape=outs,
        in_specs=specs,
        out_specs=jax.tree.map(lambda _: VMEM, outs),
        scratch_shapes=scratch,
        compiler_params=PARAMS,
        name=name,
    )(*operands)


def shaped(dtype, *shape):
    return jax.ShapeDtypeStruct(shape, dtype)


def exchange(block, d):
    size = lax.axis_size("ea")
    return block if d == 0 else lax.ppermute(block, "ea", [(e, e ^ d) for e in range(size)])


class Wires:
    def __init__(self, parts, columns):
        self.parts, self.chips = parts, columns // 2

    def over_z(self, blocks, back=False, slots=(1, 2, 3)):
        pulled = [blocks[0]]
        for s in slots:
            pairs = []
            for h in range(2 * self.chips):
                far = (h + 2 * s) % (2 * self.chips)
                pairs.append((h, far) if back else (far, h))
            pulled.append(lax.ppermute(blocks[s], "ha", pairs))
        return pulled

    def turn(self, pair):
        if 2 * self.chips == BLOCKS:
            return self.stage(pair, 0)
        one = exchange(pair[0], 1)
        return jnp.stack([one, exchange(pair[1], 1)])

    def turn_again(self, *pairs):
        both = jnp.stack([block for single, first in pairs for block in (single, first[1])])
        return self.stage(both, 1) if 2 * self.chips == BLOCKS else exchange(both, 2)

    def swap(self, block):
        return lax.ppermute(block, "ha", [(h, h ^ 1) for h in range(2 * self.chips)])

    def stage(self, block, second):
        pairs = []
        columns = 2 * self.chips
        for e in range(self.parts):
            for h in range(columns):
                d = 1 + ((h % 2) ^ second)
                pairs.append((e * columns + h, (e ^ d) * columns + h))
        return lax.ppermute(block, ("ea", "ha"), pairs)

    def spread(self, mine, behind=(), swap_behind=(), one=None):
        one = self.stage(mine, 0) if one is None else one
        two = self.stage(mine, 1)
        mine, one, two = after((mine, one, two), *behind)
        three = self.stage(one, 1)
        mine, one, two = after((mine, one, two), *swap_behind)
        own = (mine, one, two, three)
        return own, tuple(self.swap(block) for block in own)


def after(value, *others):
    return lax.optimization_barrier((value, others))[0]


def add(*terms):
    return sum(term.astype(F32) for term in terms).astype(BF16)


def vector_rows(vectors, shift, bias):
    width = bias.shape[-1]
    rows = [jnp.pad(v, (0, width - v.shape[0])) for v in vectors]
    rows += [shift[:width], jnp.pad(shift[width:], (0, 2 * width - shift.shape[0])), bias]
    return jnp.stack(rows + [jnp.zeros_like(bias)] * (VEC_ROWS - len(rows)))


def half_call(half, kernel, outs, operands, arrays, scratch, name):
    block = pl.BlockSpec((2, *arrays[0].shape[1:]), lambda i: (half, 0, 0))
    return pl.pallas_call(
        kernel,
        grid=(1,),
        out_shape=outs,
        in_specs=[SMEM] + [whole_spec(*v.shape) for v in operands[1:]] + [block] * len(arrays),
        out_specs=jax.tree.map(lambda out: whole_spec(*out.shape), outs),
        scratch_shapes=scratch,
        compiler_params=PARAMS,
        name=name,
    )(*operands, *arrays)


def whole_spec(*shape):
    return pl.BlockSpec(shape, lambda i: (0,) * len(shape))


def shards(
    tokens,
    image_counts,
    kept_patches,
    norm1_gain,
    norm1_bias,
    qkv_weight,
    query_bias,
    value_bias,
    out_weight,
    out_bias,
    norm2_gain,
    norm2_bias,
    in_weight,
    in_bias,
    back_weight,
    back_bias,
    cotangent,
):
    parts = lax.axis_size("ea")
    columns = lax.axis_size("ha")
    me = lax.axis_index("ea")
    mine = lax.axis_index("ha")
    direct = columns == BLOCKS
    wires = Wires(parts, columns)
    if direct:
        meta = jnp.stack([me, mine // 2, mine % 2]).astype(jnp.int32)
    else:
        meta = jnp.stack([me, 0 * mine, 0 * mine]).astype(jnp.int32)
    narrow, slots = tokens.shape
    full = narrow * parts
    images = image_counts.shape[0] // parts
    most = kept_patches.shape[1]
    rows = -(-most // 16) * 16
    count = images * rows
    window = min(slots, (images * most + 127 + 127) // 128 * 128)
    heads = full // HEAD_DIM
    group_heads = narrow // HEAD_DIM
    width = in_weight.shape[1] * columns // BLOCKS
    half = 3 * narrow // 2

    vectors = (norm1_gain, norm1_bias, norm2_gain, norm2_bias, out_bias, back_bias)
    if direct:
        first, second = call(
            shard_kernel,
            (shaped(BF16, narrow + VEC_ROWS, width), shaped(BF16, 2 * narrow, width)),
            (qkv_weight, out_weight, in_weight, back_weight.T, in_bias, query_bias, value_bias)
            + vectors,
            name="shard",
        )

    turn_shapes = lambda r, c: (shaped(BF16, r, c), shaped(BF16, 2, r, c), shaped(BF16, r, c))
    packed = call(
        partial(pack_kernel, images, rows, window),
        turn_shapes(count, 2 * narrow),
        (meta, image_counts, tokens, cotangent),
        (pltpu.SMEM((image_counts.shape[0],), jnp.int32), pltpu.VMEM((count, window), BF16)),
        "pack",
    )

    if direct:
        turned_once = wires.turn(packed[1])
        z_first = wires.over_z([first] * 4)
        turned_once = after(turned_once, *z_first[1:])
        xs = (packed[0], turned_once, wires.turn_again((packed[2], turned_once)))
        z_second = wires.over_z([after(second, *z_first)] * 4)
        g1 = wires.spread(jnp.stack(z_first), (), z_second)
        z_second = jnp.stack(after(z_second, g1[0][1]))
        xs = after(xs, z_second)
    else:
        turned_once = wires.turn(packed[1])
        xs = (packed[0], turned_once, wires.turn_again((packed[2], turned_once)))
        pairs = jnp.zeros((group_heads, HEAD_DIM), BF16)
        by_head = lambda bias: bias.reshape(group_heads, HEAD_DIM)
        shift = jnp.stack([by_head(query_bias), pairs, by_head(value_bias)], 1).reshape(-1)

        def whole(weight):
            wide = lax.all_gather(weight, "ha", axis=1, tiled=True)
            blocks = wide.reshape(narrow, BLOCKS, -1).transpose(1, 0, 2)
            return lax.all_gather(blocks, "ea")

        def arrange(blocks):
            sides = []
            for p in range(2):
                side = []
                for a in range(parts):
                    d = a if p == 0 or a in (0, 3) else 3 - a
                    row = lax.dynamic_index_in_dim(blocks, me ^ d, 0, False)
                    side.append(jnp.stack([row[2 * s + p] for s in range(4)]))
                sides.append(tuple(side))
            return sides

        biases = lax.all_gather(in_bias, "ha", tiled=True).reshape(BLOCKS, -1)
        below = jax.vmap(lambda bias: vector_rows(vectors, shift, bias))(biases)
        g1 = jnp.concatenate([whole(qkv_weight), whole(out_weight)], 3)
        g1 = jnp.concatenate([g1, lax.all_gather(below, "ea")], 2)
        g1 = arrange(g1)
        g2 = arrange(jnp.concatenate([whole(in_weight), whole(back_weight.T)], 2))

    omega = 1.0 / 10000.0 ** (jnp.arange(narrow, dtype=F32) / narrow)
    angles = jnp.arange(16, dtype=F32)[:, None] * omega[None, :]
    patches = jnp.pad(kept_patches, ((0, 0), (0, 128 - most)))

    x1, x0, h1, qkv, chances, mixed, vecs, inb, wq, wo = call(
        partial(attend_kernel, images, rows),
        (
            shaped(F32, count, full),
            shaped(F32, count, full),
            shaped(BF16, count, full),
            shaped(BF16, parts, count, 3 * narrow),
            shaped(BF16, heads, images, rows, rows),
            shaped(BF16, count, full),
            shaped(F32, VEC_ROWS, full),
            shaped(F32, BLOCKS, 1, width),
            shaped(BF16, parts, full, 3 * narrow),
            shaped(BF16, parts, narrow, full),
        ),
        (meta, image_counts, *xs, patches, jnp.sin(angles), jnp.cos(angles), *g1[0], *g1[1]),
        (
            pltpu.VMEM((parts, 1, 3 * narrow), F32),
            pltpu.VMEM((parts, parts, narrow, narrow), BF16),
        ),
        "attend",
    )

    if direct:
        g2 = wires.spread(z_second, (x1,))
    far_z = lambda block, s: wires.over_z([block] * 4, True, (s,))[1]
    four = shaped(BF16, 4, 2, 2 * narrow, width)
    two = shaped(BF16, 2, 2, 2 * narrow, width)
    pair_bias = shaped(F32, 2, 1, width)
    wide_low, wide = shaped(BF16, count, full), shaped(F32, count, full)
    sent2, kept2, dinb_sent, dinb_kept, h2, dy, y_first, dh_first = half_call(
        0,
        hidden_first_kernel,
        (four, four, pair_bias, pair_bias, wide_low, wide_low, wide, wide),
        (meta, x1, *xs, vecs, inb),
        (*g2[0], *g2[1]),
        (),
        "hidden_first",
    )
    arrived2 = wires.swap(sent2) if direct else jnp.zeros_like(sent2)
    sent3, dinb_a, y_first, dh_first = half_call(
        1,
        hidden_a_kernel,
        (four, pair_bias, wide, wide),
        (meta, h2, dy, y_first, dh_first, inb),
        g2[1],
        (),
        "hidden_a",
    )
    arrived3 = wires.swap(sent3) if direct else jnp.zeros_like(sent3)
    arrived2 = after(arrived2, y_first)
    passed2 = add(kept2[2:], arrived2[2:])
    if direct:
        arrived_pass2 = wires.stage(passed2, 1)
    kept3, passed3, dinb_b, *outs, dx1, da, vec_grads = half_call(
        1,
        hidden_b_kernel,
        (two, two, pair_bias) + turn_shapes(count // 2, 2 * narrow) + (wide, wide_low, shaped(F32, 8, full)),
        (meta, x1, after(h2, passed2), dy, y_first, dh_first, vecs, inb, arrived3),
        g2[0],
        (pltpu.VMEM((full, 2 * width), F32), pltpu.VMEM((full, 2 * width), F32)),
        "hidden_b",
    )
    if direct:
        arrived = after(arrived_pass2, da)
        once2 = add(kept2[0], arrived2[0], arrived[0])
        next2 = add(kept2[1], arrived2[1], arrived[1])
        arrived_next2 = wires.stage(next2, 0)
        arrived_pass3 = wires.stage(after(passed3, next2), 1)
        da = after(da, once2, next2)
    dqkv, halves, dwo, dshift, sent1 = call(
        partial(attend_back_kernel, images, rows),
        (
            shaped(BF16, parts, count, 3 * narrow),
            shaped(BF16, parts, 2, count, half),
            shaped(BF16, parts, parts, 2, narrow, narrow // 2),
            shaped(F32, parts, 1, 3 * narrow),
            shaped(BF16, 4, 4, narrow, width),
        ),
        (meta, da, mixed, qkv, chances, wo, h1),
        (pltpu.VMEM((parts, count, narrow), BF16), pltpu.VMEM((full, half), F32)),
        "attend_back",
    )
    if direct:
        arrived = after(arrived_pass3, dqkv)
        once3, next3 = add(kept3[0], arrived[0]), add(kept3[1], arrived[1])
        next3, sent1, h1 = after((next3, sent1, h1), once3)
        arrived1 = wires.swap(sent1)
    else:
        arrived1 = jnp.zeros_like(sent1)
    kept1, passed1 = call(
        first_kept_kernel,
        (shaped(BF16, 2, 4, narrow, width),) * 2,
        (meta, h1, halves, dwo, arrived1),
        (pltpu.VMEM((full, half), F32),),
        "first_kept",
    )
    if direct:
        arrived_pass1 = wires.stage(passed1, 1)
        total2 = add(once2, after(arrived_next2, kept1))
        arrived_next3 = wires.stage(next3, 0)
        x0 = after(x0, kept1, total2)
    outs[1] = wires.turn(after(outs[1], kept1))
    *gx, sent_below, kept_below = call(
        first_back_kernel,
        turn_shapes(count // 2, 2 * narrow)
        + (shaped(BF16, 4, 4, VEC_ROWS, width),) * 2,
        (meta, x0, dqkv, wq, dx1, vecs, vec_grads, dshift, dinb_sent, dinb_a, dinb_kept, dinb_b),
        (pltpu.VMEM((8, full), F32),),
        name="first_back",
    )
    gx[1] = wires.turn(gx[1])
    if direct:
        below = add(kept_below, wires.swap(sent_below))
        arrived_below = wires.stage(below[2:], 1)
        total3 = add(once3, after(arrived_next3, gx[0]))
        far = [far_z(total2[1], 1), far_z(total3[0], 2), far_z(total3[1], 3)]
        grad_in, grad_back = call(
            finish_second_kernel,
            (shaped(F32, narrow, width),) * 2,
            (total2[0], *far),
            name="finish_second",
        )
        arrived = after(arrived_pass1, gx[0], far[1], gx[1])
        once1, next1 = add(kept1[0], arrived[0]), add(kept1[1], arrived[1])
        arrived_next1 = wires.stage(next1, 0)
        below_next = add(below[1], arrived_below[1])
        below_total = add(below[0], arrived_below[0], wires.stage(below_next, 0))
        total = jnp.concatenate([add(once1, arrived_next1), below_total], 1)
        z_first = wires.over_z([total[s] for s in range(4)], back=True)
        gx[1] = after(gx[1], next1)
    second = wires.turn_again((outs[2], outs[1]), (gx[2], gx[1]))

    output, grad_tokens = call(
        partial(unpack_kernel, images, rows, window),
        (shaped(BF16, narrow, slots), shaped(F32, narrow, slots)),
        (meta, image_counts, *outs[:2], *gx[:2], second),
        (
            pltpu.SMEM((image_counts.shape[0],), jnp.int32),
            pltpu.VMEM((count, window), BF16),
            pltpu.VMEM((narrow, slots), F32),
            pltpu.VMEM((narrow, slots), F32),
        ),
        "unpack",
    )

    if direct:
        line = shaped(F32, narrow)
        grad_qkv, grad_out, grad_in_bias, grad_query, grad_value, *small = call(
            finish_kernel,
            (shaped(F32, narrow, half), shaped(F32, narrow, narrow // 2), shaped(F32, width))
            + (line,) * 8,
            z_first,
            name="finish",
        )
    else:

        def spread(sent, kept, passed):
            later = jnp.concatenate([kept, passed], 0)
            tall = []
            for e in range(parts):
                d = me ^ e
                row = [None] * BLOCKS
                for p, side in ((1, sent), (0, later)):
                    q = jnp.where((d == 0) | (d == 3) | (p == 0), d, 3 - d)
                    four = lax.dynamic_index_in_dim(side, q, 0, False)
                    for s in range(4):
                        row[2 * s + p] = four[s]
                tall.append(jnp.stack(row))
            return jnp.stack(tall).astype(F32)

        def scatter(blocks):
            flat = lax.psum_scatter(blocks, "ea").transpose(1, 0, 2).reshape(narrow, -1)
            return lax.psum_scatter(flat, "ha", scatter_dimension=1, tiled=True)

        sent1 = jnp.concatenate([sent1, sent_below], 2)
        kept1 = jnp.concatenate([kept1, kept_below[:2]], 2)
        passed1 = jnp.concatenate([passed1, kept_below[2:]], 2)
        sent2, kept2 = jnp.concatenate([sent2, sent3], 1), jnp.concatenate([kept2[:2], kept3], 1)
        d2 = spread(sent2, kept2, jnp.concatenate([passed2, passed3], 1))
        d1 = spread(sent1, kept1, passed1)
        grad_in, grad_back = scatter(d2[:, :, :narrow]), scatter(d2[:, :, narrow:])
        grad_qkv, grad_out = scatter(d1[:, :, :narrow, :half]), scatter(d1[:, :, :narrow, half:])
        small = lax.psum(d1[:, :, narrow:], ("ea", "ha"))
        size = in_bias.shape[0]
        grad_in_bias = lax.dynamic_slice_in_dim(small[0, :, 8].reshape(-1), mine * size, size, 0)
        small = lax.dynamic_index_in_dim(small[:, 0], me, 0, False)
        shift = jnp.concatenate([small[6], small[7]])[: 3 * narrow]
        shift = shift.reshape(group_heads, 3, HEAD_DIM)
        grad_query, grad_value = shift[:, 0].reshape(-1), shift[:, 2].reshape(-1)
        small = small[:, :narrow]
    return (
        output,
        grad_tokens,
        small[0],
        small[1],
        grad_qkv,
        grad_query,
        grad_value,
        grad_out,
        small[4],
        small[2],
        small[3],
        grad_in,
        grad_in_bias,
        grad_back.T,
        small[5],
    )


def solution(mesh):
    return jax.shard_map(
        shards,
        mesh=mesh,
        in_specs=(
            P("ea", "ha"),
            P("ha"),
            P("ha", None),
            P("ea"),
            P("ea"),
            P("ea", "ha"),
            P("ea"),
            P("ea"),
            P("ea", "ha"),
            P("ea"),
            P("ea"),
            P("ea"),
            P("ea", "ha"),
            P("ha"),
            P("ha", "ea"),
            P("ea"),
            P("ea", "ha"),
        ),
        out_specs=(
            P("ea", "ha"),
            P("ea", "ha"),
            P("ea"),
            P("ea"),
            P("ea", "ha"),
            P("ea"),
            P("ea"),
            P("ea", "ha"),
            P("ea"),
            P("ea"),
            P("ea"),
            P("ea", "ha"),
            P("ha"),
            P("ha", "ea"),
            P("ea"),
        ),
        check_vma=False,
    )
```
